256 devices in a mesh: dp: 16 (over z, x_lo), seq: 16 (over y, x_hi, core).
Axes of the slice: x: 4 (x_hi: 2, x_lo: 2; x = x_hi * 2 + x_lo), y: 4, z: 8, core: 2. Of those that a mesh axis runs over, the one named last changes fastest.
Arguments:
- states: bfloat16 [16, 1024, 4096], P('dp', 'seq'), may hold values from -6 to 6
- kv_weight: bfloat16 [4096, 1536], P('seq'), may hold values from -0.09375 to 0.09375
- queries: bfloat16 [16, 4096, 768], P('dp', 'seq'), may hold values from -150 to 150
- hidden: bfloat16 [16, 4096, 1536], P('dp', 'seq'), may hold values from -3 to 3
- out_proj: bfloat16 [768, 1536], P('seq'), may hold values from -0.21875 to 0.21875
- disc_in: bfloat16 [1536, 1024], replicated, may hold values from -0.15625 to 0.15625
- conv_weight: bfloat16 [41, 64, 1024], replicated, may hold values from -0.125 to 0.125
- score_weight: float32 [1024], replicated, may hold values from -0.1875 to 0.1875
- frame_len: int32 [16], replicated, may hold values from 1024 to 4096, as said below
- state_len: int32 [16], replicated, may hold values from 256 to 1024, as said below
Outputs:
- grad_out_proj: float32 [768, 1536], P('seq')
- loss_mean: float32 [], replicated
The draws below stay inside these ranges and needn't reach their ends.
Inputs may be any that keep to these rules, and one draw needn't show every extreme that they name: `frame_len`: one clip has all 4096 frames live in every draw. `state_len`: one clip has all 1024 backbone frames live in every draw.
All inputs are finite; a program needn't handle non-finite values.
Results may differ from the reference program's by a relative error of at most 0.005.
Values may be sent and summed in bfloat16 or wider, within the bound.
No kernel may reach another device: no remote copies, remote signals or barrier semaphores. Data moves between devices by JAX's collectives and lax.ppermute only.
A program may use at most 128 MiB of HBM per device.

```python
import math
import jax
import jax.numpy as jnp
from jax import lax

D_MODEL = 1536
HEADS = 6
HEAD_DIM = 128
ATT = 768
D_STATE = 4096
DISC_CH = 1024
GROUPS = 16
GROUP_CH = 64
KERNEL = 41
STRIDE = 4
S = 4096
L = 1024
CLIPS = 16


def draw_queries(key, part):
    full_shape = (CLIPS, S, HEADS * HEAD_DIM)
    return (1.5 * jax.random.truncated_normal(jax.random.fold_in(key, 24), -6.0, 6.0, full_shape, jnp.float32)).astype(jnp.bfloat16)


def draw_frame_len(key, part):
    lengths = jax.random.randint(jax.random.fold_in(key, 11), (CLIPS,), S // 4, S + 1)
    chosen = jax.random.randint(jax.random.fold_in(key, 12), (), 0, CLIPS)
    return jnp.where(jnp.arange(CLIPS) == chosen, S, lengths).astype(jnp.int32)


def draw_state_len(key, part):
    lengths = jax.random.randint(jax.random.fold_in(key, 31), (CLIPS,), L // 4, L + 1)
    chosen = jax.random.randint(jax.random.fold_in(key, 32), (), 0, CLIPS)
    return jnp.where(jnp.arange(CLIPS) == chosen, L, lengths).astype(jnp.int32)


def block_levels(own_key, dims, split, low, high):
    level = 1.0
    for position, parts in split:
        draws = jax.random.uniform(jax.random.fold_in(jax.random.fold_in(own_key, 6), position), (parts,), jnp.float32, low / len(split), high / len(split))
        level = level * jnp.repeat(jnp.exp(draws), dims[position] // parts).reshape((-1,) + (1,) * (len(dims) - 1 - position))
    return level


def noise(stream_key, shape, width, limit, pieces=(), dtype=jnp.bfloat16):
    values = jax.random.normal(stream_key, shape, jnp.float32) * width
    if len(pieces) > 0:
        values = block_levels(stream_key, shape, pieces, -0.22, 0.18) * values
    return jnp.clip(values, min=-limit, max=limit).astype(dtype)


def setup_inputs(seed: int = 0) -> dict:
    splits = jax.random.split(jax.random.key(seed), 11)
    states = noise(splits[0], (CLIPS, L, D_STATE), 1.0, 6.0, ((0, 16), (1, 16)))
    kv_weight = noise(splits[1], (D_STATE, 2 * ATT), D_STATE ** -0.5, 0.09375, ((0, 16),))
    queries = draw_queries(jax.random.fold_in(splits[10], 71), 0)
    hidden = noise(splits[3], (CLIPS, S, D_MODEL), 0.5, 3.0, ((0, 16), (1, 16)))
    out_proj = noise(splits[4], (ATT, D_MODEL), ATT ** -0.5, 0.21875, ((0, 16),))
    disc_in = noise(splits[5], (D_MODEL, DISC_CH), D_MODEL ** -0.5, 0.15625)
    conv_weight = noise(splits[6], (KERNEL, GROUP_CH, DISC_CH), (GROUP_CH * KERNEL) ** -0.5, 0.125)
    score_weight = noise(splits[7], (DISC_CH,), DISC_CH ** -0.5, 0.1875, (), jnp.float32)
    frame_len = draw_frame_len(jax.random.fold_in(splits[10], 71), 0)
    state_len = draw_state_len(jax.random.fold_in(splits[10], 71), 0)
    return {"states": states, "kv_weight": kv_weight, "queries": queries, "hidden": hidden, "out_proj": out_proj, "disc_in": disc_in, "conv_weight": conv_weight, "score_weight": score_weight, "frame_len": frame_len, "state_len": state_len}


def regroup(weight_taps, group_count):
    kernel, group_in, channels = weight_taps.shape
    blocks = weight_taps.reshape(kernel, group_in, group_count, channels // group_count)
    turned = jnp.transpose(blocks, (0, 3, 2, 1)).reshape(kernel, channels // group_count, channels)
    return jnp.flip(turned, 0)

def disc_conv(padded, weight_taps, group_count, stride):
    return lax.conv_general_dilated(padded[None], weight_taps, (stride,), 'VALID', dimension_numbers=('NWC', 'WIO', 'NWC'), feature_group_count=group_count, preferred_element_type=jnp.float32)[0]

def disc_back(grad_wide, flipped, group_count, stride, high_pad):
    return lax.conv_general_dilated(grad_wide[None], flipped, (1,), [(0, high_pad)], lhs_dilation=(stride,), dimension_numbers=('NWC', 'WIO', 'NWC'), feature_group_count=group_count, preferred_element_type=jnp.float32)[0]

def attend_ref(query, keys_values, live_keys):
    row_count, att_width = query.shape
    head_count = att_width // HEAD_DIM
    query_heads = query.astype(jnp.float32).reshape(row_count, head_count, HEAD_DIM)
    key_heads = keys_values[:, :att_width].reshape(-1, head_count, HEAD_DIM)
    value_heads = keys_values[:, att_width:].reshape(-1, head_count, HEAD_DIM)
    scores = jnp.einsum('qhd,khd->hqk', query_heads, key_heads, precision=lax.Precision.HIGHEST) / math.sqrt(HEAD_DIM)
    scores = jnp.where(live_keys[None, None, :], scores, -1e+30)
    row_max = lax.optimization_barrier(jnp.max(scores, axis=2, keepdims=True))
    expo_scores = jnp.where(live_keys[None, None, :], jnp.exp(scores - row_max), 0.0)
    denom = lax.optimization_barrier(jnp.sum(expo_scores, axis=2))
    weights = lax.optimization_barrier(expo_scores.astype(jnp.bfloat16)).astype(jnp.float32)
    mixed_heads = jnp.einsum('hqk,khd->qhd', weights, value_heads, precision=lax.Precision.HIGHEST)
    mixed_heads = mixed_heads / jnp.transpose(denom)[:, :, None]
    return mixed_heads.reshape(row_count, att_width).astype(jnp.bfloat16)

def reference(states, kv_weight, queries, hidden, out_proj, disc_in, conv_weight, score_weight, frame_len, state_len):
    margin_rows = (KERNEL - 1) // 2
    reach_out = margin_rows // STRIDE
    flipped = regroup(conv_weight.astype(jnp.float32), GROUPS)
    taps_float = conv_weight.astype(jnp.float32)

    def one_clip(carry, inputs):
        grad_sum, loss_sum = carry
        states_clip, queries_clip, hidden_clip, frames_live, states_live = inputs
        keys_values = jnp.dot(states_clip, kv_weight, preferred_element_type=jnp.float32)
        live_keys = jnp.arange(keys_values.shape[0]) < states_live
        block_rows = math.gcd(queries_clip.shape[0], 1024)
        query_blocks = queries_clip.reshape(-1, block_rows, queries_clip.shape[1])

        def attend_block(block_in):
            return attend_ref(block_in, keys_values, live_keys)
        attended = lax.map(attend_block, query_blocks).reshape(queries_clip.shape)
        lifted = hidden_clip.astype(jnp.float32) + jnp.dot(attended, out_proj, preferred_element_type=jnp.float32)
        mixed_rows = lifted.astype(jnp.bfloat16)
        inside = (jnp.arange(mixed_rows.shape[0]) < frames_live)[:, None]
        disc_feed = jnp.where(inside, jnp.dot(mixed_rows, disc_in, preferred_element_type=jnp.float32), 0.0).astype(jnp.bfloat16)
        padded = jnp.pad(disc_feed.astype(jnp.float32), ((margin_rows, margin_rows), (0, 0)))
        pre = disc_conv(padded, taps_float, GROUPS, STRIDE)
        sigmoid_pre = jax.nn.sigmoid(pre)
        critic = jnp.dot(pre * sigmoid_pre, score_weight, precision=lax.Precision.HIGHEST)
        valid_out = STRIDE * jnp.arange(pre.shape[0]) < frames_live
        shortfall = 1.0 - critic
        loss_part = jnp.sum(jnp.where(valid_out, shortfall * shortfall, 0.0))
        push_score = jnp.where(valid_out, -2.0 * shortfall, 0.0)
        slope_pre = sigmoid_pre * (1.0 + pre * (1.0 - sigmoid_pre))
        grad_pre = (push_score[:, None] * score_weight[None, :] * slope_pre).astype(jnp.bfloat16)
        grad_wide = jnp.pad(grad_pre.astype(jnp.float32), ((reach_out, reach_out), (0, 0)))
        grad_feed = disc_back(grad_wide, flipped, GROUPS, STRIDE, STRIDE - 1)
        grad_feed = jnp.where(inside, grad_feed, 0.0).astype(jnp.bfloat16)
        grad_mixed = jnp.dot(grad_feed, disc_in.T, preferred_element_type=jnp.float32).astype(jnp.bfloat16)
        term = jnp.dot(attended.T, grad_mixed, preferred_element_type=jnp.float32)
        return ((grad_sum + term, loss_sum + loss_part), None)
    start = (jnp.zeros((out_proj.shape[0], out_proj.shape[1]), jnp.float32), jnp.zeros((), jnp.float32))
    (grad_sum, loss_sum), _ = lax.scan(one_clip, start, (states, queries, hidden, frame_len, state_len))
    counted = jnp.sum((frame_len + STRIDE - 1) // STRIDE).astype(jnp.float32)
    return (grad_sum, loss_sum / counted)
```

```python
import functools
import math

import jax
import jax.numpy as jnp
from jax import lax
from jax.experimental import pallas as pl
from jax.experimental.pallas import tpu as pltpu
from jax.sharding import PartitionSpec as P

HEAD_DIM = 128
HALF_HEADS = 3
HALF_ATT = HEAD_DIM * HALF_HEADS
GROUP_CH = 64
STRIDE = 4
TAPS = 41
TAP_SETS = 12
MARGIN = 20
HALO = 40
REACH = 5
F32 = jnp.float32
BF16 = jnp.bfloat16
VMEM_LIMIT = 50 * 1024 * 1024


def params():
    return pltpu.CompilerParams(vmem_limit_bytes=VMEM_LIMIT)


def smem():
    return pl.BlockSpec(memory_space=pltpu.SMEM)


def vmem():
    return pl.BlockSpec(memory_space=pltpu.VMEM)


def low_lanes(shape):
    return lax.broadcasted_iota(jnp.int32, shape, 1) % 128 < 64


def roll_half(x):
    return pltpu.roll(x, 64, 1)


def arrange_kernel(w_ref, o_ref):
    low = low_lanes((GROUP_CH, 128))
    zero = jnp.zeros((GROUP_CH, 128), F32)

    def tap(k):
        return w_ref[k].astype(F32) if k < TAPS else zero

    for b in range(STRIDE):
        for pair in range(TAP_SETS // 2):
            first = tap(8 * pair + b)
            second = tap(8 * pair + 4 + b)
            rows, lanes = (slice(b * 64, b * 64 + 64), slice(pair * 128, pair * 128 + 128))
            o_ref[0, rows, lanes] = jnp.where(low, first, roll_half(second)).astype(BF16)
            o_ref[1, rows, lanes] = jnp.where(low, roll_half(first), second).astype(BF16)


def arrange(conv_weight):
    taps, group_in, channels = conv_weight.shape
    groups = channels // GROUP_CH
    return pl.pallas_call(
        arrange_kernel,
        grid=(channels // 128,),
        in_specs=[pl.BlockSpec((taps, group_in, 128), lambda l: (0, 0, l))],
        out_specs=pl.BlockSpec((2, STRIDE * 64, TAP_SETS * 64), lambda l: (l, 0, 0)),
        out_shape=jax.ShapeDtypeStruct((groups, STRIDE * 64, TAP_SETS * 64), BF16),
        compiler_params=params(),
        cost_estimate=pl.CostEstimate(flops=20_000_000, bytes_accessed=20_000_000, transcendentals=0),
    )(conv_weight)


def project_kernel(cols_ref, *refs):
    states, weights, o_ref = (refs[:4], refs[4:12], refs[12])
    total = None
    for i, weight in enumerate(weights):
        for half in range(2):
            start = pl.multiple_of(cols_ref[2 * i + half], 256)
            left = jnp.concatenate([s[:, pl.ds(start, 256)] for s in states], axis=0)
            part = jnp.dot(left, weight[256 * half : 256 * half + 256, :], preferred_element_type=F32)
            total = part if total is None else total + part
    o_ref[...] = total


def project(cols, states, weights):
    return pl.pallas_call(
        project_kernel,
        in_specs=[smem()] + [vmem()] * 12,
        out_specs=vmem(),
        out_shape=jax.ShapeDtypeStruct((256, HALF_ATT), F32),
        compiler_params=params(),
        cost_estimate=pl.CostEstimate(flops=800_000_000, bytes_accessed=6_000_000, transcendentals=0),
    )(cols, *states, *weights)


def split(x):
    high = x.astype(BF16)
    return high, (x - high.astype(F32)).astype(BF16)


def attend_kernel(meta_ref, q_ref, *refs):
    mine, other, o_ref = (refs[:4], refs[4:8], refs[8])
    live, core, half, row = (meta_ref[0], meta_ref[1], meta_ref[2], meta_ref[3])
    first = core == 0
    keys, values = ([], [])
    for m, o in zip(mine, other):
        keys.append(jnp.where(first, m[...], o[...]))
        turned = []
        for j in range(4):
            k = slice(64 * (j ^ 1), 64 * (j ^ 1) + 64)
            turned.append(jnp.where(first, o[k, :], m[k, :]))
        values.extend(turned)
    key_high, key_low = split(jnp.concatenate(keys, axis=0))
    value_high, value_low = split(jnp.concatenate(values, axis=0))
    spot = lax.broadcasted_iota(jnp.int32, (1, 1024), 1)
    hop, block, rest = (spot // 256, (spot // 64) % 4, spot % 64)
    where_y = (row - hop + 4) % 4
    where_h = (half + block // 2) % 2
    position = ((where_y * 2 + where_h) * 2 + block % 2) * 64 + rest
    alive = position < live
    contract = (((1,), (1,)), ((), ()))
    rows = 112
    for start in range(0, q_ref.shape[0], rows):
        q = q_ref[start : start + rows, :]
        scores = lax.dot_general(q, key_high, contract, preferred_element_type=F32)
        scores = scores + lax.dot_general(q, key_low, contract, preferred_element_type=F32)
        scores = jnp.where(alive, scores * (1.0 / math.sqrt(HEAD_DIM)), -1e30)
        top = jnp.max(scores, axis=1, keepdims=True)
        expo = jnp.where(alive, jnp.exp(scores - top), 0.0)
        denom = jnp.sum(expo, axis=1, keepdims=True)
        weights = expo.astype(BF16)
        mixed = jnp.dot(weights, value_high, preferred_element_type=F32)
        mixed = mixed + jnp.dot(weights, value_low, preferred_element_type=F32)
        o_ref[start : start + rows, :] = (mixed / denom).astype(BF16)


def attend(meta, query, mine, other):
    rows, width = query.shape
    block = lambda n: pl.BlockSpec((n, HEAD_DIM), lambda h: (0, h))
    return pl.pallas_call(
        attend_kernel,
        grid=(width // HEAD_DIM,),
        in_specs=[smem(), block(rows)] + [block(256)] * 8,
        out_specs=block(rows),
        out_shape=jax.ShapeDtypeStruct((rows, width), BF16),
        compiler_params=params(),
        cost_estimate=pl.CostEstimate(
            flops=8 * rows * 1024 * width, bytes_accessed=4_000_000, transcendentals=rows * 3072
        ),
    )(meta, query, *mine, *other)


def critic_kernel(
    meta_ref, lifted_ref, mine_ref, other_ref, proj_ref, conv_ref, score_ref,
    out_ref, loss_ref,
    feed_s, y_s, pre_s, grad_s, turned_s, back_s, att_s,
):
    live, first_frame, half = (meta_ref[0], meta_ref[1], meta_ref[2])
    total_frames = meta_ref[3]
    ext = lifted_ref.shape[0]
    own_out = (ext - 2 * HALO) // STRIDE
    tiles = lifted_ref.shape[1] // 128
    feed = lifted_ref[...]
    feed = feed + jnp.dot(mine_ref[...], proj_ref[half], preferred_element_type=F32)
    feed = feed + jnp.dot(other_ref[...], proj_ref[1 - half], preferred_element_type=F32)
    frame = first_frame - HALO + lax.broadcasted_iota(jnp.int32, (ext, 1), 0)
    inside = (frame >= 0) & (frame < live)
    feed = jnp.where(inside, feed, 0.0).astype(BF16).astype(F32)
    for i in range(tiles):
        feed_s[i, :ext, :] = feed[:, 128 * i : 128 * i + 128]
        feed_s[i, ext:, :] = jnp.zeros((feed_s.shape[1] - ext, 128), F32)
    rows = y_s.shape[0]
    low = low_lanes((rows, 128))
    low_out = low_lanes((80, 128))

    @pl.loop(0, tiles)
    def _(tile):
        lanes = pl.ds(pl.multiple_of(tile * 128, 128), 128)
        phase = [feed_s[tile, pl.ds(b, rows, stride=STRIDE), :] for b in range(STRIDE)]
        turned = [roll_half(p) for p in phase]
        even = [jnp.where(low, phase[b], turned[b + 1]) for b in (0, 2)]
        odd = [jnp.where(low, turned[b], phase[b + 1]) for b in (0, 2)]
        sums = []
        for g, pieces in enumerate((even, odd)):
            left = jnp.concatenate(pieces, axis=1).astype(BF16)
            y_s[...] = jnp.dot(left, conv_ref[2 * tile + g], preferred_element_type=F32)
            at, after = (None, None)
            for pair in range(TAP_SETS // 2):
                cols = slice(128 * pair, 128 * pair + 128)
                a = y_s[2 * pair : 2 * pair + 80, cols]
                b = y_s[2 * pair + 1 : 2 * pair + 81, cols]
                at = a if at is None else at + a
                after = b if after is None else after + b
            sums.append((at, after))
        pre_even = sums[0][0] + roll_half(sums[0][1])
        pre_odd = roll_half(sums[1][0]) + sums[1][1]
        pre_s[:, lanes] = jnp.where(low_out, pre_even, pre_odd)

    pre = pre_s[...]
    sig = 1.0 / (1.0 + jnp.exp(-pre))
    score = score_ref[...]
    critic = jnp.sum(pre * sig * score, axis=1, keepdims=True)
    slot = lax.broadcasted_iota(jnp.int32, (80, 1), 0)
    frame_out = first_frame - STRIDE * REACH + STRIDE * slot
    valid = (frame_out >= 0) & (frame_out < total_frames) & (frame_out < live) & (slot < own_out + 2 * REACH)
    shortfall = 1.0 - critic
    own = valid & (slot >= REACH) & (slot < REACH + own_out)
    loss = jnp.sum(jnp.where(own, shortfall * shortfall, 0.0), axis=0, keepdims=True)
    loss_ref[...] = jnp.broadcast_to(loss, loss_ref.shape)
    push = jnp.where(valid, -2.0 * shortfall, 0.0)
    grad = push * score * (sig * (1.0 + pre * (1.0 - sig)))
    grad = jnp.where(valid, grad, 0.0).astype(BF16).astype(F32)
    grad_s[:8, :] = jnp.zeros((8, grad_s.shape[1]), F32)
    grad_s[8:, :] = grad

    contract = (((1,), (1,)), ((), ()))
    low_back = low_lanes((own_out, 128))

    @pl.loop(0, tiles)
    def _(tile):
        lanes = pl.ds(pl.multiple_of(tile * 128, 128), 128)
        turned_s[...] = roll_half(grad_s[:, lanes])
        even, odd = ([], [])
        for pair in range(TAP_SETS // 2):
            up, down = (18 - 2 * pair, 17 - 2 * pair)
            even.append(
                jnp.where(low_back, grad_s[up : up + own_out, lanes], turned_s[down : down + own_out, :])
            )
            odd.append(
                jnp.where(low_back, turned_s[up : up + own_out, :], grad_s[down : down + own_out, lanes])
            )
        back = []
        for g, pieces in enumerate((even, odd)):
            left = jnp.concatenate(pieces, axis=1).astype(BF16)
            back.append(
                lax.dot_general(left, conv_ref[2 * tile + g], contract, preferred_element_type=F32)
            )
        step = lax.broadcasted_iota(jnp.int32, (own_out, 1), 0)
        for b in range(STRIDE):
            cols = slice(128 * (b // 2), 128 * (b // 2) + 128)
            e, o = (back[0][:, cols], back[1][:, cols])
            both = jnp.where(low_back, e, roll_half(o)) if b % 2 == 0 else jnp.where(low_back, roll_half(e), o)
            both = jnp.where(first_frame + STRIDE * step + b < live, both, 0.0)
            back_s[b * own_out : (b + 1) * own_out, lanes] = both.astype(BF16)

    for part, ref in enumerate((mine_ref, other_ref)):
        own_rows = ref[...].astype(F32)[HALO : ext - HALO, :]
        for c in range(HALF_HEADS):
            cols = slice(c * 128, c * 128 + 128)
            att_s[...] = own_rows[:, cols]
            left = jnp.concatenate(
                [att_s[pl.ds(b, own_out, stride=STRIDE), :] for b in range(STRIDE)], axis=0
            )
            left = jnp.transpose(left).astype(BF16)
            which = half if part == 0 else 1 - half
            out_ref[which, cols, :] = jnp.dot(left, back_s[...], preferred_element_type=F32)


def critic(meta, lifted, mine, other, proj, conv, score):
    ext, channels = lifted.shape
    own = ext - 2 * HALO
    return pl.pallas_call(
        critic_kernel,
        in_specs=[smem()] + [vmem()] * 6,
        out_specs=[vmem(), vmem()],
        out_shape=[
            jax.ShapeDtypeStruct((2, HALF_ATT, channels), F32),
            jax.ShapeDtypeStruct((8, 128), F32),
        ],
        scratch_shapes=[
            pltpu.VMEM((channels // 128, 384, 128), F32),
            pltpu.VMEM((96, TAP_SETS * 64), F32),
            pltpu.VMEM((80, channels), F32),
            pltpu.VMEM((88, channels), F32),
            pltpu.VMEM((88, 128), F32),
            pltpu.VMEM((own, channels), BF16),
            pltpu.VMEM((own, 128), F32),
        ],
        compiler_params=params(),
        cost_estimate=pl.CostEstimate(
            flops=3_000_000_000, bytes_accessed=14_000_000, transcendentals=100_000
        ),
    )(meta, lifted, mine, other, proj, conv, score)


def shards(
    states, kv_weight, queries, hidden, out_proj, disc_in, conv_weight, score_weight, frame_len, state_len
):
    frames = hidden.shape[1]
    dp_size, seq_size = (lax.axis_size("dp"), lax.axis_size("seq"))
    clip, seq = (lax.axis_index("dp"), lax.axis_index("seq"))
    core, half, row = (seq % 2, (seq // 2) % 2, seq // 4)
    pick = jnp.arange(frame_len.shape[0]) == clip
    clip_frames = jnp.sum(jnp.where(pick, frame_len, 0))
    clip_states = jnp.sum(jnp.where(pick, state_len, 0))

    def flip(x, bit):
        return lax.ppermute(x, "seq", [(i, i ^ bit) for i in range(seq_size)])

    def turn(x, hops):
        return lax.ppermute(x, "seq", [(i, (i + 4 * hops) % seq_size) for i in range(seq_size)])

    def across(x):
        pairs = []
        for i in range(dp_size * seq_size):
            d, s = divmod(i, seq_size)
            pairs.append((i, (d ^ 1) * seq_size + (s ^ 2)))
        return lax.ppermute(x, ("dp", "seq"), pairs)

    att = 2 * HALF_ATT
    own_cols = lax.dynamic_slice_in_dim(kv_weight, core * att, att, axis=1)
    partner_cols = lax.dynamic_slice_in_dim(kv_weight, (1 - core) * att, att, axis=1)
    pair_rows = jnp.concatenate([own_cols, flip(partner_cols, 1)], axis=0)
    near = lax.dynamic_slice_in_dim(pair_rows, half * HALF_ATT, HALF_ATT, axis=1)
    far = across(lax.dynamic_slice_in_dim(pair_rows, (1 - half) * HALF_ATT, HALF_ATT, axis=1))
    hops = (1, 3, 2)
    near_blocks = [near] + [turn(near, j) for j in hops]
    far_blocks = [far] + [turn(far, j) for j in hops]

    rows_in = jnp.concatenate([queries[0], hidden[0]], axis=1)
    up = [(i, i + 1) for i in range(seq_size - 1)]
    down = [(i + 1, i) for i in range(seq_size - 1)]
    before = lax.ppermute(rows_in[frames - HALO :], "seq", up)
    after = lax.ppermute(rows_in[:HALO], "seq", down)
    rows_ext = jnp.concatenate([before, rows_in, after], axis=0)
    query_ext, hidden_ext = (rows_ext[:, :att], rows_ext[:, att:])
    query_mine = lax.dynamic_slice_in_dim(query_ext, half * HALF_ATT, HALF_ATT, axis=1)
    query_far = flip(lax.dynamic_slice_in_dim(query_ext, (1 - half) * HALF_ATT, HALF_ATT, axis=1), 2)

    state_far = flip(states[0], 2)
    state_parts = [states[0], flip(states[0], 1), state_far, flip(state_far, 1)]

    proj_own = jnp.dot(out_proj, disc_in, preferred_element_type=F32).astype(BF16)
    proj = lax.all_gather(proj_own, "seq", axis=0, tiled=True).reshape(2, HALF_ATT, disc_in.shape[1])
    lifted = jnp.dot(hidden_ext, disc_in, preferred_element_type=F32)
    conv = arrange(conv_weight)

    cols = []
    for hop in (0,) + hops:
        for flip_half in (0, 1):
            for flip_core in (0, 1):
                where = (((row - hop) % 4) * 2 + (half ^ flip_half)) * 2 + (core ^ flip_core)
                cols.append(where * kv_weight.shape[0])
    blocks = [b for pair in zip(near_blocks, far_blocks) for b in pair]
    mine_kv = project(jnp.stack(cols).astype(jnp.int32), state_parts, blocks)
    got = [mine_kv] + [turn(mine_kv, j) for j in (1, 2, 3)]
    other = [flip(g, 1) for g in got]

    meta = jnp.stack([clip_states, core, half, row]).astype(jnp.int32)
    attended_far = flip(attend(meta, query_far, got, other), 2)
    attended_mine = attend(meta, query_mine, got, other)

    total_frames = frames * seq_size
    meta2 = jnp.stack([clip_frames, seq * frames, half, jnp.int32(total_frames)]).astype(jnp.int32)
    grown, loss = critic(
        meta2, lifted, attended_mine, attended_far, proj, conv, score_weight.reshape(1, -1)
    )

    own_rows = att // seq_size
    channels = disc_in.shape[1]

    def at(x, i):
        return lax.dynamic_index_in_dim(x, i, axis=0, keepdims=False)

    by_core = grown.reshape(seq_size // 2, 2, own_rows, channels)
    pick_core = lambda c: lax.dynamic_index_in_dim(by_core, c, axis=1, keepdims=False)
    total = pick_core(core) + flip(pick_core(1 - core), 1)
    loss = loss + flip(loss, 1)
    by_row = total.reshape(4, 2, own_rows, channels)
    sent = [turn(at(by_row, (row + j) % 4).astype(BF16), j) for j in (1, 2, 3)]
    sent_loss = [turn(loss, j) for j in (1, 2, 3)]
    total = at(by_row, row)
    for s, l in zip(sent, sent_loss):
        total, loss = (total + s.astype(F32), loss + l)
    total = at(total, half) + flip(at(total, 1 - half), 2)
    loss = loss + flip(loss, 2)
    share = own_rows // dp_size
    pieces = total.reshape(dp_size, share, channels)
    loss_row = jnp.broadcast_to(loss[:1, :1], (dp_size, 1, channels))
    pieces = lax.all_to_all(jnp.concatenate([pieces, loss_row], axis=1), "dp", 0, 0, tiled=True)
    pieces = jnp.sum(pieces, axis=0)
    total_loss = pieces[share, 0]
    spread = jnp.broadcast_to(pieces[None, :share], (dp_size, share, channels))
    full = lax.all_to_all(spread, "dp", 0, 0, tiled=True).reshape(own_rows, channels)
    high = lax.reduce_precision(full, 8, 7)
    high, low = (high.astype(BF16), (full - high).astype(BF16))
    contract = (((1,), (1,)), ((), ()))
    grad_proj = lax.dot_general(high, disc_in, contract, preferred_element_type=F32)
    grad_proj = grad_proj + lax.dot_general(low, disc_in, contract, preferred_element_type=F32)
    counted = jnp.sum((frame_len + STRIDE - 1) // STRIDE).astype(F32)
    return (grad_proj, total_loss / counted)


def solution(mesh):
    return jax.shard_map(
        shards,
        mesh=mesh,
        in_specs=(
            P("dp", "seq", None),
            P("seq", None),
            P("dp", "seq", None),
            P("dp", "seq", None),
            P("seq", None),
            P(),
            P(),
            P(),
            P(),
            P(),
        ),
        out_specs=(P("seq", None), P()),
        check_vma=False,
    )
```

```python
import functools
import math

import jax
import jax.numpy as jnp
from jax import lax
from jax.experimental import pallas as pl
from jax.experimental.pallas import tpu as pltpu
from jax.sharding import PartitionSpec as P

HEAD_DIM = 128
HALF_HEADS = 3
HALF_ATT = HEAD_DIM * HALF_HEADS
GROUP_CH = 64
STRIDE = 4
TAPS = 41
TAP_SETS = 12
MARGIN = 20
HALO = 40
REACH = 5
F32 = jnp.float32
BF16 = jnp.bfloat16
MIB = 1024 * 1024


def params(mib):
    return pltpu.CompilerParams(vmem_limit_bytes=mib * MIB)


def smem():
    return pl.BlockSpec(memory_space=pltpu.SMEM)


def vmem():
    return pl.BlockSpec(memory_space=pltpu.VMEM)


def anywhere():
    return pl.BlockSpec(memory_space=pltpu.HBM)


def low_lanes(shape):
    return lax.broadcasted_iota(jnp.int32, shape, 1) % 128 < 64


def roll_half(x):
    return pltpu.roll(x, 64, 1)


def arrange_kernel(w_ref, o_ref):
    low = low_lanes((GROUP_CH, 128))
    zero = jnp.zeros((GROUP_CH, 128), F32)

    def tap(k):
        return w_ref[k].astype(F32) if k < TAPS else zero

    for b in range(STRIDE):
        for pair in range(TAP_SETS // 2):
            first = tap(8 * pair + b)
            second = tap(8 * pair + 4 + b)
            rows, lanes = (slice(b * 64, b * 64 + 64), slice(pair * 128, pair * 128 + 128))
            o_ref[0, rows, lanes] = jnp.where(low, first, roll_half(second)).astype(BF16)
            o_ref[1, rows, lanes] = jnp.where(low, roll_half(first), second).astype(BF16)


def arrange(conv_weight):
    taps, group_in, channels = conv_weight.shape
    groups = channels // GROUP_CH
    return pl.pallas_call(
        arrange_kernel,
        grid=(channels // 128,),
        in_specs=[pl.BlockSpec((taps, group_in, 128), lambda l: (0, 0, l))],
        out_specs=pl.BlockSpec((2, STRIDE * 64, TAP_SETS * 64), lambda l: (l, 0, 0)),
        out_shape=jax.ShapeDtypeStruct((groups, STRIDE * 64, TAP_SETS * 64), BF16),
        compiler_params=params(58),
        cost_estimate=pl.CostEstimate(flops=20_000_000, bytes_accessed=20_000_000, transcendentals=0),
    )(conv_weight)


def project_kernel(cols_ref, *refs):
    states, weights, (keep_ref, send_ref) = (refs[:4], refs[4:12], refs[12:14])
    state_s, weight_s, total_s, state_sem, weight_sem = refs[14:]
    core = cols_ref[8]
    state_copies = [
        pltpu.make_async_copy(s, state_s.at[i], state_sem.at[i]) for i, s in enumerate(states)
    ]
    weight_copies = [
        pltpu.make_async_copy(w, weight_s.at[i], weight_sem.at[i]) for i, w in enumerate(weights)
    ]
    for copy in state_copies + weight_copies:
        copy.start()
    for copy in state_copies:
        copy.wait()
    for i, copy in enumerate(weight_copies):
        copy.wait()
        start = pl.multiple_of(cols_ref[i], 256)
        left = jnp.concatenate([state_s[j, :, pl.ds(start, 256)] for j in range(4)], axis=0)
        part = jnp.dot(left, weight_s[i], preferred_element_type=F32)
        if i == 0:
            total_s[...] = part
        else:
            total_s[...] += part
    kept = pl.ds(pl.multiple_of(core * HALF_ATT, 128), HALF_ATT)
    sent = pl.ds(pl.multiple_of((1 - core) * HALF_ATT, 128), HALF_ATT)
    for j in range(4):
        rows = slice(64 * j, 64 * j + 64)
        block = 2 * (j // 2) + (core + j) % 2
        keep_ref[block] = total_s[rows, kept]
        send_ref[block] = total_s[rows, sent]


def project(cols, states, weights):
    width = 2 * HALF_ATT
    out = jax.ShapeDtypeStruct((4, 64, HALF_ATT), F32)
    return pl.pallas_call(
        project_kernel,
        in_specs=[smem()] + [anywhere()] * 12,
        out_specs=[vmem(), vmem()],
        out_shape=[out, out],
        scratch_shapes=[
            pltpu.VMEM((4,) + states[0].shape, BF16),
            pltpu.VMEM((8,) + weights[0].shape, BF16),
            pltpu.VMEM((256, width), F32),
            pltpu.SemaphoreType.DMA((4,)),
            pltpu.SemaphoreType.DMA((8,)),
        ],
        compiler_params=params(58),
        cost_estimate=pl.CostEstimate(flops=800_000_000, bytes_accessed=6_000_000, transcendentals=0),
    )(cols, *states, *weights)


def split(x):
    high = x.astype(BF16)
    return high, (x - high.astype(F32)).astype(BF16)


def attend_kernel(meta_ref, q_ref, *refs):
    mine, other, o_ref = (refs[:4], refs[4:8], refs[8])
    live, core, half, row = (meta_ref[0], meta_ref[1], meta_ref[2], meta_ref[3])
    first = core == 0
    keys, values = ([], [])
    for m, o in zip(mine, other):
        keys.append(jnp.where(first, m[...], o[...]))
        values.append(jnp.where(first, o[...], m[...]))
    key_high, key_low = split(jnp.concatenate(keys, axis=0))
    value_high, value_low = split(jnp.concatenate(values, axis=0))
    spot = lax.broadcasted_iota(jnp.int32, (1, 1024), 1)
    hop, block, rest = (spot // 256, (spot // 64) % 4, spot % 64)
    where_y = (row - hop + 4) % 4
    where_h = (half + block // 2) % 2
    position = ((where_y * 2 + where_h) * 2 + block % 2) * 64 + rest
    alive = position < live
    contract = (((1,), (1,)), ((), ()))
    rows = 112
    for start in range(0, q_ref.shape[0], rows):
        q = q_ref[start : start + rows, :]
        scores = lax.dot_general(q, key_high, contract, preferred_element_type=F32)
        scores = scores + lax.dot_general(q, key_low, contract, preferred_element_type=F32)
        scores = jnp.where(alive, scores * (1.0 / math.sqrt(HEAD_DIM)), -1e30)
        top = jnp.max(scores, axis=1, keepdims=True)
        expo = jnp.where(alive, jnp.exp(scores - top), 0.0)
        denom = jnp.sum(expo, axis=1, keepdims=True)
        weights = expo.astype(BF16)
        mixed = jnp.dot(weights, value_high, preferred_element_type=F32)
        mixed = mixed + jnp.dot(weights, value_low, preferred_element_type=F32)
        o_ref[start : start + rows, :] = (mixed / denom).astype(BF16)


def attend(meta, query, mine, other):
    rows, width = query.shape
    block = lambda n: pl.BlockSpec((n, HEAD_DIM), lambda h: (0, h))
    return pl.pallas_call(
        attend_kernel,
        grid=(width // HEAD_DIM,),
        in_specs=[smem(), block(rows)] + [block(256)] * 8,
        out_specs=block(rows),
        out_shape=jax.ShapeDtypeStruct((rows, width), BF16),
        compiler_params=params(12),
        cost_estimate=pl.CostEstimate(
            flops=8 * rows * 1024 * width, bytes_accessed=4_000_000, transcendentals=rows * 3072
        ),
    )(meta, query, *mine, *other)


def coded_rows(value):
    high = value.astype(BF16).astype(F32)
    middle = (value - high).astype(BF16).astype(F32)
    low = value - high - middle
    line = lax.broadcasted_iota(jnp.int32, value.shape, 0)
    return jnp.where(line == 0, high, jnp.where(line == 1, middle, low)).astype(BF16)


def decoded_rows(rows):
    rows = rows.astype(F32)
    return (rows[0:1] + rows[1:2]) + rows[2:3]


def core_sum_kernel(meta_ref, kept_ref, arrived_ref, loss_ref, own_ref, *piece_refs):
    row = meta_ref[0]
    loss = loss_ref[:1] + decoded_rows(arrived_ref[384:, :])
    cells = coded_rows(jnp.broadcast_to(loss, (16, loss.shape[1])))
    for j in range(4):
        where = (row + j) % 4 if j == 0 else lax.bitwise_xor(row, j)
        for q in range(2):
            rows = pl.ds(pl.multiple_of(96 * where + 48 * q, 48), 48)
            total = kept_ref[2 * where + q] + arrived_ref[rows, :].astype(F32)
            if j == 0:
                own_ref[48 * q : 48 * q + 48, :] = total
            else:
                piece_refs[j - 1][48 * q : 48 * q + 48, :] = total.astype(BF16)
        if j == 0:
            own_ref[96:, :] = jnp.broadcast_to(loss, (8, loss.shape[1]))
        else:
            piece_refs[j - 1][96:, :] = cells


def core_sum(meta, kept, arrived, loss):
    channels = kept.shape[2]
    return pl.pallas_call(
        core_sum_kernel,
        in_specs=[smem()] + [vmem()] * 3,
        out_specs=[vmem()] * 4,
        out_shape=[jax.ShapeDtypeStruct((104, channels), F32)]
        + [jax.ShapeDtypeStruct((112, channels), BF16)] * 3,
        compiler_params=params(12),
        cost_estimate=pl.CostEstimate(flops=1_000_000, bytes_accessed=4_000_000, transcendentals=0),
    )(meta, kept, arrived, loss)


def row_sum_kernel(meta_ref, own_ref, one_ref, two_ref, three_ref, *out_refs):
    place = meta_ref[1]
    refs = (one_ref, two_ref, three_ref)
    first, second, third = [decoded_rows(r[96:, :]) for r in refs]
    loss = (own_ref[96:97, :] + first) + (second + third)
    for j in range(4):
        start = pl.multiple_of(24 * lax.bitwise_xor(place, j), 8)
        at = 48 * (lax.bitwise_xor(place, j) // 2)
        total = own_ref[pl.ds(start, 24), :]
        upper = lax.bitwise_xor(place, j) % 2 == 1
        for r in refs:
            rows = r[pl.ds(pl.multiple_of(at, 48), 48), :].astype(F32)
            total = total + jnp.where(upper, rows[24:], rows[:24])
        out_refs[j][:24, :] = total
        out_refs[j][24:, :] = jnp.broadcast_to(loss, (8, loss.shape[1]))


def row_sum(meta, own, arrived):
    channels = own.shape[1]
    return pl.pallas_call(
        row_sum_kernel,
        in_specs=[smem()] + [vmem()] * 4,
        out_specs=[vmem()] * 4,
        out_shape=[jax.ShapeDtypeStruct((32, channels), F32)] * 4,
        compiler_params=params(8),
        cost_estimate=pl.CostEstimate(flops=1_000_000, bytes_accessed=2_000_000, transcendentals=0),
    )(meta, own, *arrived)


def lift_kernel(full_ref, disc_ref, out_ref):
    rows = full_ref.shape[0]
    both = jnp.concatenate(split(full_ref[...]), axis=0)
    wide = disc_ref.shape[0] // 3
    for i in range(3):
        cols = slice(wide * i, wide * i + wide)
        product = lax.dot_general(
            both, disc_ref[cols, :], (((1,), (1,)), ((), ())), preferred_element_type=F32
        )
        out_ref[:, cols] = product[:rows] + product[rows:]


def lift(full, disc_in):
    return pl.pallas_call(
        lift_kernel,
        in_specs=[vmem()] * 2,
        out_specs=vmem(),
        out_shape=jax.ShapeDtypeStruct((full.shape[0], disc_in.shape[0]), F32),
        compiler_params=params(12),
        cost_estimate=pl.CostEstimate(flops=300_000_000, bytes_accessed=3_500_000, transcendentals=0),
    )(full, disc_in)


def critic_kernel(
    meta_ref, lifted_hbm, mine_hbm, other_hbm, proj_0, proj_1, proj_2, proj_3, conv_hbm, score_ref,
    keep_ref, send_ref, loss_ref,
    feed_s, y_s, pre_s, grad_s, turned_s, back_s, att_s, proj_s, conv_ref, lifted_ref, mine_ref, other_ref, proj_sem, conv_sem,
):
    live, first_frame, half = (meta_ref[0], meta_ref[1], meta_ref[2])
    total_frames, core = (meta_ref[3], meta_ref[4])
    row = meta_ref[5]
    pairs = [(lifted_hbm, lifted_ref), (mine_hbm, mine_ref), (other_hbm, other_ref)]
    for hop, block in enumerate((proj_0, proj_1, proj_2, proj_3)):
        for j in range(4):
            where = ((row - hop + 4) % 4) * 4 + ((half + j) % 2) * 2 + (core + j // 2) % 2
            pairs.append((block.at[j], proj_s.at[where]))
    proj_copies = [pltpu.make_async_copy(a, b, proj_sem.at[i]) for i, (a, b) in enumerate(pairs)]
    conv_copies = [
        pltpu.make_async_copy(conv_hbm.at[g], conv_ref.at[g], conv_sem.at[g])
        for g in range(conv_ref.shape[0])
    ]
    for copy in proj_copies + conv_copies:
        copy.start()
    ext = lifted_ref.shape[0]
    own_out = (ext - 2 * HALO) // STRIDE
    tiles = lifted_ref.shape[1] // 128
    for copy in proj_copies:
        copy.wait()
    feed = lifted_ref[...]
    for ref, which in ((mine_ref, half), (other_ref, 1 - half)):
        proj = proj_s[pl.ds(8 * which, 8)].reshape(HALF_ATT, lifted_ref.shape[1])
        feed = feed + jnp.dot(ref[...], proj, preferred_element_type=F32)
    frame = first_frame - HALO + lax.broadcasted_iota(jnp.int32, (ext, 1), 0)
    inside = (frame >= 0) & (frame < live)
    feed = jnp.where(inside, feed, 0.0).astype(BF16).astype(F32)
    for i in range(tiles):
        feed_s[i, :ext, :] = feed[:, 128 * i : 128 * i + 128]
        feed_s[i, ext:, :] = jnp.zeros((feed_s.shape[1] - ext, 128), F32)
    rows = y_s.shape[0]
    low = low_lanes((rows, 128))
    low_out = low_lanes((80, 128))
    for copy in conv_copies:
        copy.wait()

    @pl.loop(0, tiles)
    def _(tile):
        lanes = pl.ds(pl.multiple_of(tile * 128, 128), 128)
        phase = [feed_s[tile, pl.ds(b, rows, stride=STRIDE), :] for b in range(STRIDE)]
        turned = [roll_half(p) for p in phase]
        even = [jnp.where(low, phase[b], turned[b + 1]) for b in (0, 2)]
        odd = [jnp.where(low, turned[b], phase[b + 1]) for b in (0, 2)]
        sums = []
        for g, pieces in enumerate((even, odd)):
            left = jnp.concatenate(pieces, axis=1).astype(BF16)
            y_s[...] = jnp.dot(left, conv_ref[2 * tile + g], preferred_element_type=F32)
            at, after = (None, None)
            for pair in range(TAP_SETS // 2):
                cols = slice(128 * pair, 128 * pair + 128)
                a = y_s[2 * pair : 2 * pair + 80, cols]
                b = y_s[2 * pair + 1 : 2 * pair + 81, cols]
                at = a if at is None else at + a
                after = b if after is None else after + b
            sums.append((at, after))
        pre_even = sums[0][0] + roll_half(sums[0][1])
        pre_odd = roll_half(sums[1][0]) + sums[1][1]
        pre_s[:, lanes] = jnp.where(low_out, pre_even, pre_odd)

    pre = pre_s[...]
    sig = 1.0 / (1.0 + jnp.exp(-pre))
    score = score_ref[...]
    critic = jnp.sum(pre * sig * score, axis=1, keepdims=True)
    slot = lax.broadcasted_iota(jnp.int32, (80, 1), 0)
    frame_out = first_frame - STRIDE * REACH + STRIDE * slot
    valid = (frame_out >= 0) & (frame_out < total_frames) & (frame_out < live) & (slot < own_out + 2 * REACH)
    shortfall = 1.0 - critic
    own = valid & (slot >= REACH) & (slot < REACH + own_out)
    loss = jnp.sum(jnp.where(own, shortfall * shortfall, 0.0), axis=0, keepdims=True)
    loss_ref[...] = jnp.broadcast_to(loss, loss_ref.shape)
    send_ref[384:, :] = coded_rows(jnp.broadcast_to(loss, (16, send_ref.shape[1])))
    push = jnp.where(valid, -2.0 * shortfall, 0.0)
    grad = push * score * (sig * (1.0 + pre * (1.0 - sig)))
    grad = jnp.where(valid, grad, 0.0).astype(BF16).astype(F32)
    grad_s[:8, :] = jnp.zeros((8, grad_s.shape[1]), F32)
    grad_s[8:, :] = grad

    contract = (((1,), (1,)), ((), ()))
    low_back = low_lanes((own_out, 128))

    @pl.loop(0, tiles)
    def _(tile):
        lanes = pl.ds(pl.multiple_of(tile * 128, 128), 128)
        turned_s[...] = roll_half(grad_s[:, lanes])
        even, odd = ([], [])
        for pair in range(TAP_SETS // 2):
            up, down = (18 - 2 * pair, 17 - 2 * pair)
            even.append(
                jnp.where(low_back, grad_s[up : up + own_out, lanes], turned_s[down : down + own_out, :])
            )
            odd.append(
                jnp.where(low_back, turned_s[up : up + own_out, :], grad_s[down : down + own_out, lanes])
            )
        back = []
        for g, pieces in enumerate((even, odd)):
            left = jnp.concatenate(pieces, axis=1).astype(BF16)
            back.append(
                lax.dot_general(left, conv_ref[2 * tile + g], contract, preferred_element_type=F32)
            )
        step = lax.broadcasted_iota(jnp.int32, (own_out, 1), 0)
        for b in range(STRIDE):
            cols = slice(128 * (b // 2), 128 * (b // 2) + 128)
            e, o = (back[0][:, cols], back[1][:, cols])
            both = jnp.where(low_back, e, roll_half(o)) if b % 2 == 0 else jnp.where(low_back, roll_half(e), o)
            both = jnp.where(first_frame + STRIDE * step + b < live, both, 0.0)
            back_s[b * own_out : (b + 1) * own_out, lanes] = both.astype(BF16)

    first = core == 0
    for part, ref in enumerate((mine_ref, other_ref)):
        own_rows = ref[...].astype(F32)[HALO : ext - HALO, :]
        lefts = []
        for c in range(HALF_HEADS):
            att_s[...] = own_rows[:, c * 128 : c * 128 + 128]
            left = jnp.concatenate(
                [att_s[pl.ds(b, own_out, stride=STRIDE), :] for b in range(STRIDE)], axis=0
            )
            lefts.append(jnp.transpose(left))
        left = jnp.concatenate(lefts, axis=0).astype(BF16)
        which = half if part == 0 else 1 - half
        for q in range(4):
            block = jnp.dot(left[96 * q : 96 * q + 96], back_s[...], preferred_element_type=F32)
            one, two = (block[:48], block[48:])
            keep_ref[4 * which + q] = jnp.where(first, one, two)
            rows = pl.ds(pl.multiple_of(48 * (4 * which + q), 48), 48)
            send_ref[rows, :] = jnp.where(first, two, one).astype(BF16)


def critic(meta, lifted, mine, other, proj, conv, score):
    ext, channels = lifted.shape
    own = ext - 2 * HALO
    return pl.pallas_call(
        critic_kernel,
        in_specs=[smem()] + [anywhere()] * 8 + [vmem()],
        out_specs=[vmem(), vmem(), vmem()],
        out_shape=[
            jax.ShapeDtypeStruct((8, 48, channels), F32),
            jax.ShapeDtypeStruct((400, channels), BF16),
            jax.ShapeDtypeStruct((8, channels), F32),
        ],
        scratch_shapes=[
            pltpu.VMEM((channels // 128, 384, 128), F32),
            pltpu.VMEM((96, TAP_SETS * 64), F32),
            pltpu.VMEM((80, channels), F32),
            pltpu.VMEM((88, channels), F32),
            pltpu.VMEM((88, 128), F32),
            pltpu.VMEM((own, channels), BF16),
            pltpu.VMEM((own, 128), F32),
            pltpu.VMEM((16, 48, channels), BF16),
            pltpu.VMEM(conv.shape, BF16),
            pltpu.VMEM(lifted.shape, F32),
            pltpu.VMEM(mine.shape, BF16),
            pltpu.VMEM(other.shape, BF16),
            pltpu.SemaphoreType.DMA((19,)),
            pltpu.SemaphoreType.DMA((conv.shape[0],)),
        ],
        compiler_params=params(58),
        cost_estimate=pl.CostEstimate(
            flops=3_000_000_000, bytes_accessed=14_000_000, transcendentals=100_000
        ),
    )(meta, lifted, mine, other, *proj, conv, score)


def shards(
    states, kv_weight, queries, hidden, out_proj, disc_in, conv_weight, score_weight, frame_len, state_len
):
    frames = hidden.shape[1]
    dp_size, seq_size = (lax.axis_size("dp"), lax.axis_size("seq"))
    clip, seq = (lax.axis_index("dp"), lax.axis_index("seq"))
    core, half, row = (seq % 2, (seq // 2) % 2, seq // 4)
    pick = jnp.arange(frame_len.shape[0]) == clip
    clip_frames = jnp.sum(jnp.where(pick, frame_len, 0))
    clip_states = jnp.sum(jnp.where(pick, state_len, 0))

    def flip(x, bit):
        return lax.ppermute(x, "seq", [(i, i ^ bit) for i in range(seq_size)])

    def turn(x, hops):
        return lax.ppermute(x, "seq", [(i, (i + 4 * hops) % seq_size) for i in range(seq_size)])

    def swap(x, dp_bits, seq_bits):
        pairs = []
        for i in range(dp_size * seq_size):
            d, q = divmod(i, seq_size)
            pairs.append((i, (d ^ dp_bits) * seq_size + (q ^ seq_bits)))
        return lax.ppermute(x, ("dp", "seq"), pairs)

    def at(x, i):
        return lax.dynamic_index_in_dim(x, i, axis=0, keepdims=False)

    att = 2 * HALF_ATT

    def head_cols(which):
        parts = [
            lax.dynamic_slice_in_dim(kv_weight, kind * att + which * HALF_ATT, HALF_ATT, axis=1)
            for kind in (0, 1)
        ]
        return jnp.concatenate(parts, axis=1)

    near = head_cols(half)
    far = swap(head_cols(1 - half), 1, 2)
    hops = (1, 3, 2)
    near_turned = [turn(near, j) for j in hops]
    near, near_turned, far, states_in, queries_in, hidden_in, proj_in = lax.optimization_barrier(
        (near, near_turned, far, states[0], queries[0], hidden[0], out_proj)
    )

    lower = clip % 2
    channels = disc_in.shape[1]
    near_blocks = [near] + near_turned
    far_blocks = [far] + [turn(far, j) for j in hops]
    state_far = flip(states_in, 2)
    state_near = flip(states_in, 1)
    proj_own = jnp.dot(proj_in, disc_in, preferred_element_type=F32).astype(BF16)
    proj_far = swap(proj_own, 1, 2)
    up = [(i, i + 1) for i in range(seq_size - 1)]
    down = [(i + 1, i) for i in range(seq_size - 1)]
    before = jnp.concatenate([queries_in[frames - HALO :], hidden_in[frames - HALO :]], axis=1)
    after = jnp.concatenate([queries_in[:HALO], hidden_in[:HALO]], axis=1)
    before, after = (lax.ppermute(before, "seq", up), lax.ppermute(after, "seq", down))
    query_ext = jnp.concatenate([before[:, :att], queries_in, after[:, :att]], axis=0)
    hidden_ext = jnp.concatenate([before[:, att:], hidden_in, after[:, att:]], axis=0)
    query_mine = lax.dynamic_slice_in_dim(query_ext, half * HALF_ATT, HALF_ATT, axis=1)
    query_sent = lax.dynamic_slice_in_dim(query_ext, (1 - half) * HALF_ATT, HALF_ATT, axis=1)
    lifted = jnp.dot(hidden_ext, disc_in, preferred_element_type=F32)

    cols = []
    for hop in (0, 1, 3, 2):
        for flip_half in (0, 1):
            where = (((row - hop) % 4) * 2 + (half ^ flip_half)) * 2 + core
            cols.append(where * kv_weight.shape[0])
    total_frames = frames * seq_size
    cols = jnp.stack(cols + [core]).astype(jnp.int32)
    meta = jnp.stack([clip_states, core, half, row]).astype(jnp.int32)
    meta2 = jnp.stack([clip_frames, seq * frames, half, jnp.int32(total_frames), core, row])
    meta3 = jnp.stack([row, 2 * half + lower, clip // 2]).astype(jnp.int32)
    blocks = [b for pair in zip(near_blocks, far_blocks) for b in pair]
    tables = (cols, meta, meta2.astype(jnp.int32), meta3)
    blocks, state_far, state_near, tables, proj_far, query_mine, query_sent, lifted = lax.optimization_barrier(
        (blocks, state_far, state_near, tables, proj_far, query_mine, query_sent, lifted)
    )
    cols, meta, meta2, meta3 = tables
    state_parts = [states_in, state_near, state_far, flip(state_far, 1)]
    kept, sent = project(cols, state_parts, blocks)
    mine_kv = (kept + flip(sent, 1)).reshape(256, HALF_ATT)

    mine_kv, conv_in, query_sent, proj_own, proj_far = lax.optimization_barrier(
        (mine_kv, conv_weight, query_sent, proj_own, proj_far)
    )
    got = [mine_kv] + [turn(mine_kv, j) for j in (1, 2, 3)]
    query_far = flip(query_sent, 2)
    proj_pair = jnp.stack([proj_own, proj_far])
    proj_quad = jnp.concatenate([proj_pair, flip(proj_pair, 1)], axis=0)
    conv = arrange(conv_in)
    got, conv, query_far, proj_quad = lax.optimization_barrier((got, conv, query_far, proj_quad))
    other = [flip(g, 1) for g in got]
    proj = [proj_quad] + [turn(proj_quad, j) for j in (1, 2, 3)]

    attended_far = flip(attend(meta, query_far, got, other), 2)
    attended_mine = attend(meta, query_mine, got, other)

    kept, sent, loss = critic(
        meta2, lifted, attended_mine, attended_far, proj, conv, score_weight.reshape(1, -1)
    )

    own_rows = att // seq_size
    share = own_rows // 2
    own, *pieces = core_sum(meta3, kept, flip(sent, 1), loss)
    arrived = [flip(p, 4 * (j + 1)) for j, p in enumerate(pieces)]
    own, *pieces = row_sum(meta3, own, arrived)
    a, b, c = [swap(p, j & 1, j & 2) for j, p in zip((1, 2, 3), pieces)]
    total = (own + a) + (b + c)
    a, b, c = [swap(total, d, 0) for d in (2, 4, 6)]
    total = (total + a) + (b + c)
    total = total + swap(total, 8, 0)
    total_loss = total[share, 0]
    total = total[:share]
    beside = swap(total, 1, 0)
    first = lower == 0
    total = jnp.concatenate([jnp.where(first, total, beside), jnp.where(first, beside, total)], axis=0)
    grad_proj = lift(total, disc_in)
    counted = jnp.sum((frame_len + STRIDE - 1) // STRIDE).astype(F32)
    return (grad_proj, total_loss / counted)


def solution(mesh):
    return jax.shard_map(
        shards,
        mesh=mesh,
        in_specs=(
            P("dp", "seq", None),
            P("seq", None),
            P("dp", "seq", None),
            P("dp", "seq", None),
            P("seq", None),
            P(),
            P(),
            P(),
            P(),
            P(),
        ),
        out_specs=(P("seq", None), P()),
        check_vma=False,
    )
```

```python
import functools
import math

import jax
import jax.numpy as jnp
from jax import lax
from jax.experimental import pallas as pl
from jax.experimental.pallas import tpu as pltpu
from jax.sharding import PartitionSpec as P

HEAD_DIM = 128
HALF_HEADS = 3
HALF_ATT = HEAD_DIM * HALF_HEADS
GROUP_CH = 64
STRIDE = 4
TAPS = 41
TAP_SETS = 12
MARGIN = 20
HALO = 40
REACH = 5
F32 = jnp.float32
BF16 = jnp.bfloat16
MIB = 1024 * 1024


def params(mib):
    return pltpu.CompilerParams(vmem_limit_bytes=mib * MIB)


def smem():
    return pl.BlockSpec(memory_space=pltpu.SMEM)


def vmem():
    return pl.BlockSpec(memory_space=pltpu.VMEM)


def anywhere():
    return pl.BlockSpec(memory_space=pltpu.HBM)


def low_lanes(shape):
    return lax.broadcasted_iota(jnp.int32, shape, 1) % 128 < 64


def roll_half(x):
    return pltpu.roll(x, 64, 1)


def arrange_kernel(w_ref, o_ref):
    low = low_lanes((GROUP_CH, 128))
    zero = jnp.zeros((GROUP_CH, 128), F32)

    def tap(k):
        return w_ref[k].astype(F32) if k < TAPS else zero

    for b in range(STRIDE):
        for pair in range(TAP_SETS // 2):
            first = tap(8 * pair + b)
            second = tap(8 * pair + 4 + b)
            rows, lanes = (slice(b * 64, b * 64 + 64), slice(pair * 128, pair * 128 + 128))
            o_ref[0, rows, lanes] = jnp.where(low, first, roll_half(second)).astype(BF16)
            o_ref[1, rows, lanes] = jnp.where(low, roll_half(first), second).astype(BF16)


def arrange(conv_weight):
    taps, group_in, channels = conv_weight.shape
    groups = channels // GROUP_CH
    return pl.pallas_call(
        arrange_kernel,
        grid=(channels // 128,),
        in_specs=[pl.BlockSpec((taps, group_in, 128), lambda l: (0, 0, l))],
        out_specs=pl.BlockSpec((2, STRIDE * 64, TAP_SETS * 64), lambda l: (l, 0, 0)),
        out_shape=jax.ShapeDtypeStruct((groups, STRIDE * 64, TAP_SETS * 64), BF16),
        compiler_params=params(58),
        cost_estimate=pl.CostEstimate(flops=20_000_000, bytes_accessed=20_000_000, transcendentals=0),
    )(conv_weight)


def project_kernel(cols_ref, *refs):
    states, weights, (keep_ref, send_ref) = (refs[:4], refs[4:12], refs[12:14])
    state_s, weight_s, total_s, state_sem, weight_sem = refs[14:]
    core = cols_ref[8]
    state_copies = [
        pltpu.make_async_copy(s, state_s.at[i], state_sem.at[i]) for i, s in enumerate(states)
    ]
    weight_copies = [
        pltpu.make_async_copy(w, weight_s.at[i], weight_sem.at[i]) for i, w in enumerate(weights)
    ]
    for copy in state_copies + weight_copies:
        copy.start()
    for copy in state_copies:
        copy.wait()
    for i, copy in enumerate(weight_copies):
        copy.wait()
        start = pl.multiple_of(cols_ref[i], 256)
        left = jnp.concatenate([state_s[j, :, pl.ds(start, 256)] for j in range(4)], axis=0)
        part = jnp.dot(left, weight_s[i], preferred_element_type=F32)
        if i == 0:
            total_s[...] = part
        else:
            total_s[...] += part
    kept = pl.ds(pl.multiple_of(core * HALF_ATT, 128), HALF_ATT)
    sent = pl.ds(pl.multiple_of((1 - core) * HALF_ATT, 128), HALF_ATT)
    for j in range(4):
        rows = slice(64 * j, 64 * j + 64)
        block = 2 * (j // 2) + (core + j) % 2
        keep_ref[block] = total_s[rows, kept]
        send_ref[block] = total_s[rows, sent]


def project(cols, states, weights):
    width = 2 * HALF_ATT
    out = jax.ShapeDtypeStruct((4, 64, HALF_ATT), F32)
    return pl.pallas_call(
        project_kernel,
        in_specs=[smem()] + [anywhere()] * 12,
        out_specs=[vmem(), vmem()],
        out_shape=[out, out],
        scratch_shapes=[
            pltpu.VMEM((4,) + states[0].shape, BF16),
            pltpu.VMEM((8,) + weights[0].shape, BF16),
            pltpu.VMEM((256, width), F32),
            pltpu.SemaphoreType.DMA((4,)),
            pltpu.SemaphoreType.DMA((8,)),
        ],
        compiler_params=params(58),
        cost_estimate=pl.CostEstimate(flops=800_000_000, bytes_accessed=6_000_000, transcendentals=0),
    )(cols, *states, *weights)


def split(x):
    high = x.astype(BF16)
    return high, (x - high.astype(F32)).astype(BF16)


def attend_kernel(meta_ref, q_ref, *refs):
    mine, other, o_ref = (refs[:4], refs[4:8], refs[8])
    live, core, half, row = (meta_ref[0], meta_ref[1], meta_ref[2], meta_ref[3])
    first = core == 0
    keys, values = ([], [])
    for m, o in zip(mine, other):
        keys.append(jnp.where(first, m[...], o[...]))
        values.append(jnp.where(first, o[...], m[...]))
    key_high, key_low = split(jnp.concatenate(keys, axis=0))
    value_high, value_low = split(jnp.concatenate(values, axis=0))
    spot = lax.broadcasted_iota(jnp.int32, (1, 1024), 1)
    hop, block, rest = (spot // 256, (spot // 64) % 4, spot % 64)
    where_y = (row - hop + 4) % 4
    where_h = (half + block // 2) % 2
    position = ((where_y * 2 + where_h) * 2 + block % 2) * 64 + rest
    alive = position < live
    contract = (((1,), (1,)), ((), ()))
    rows = 112
    for start in range(0, q_ref.shape[0], rows):
        q = q_ref[start : start + rows, :]
        scores = lax.dot_general(q, key_high, contract, preferred_element_type=F32)
        scores = scores + lax.dot_general(q, key_low, contract, preferred_element_type=F32)
        scores = jnp.where(alive, scores * (1.0 / math.sqrt(HEAD_DIM)), -1e30)
        top = jnp.max(scores, axis=1, keepdims=True)
        expo = jnp.where(alive, jnp.exp(scores - top), 0.0)
        denom = jnp.sum(expo, axis=1, keepdims=True)
        weights = expo.astype(BF16)
        mixed = jnp.dot(weights, value_high, preferred_element_type=F32)
        mixed = mixed + jnp.dot(weights, value_low, preferred_element_type=F32)
        o_ref[start : start + rows, :] = (mixed / denom).astype(BF16)


def attend(meta, query, mine, other):
    rows, width = query.shape
    block = lambda n: pl.BlockSpec((n, HEAD_DIM), lambda h: (0, h))
    return pl.pallas_call(
        attend_kernel,
        grid=(width // HEAD_DIM,),
        in_specs=[smem(), block(rows)] + [block(256)] * 8,
        out_specs=block(rows),
        out_shape=jax.ShapeDtypeStruct((rows, width), BF16),
        compiler_params=params(12),
        cost_estimate=pl.CostEstimate(
            flops=8 * rows * 1024 * width, bytes_accessed=4_000_000, transcendentals=rows * 3072
        ),
    )(meta, query, *mine, *other)


def coded_rows(value):
    high = value.astype(BF16).astype(F32)
    middle = (value - high).astype(BF16).astype(F32)
    low = value - high - middle
    line = lax.broadcasted_iota(jnp.int32, value.shape, 0)
    return jnp.where(line == 0, high, jnp.where(line == 1, middle, low)).astype(BF16)


def decoded_rows(rows):
    rows = rows.astype(F32)
    return (rows[0:1] + rows[1:2]) + rows[2:3]


def core_sum_kernel(meta_ref, kept_ref, arrived_ref, loss_ref, own_ref, *piece_refs):
    row = meta_ref[0]
    loss = loss_ref[:1] + decoded_rows(arrived_ref[384:, :])
    cells = coded_rows(jnp.broadcast_to(loss, (16, loss.shape[1])))
    for j in range(4):
        where = (row + j) % 4 if j == 0 else lax.bitwise_xor(row, j)
        for q in range(2):
            rows = pl.ds(pl.multiple_of(96 * where + 48 * q, 48), 48)
            total = kept_ref[2 * where + q] + arrived_ref[rows, :].astype(F32)
            if j == 0:
                own_ref[48 * q : 48 * q + 48, :] = total
            else:
                piece_refs[j - 1][48 * q : 48 * q + 48, :] = total.astype(BF16)
        if j == 0:
            own_ref[96:, :] = jnp.broadcast_to(loss, (8, loss.shape[1]))
        else:
            piece_refs[j - 1][96:, :] = cells


def core_sum(meta, kept, arrived, loss):
    channels = kept.shape[2]
    return pl.pallas_call(
        core_sum_kernel,
        in_specs=[smem()] + [vmem()] * 3,
        out_specs=[vmem()] * 4,
        out_shape=[jax.ShapeDtypeStruct((104, channels), F32)]
        + [jax.ShapeDtypeStruct((112, channels), BF16)] * 3,
        compiler_params=params(12),
        cost_estimate=pl.CostEstimate(flops=1_000_000, bytes_accessed=4_000_000, transcendentals=0),
    )(meta, kept, arrived, loss)


def row_sum_kernel(meta_ref, own_ref, one_ref, two_ref, three_ref, *out_refs):
    place = meta_ref[1]
    refs = (one_ref, two_ref, three_ref)
    first, second, third = [decoded_rows(r[96:, :]) for r in refs]
    loss = (own_ref[96:97, :] + first) + (second + third)
    for j in range(4):
        start = pl.multiple_of(24 * lax.bitwise_xor(place, j), 8)
        at = 48 * (lax.bitwise_xor(place, j) // 2)
        total = own_ref[pl.ds(start, 24), :]
        upper = lax.bitwise_xor(place, j) % 2 == 1
        for r in refs:
            rows = r[pl.ds(pl.multiple_of(at, 48), 48), :].astype(F32)
            total = total + jnp.where(upper, rows[24:], rows[:24])
        out_refs[j][:24, :] = total
        out_refs[j][24:, :] = jnp.broadcast_to(loss, (8, loss.shape[1]))


def row_sum(meta, own, arrived):
    channels = own.shape[1]
    return pl.pallas_call(
        row_sum_kernel,
        in_specs=[smem()] + [vmem()] * 4,
        out_specs=[vmem()] * 4,
        out_shape=[jax.ShapeDtypeStruct((32, channels), F32)] * 4,
        compiler_params=params(8),
        cost_estimate=pl.CostEstimate(flops=1_000_000, bytes_accessed=2_000_000, transcendentals=0),
    )(meta, own, *arrived)


def lift_kernel(full_ref, disc_ref, out_ref):
    rows = full_ref.shape[0]
    both = jnp.concatenate(split(full_ref[...]), axis=0)
    wide = disc_ref.shape[0] // 3
    for i in range(3):
        cols = slice(wide * i, wide * i + wide)
        product = lax.dot_general(
            both, disc_ref[cols, :], (((1,), (1,)), ((), ())), preferred_element_type=F32
        )
        out_ref[:, cols] = product[:rows] + product[rows:]


def lift(full, disc_in):
    return pl.pallas_call(
        lift_kernel,
        in_specs=[vmem()] * 2,
        out_specs=vmem(),
        out_shape=jax.ShapeDtypeStruct((full.shape[0], disc_in.shape[0]), F32),
        compiler_params=params(12),
        cost_estimate=pl.CostEstimate(flops=300_000_000, bytes_accessed=3_500_000, transcendentals=0),
    )(full, disc_in)


def critic_kernel(
    meta_ref, lifted_hbm, mine_hbm, other_hbm, proj_hbm, conv_hbm, score_ref,
    keep_ref, send_ref, loss_ref,
    feed_s, y_s, pre_s, grad_s, turned_s, back_s, att_s, proj_s, conv_ref, lifted_ref, mine_ref, other_ref, proj_sem, conv_sem,
):
    live, first_frame, half = (meta_ref[0], meta_ref[1], meta_ref[2])
    total_frames, core = (meta_ref[3], meta_ref[4])
    pairs = [(lifted_hbm, lifted_ref), (mine_hbm, mine_ref), (other_hbm, other_ref), (proj_hbm, proj_s)]
    proj_copies = [pltpu.make_async_copy(a, b, proj_sem.at[i]) for i, (a, b) in enumerate(pairs)]
    conv_copies = [
        pltpu.make_async_copy(conv_hbm.at[g], conv_ref.at[g], conv_sem.at[g])
        for g in range(conv_ref.shape[0])
    ]
    for copy in proj_copies + conv_copies:
        copy.start()
    ext = lifted_ref.shape[0]
    own_out = (ext - 2 * HALO) // STRIDE
    tiles = lifted_ref.shape[1] // 128
    for copy in proj_copies:
        copy.wait()
    feed = lifted_ref[...]
    for ref, which in ((mine_ref, half), (other_ref, 1 - half)):
        proj = proj_s[pl.ds(pl.multiple_of(HALF_ATT * which, HALF_ATT), HALF_ATT), :]
        feed = feed + jnp.dot(ref[...], proj, preferred_element_type=F32)
    frame = first_frame - HALO + lax.broadcasted_iota(jnp.int32, (ext, 1), 0)
    inside = (frame >= 0) & (frame < live)
    feed = jnp.where(inside, feed, 0.0).astype(BF16).astype(F32)
    for i in range(tiles):
        feed_s[i, :ext, :] = feed[:, 128 * i : 128 * i + 128]
        feed_s[i, ext:, :] = jnp.zeros((feed_s.shape[1] - ext, 128), F32)
    rows = y_s.shape[0]
    low = low_lanes((rows, 128))
    low_out = low_lanes((80, 128))
    for copy in conv_copies:
        copy.wait()

    @pl.loop(0, tiles)
    def _(tile):
        lanes = pl.ds(pl.multiple_of(tile * 128, 128), 128)
        phase = [feed_s[tile, pl.ds(b, rows, stride=STRIDE), :] for b in range(STRIDE)]
        turned = [roll_half(p) for p in phase]
        even = [jnp.where(low, phase[b], turned[b + 1]) for b in (0, 2)]
        odd = [jnp.where(low, turned[b], phase[b + 1]) for b in (0, 2)]
        sums = []
        for g, pieces in enumerate((even, odd)):
            left = jnp.concatenate(pieces, axis=1).astype(BF16)
            y_s[...] = jnp.dot(left, conv_ref[2 * tile + g], preferred_element_type=F32)
            at, after = (None, None)
            for pair in range(TAP_SETS // 2):
                cols = slice(128 * pair, 128 * pair + 128)
                a = y_s[2 * pair : 2 * pair + 80, cols]
                b = y_s[2 * pair + 1 : 2 * pair + 81, cols]
                at = a if at is None else at + a
                after = b if after is None else after + b
            sums.append((at, after))
        pre_even = sums[0][0] + roll_half(sums[0][1])
        pre_odd = roll_half(sums[1][0]) + sums[1][1]
        pre_s[:, lanes] = jnp.where(low_out, pre_even, pre_odd)

    pre = pre_s[...]
    sig = 1.0 / (1.0 + jnp.exp(-pre))
    score = score_ref[...]
    critic = jnp.sum(pre * sig * score, axis=1, keepdims=True)
    slot = lax.broadcasted_iota(jnp.int32, (80, 1), 0)
    frame_out = first_frame - STRIDE * REACH + STRIDE * slot
    valid = (frame_out >= 0) & (frame_out < total_frames) & (frame_out < live) & (slot < own_out + 2 * REACH)
    shortfall = 1.0 - critic
    own = valid & (slot >= REACH) & (slot < REACH + own_out)
    loss = jnp.sum(jnp.where(own, shortfall * shortfall, 0.0), axis=0, keepdims=True)
    loss_ref[...] = jnp.broadcast_to(loss, loss_ref.shape)
    send_ref[384:, :] = coded_rows(jnp.broadcast_to(loss, (16, send_ref.shape[1])))
    push = jnp.where(valid, -2.0 * shortfall, 0.0)
    grad = push * score * (sig * (1.0 + pre * (1.0 - sig)))
    grad = jnp.where(valid, grad, 0.0).astype(BF16).astype(F32)
    grad_s[:8, :] = jnp.zeros((8, grad_s.shape[1]), F32)
    grad_s[8:, :] = grad

    contract = (((1,), (1,)), ((), ()))
    low_back = low_lanes((own_out, 128))

    @pl.loop(0, tiles)
    def _(tile):
        lanes = pl.ds(pl.multiple_of(tile * 128, 128), 128)
        turned_s[...] = roll_half(grad_s[:, lanes])
        even, odd = ([], [])
        for pair in range(TAP_SETS // 2):
            up, down = (18 - 2 * pair, 17 - 2 * pair)
            even.append(
                jnp.where(low_back, grad_s[up : up + own_out, lanes], turned_s[down : down + own_out, :])
            )
            odd.append(
                jnp.where(low_back, turned_s[up : up + own_out, :], grad_s[down : down + own_out, lanes])
            )
        back = []
        for g, pieces in enumerate((even, odd)):
            left = jnp.concatenate(pieces, axis=1).astype(BF16)
            back.append(
                lax.dot_general(left, conv_ref[2 * tile + g], contract, preferred_element_type=F32)
            )
        step = lax.broadcasted_iota(jnp.int32, (own_out, 1), 0)
        for b in range(STRIDE):
            cols = slice(128 * (b // 2), 128 * (b // 2) + 128)
            e, o = (back[0][:, cols], back[1][:, cols])
            both = jnp.where(low_back, e, roll_half(o)) if b % 2 == 0 else jnp.where(low_back, roll_half(e), o)
            both = jnp.where(first_frame + STRIDE * step + b < live, both, 0.0)
            back_s[b * own_out : (b + 1) * own_out, lanes] = both.astype(BF16)

    first = core == 0
    for part, ref in enumerate((mine_ref, other_ref)):
        own_rows = ref[...].astype(F32)[HALO : ext - HALO, :]
        lefts = []
        for c in range(HALF_HEADS):
            att_s[...] = own_rows[:, c * 128 : c * 128 + 128]
            left = jnp.concatenate(
                [att_s[pl.ds(b, own_out, stride=STRIDE), :] for b in range(STRIDE)], axis=0
            )
            lefts.append(jnp.transpose(left))
        left = jnp.concatenate(lefts, axis=0).astype(BF16)
        which = half if part == 0 else 1 - half
        for q in range(4):
            block = jnp.dot(left[96 * q : 96 * q + 96], back_s[...], preferred_element_type=F32)
            one, two = (block[:48], block[48:])
            keep_ref[4 * which + q] = jnp.where(first, one, two)
            rows = pl.ds(pl.multiple_of(48 * (4 * which + q), 48), 48)
            send_ref[rows, :] = jnp.where(first, two, one).astype(BF16)


def critic(meta, lifted, mine, other, proj, conv, score):
    ext, channels = lifted.shape
    own = ext - 2 * HALO
    return pl.pallas_call(
        critic_kernel,
        in_specs=[smem()] + [anywhere()] * 5 + [vmem()],
        out_specs=[vmem(), vmem(), vmem()],
        out_shape=[
            jax.ShapeDtypeStruct((8, 48, channels), F32),
            jax.ShapeDtypeStruct((400, channels), BF16),
            jax.ShapeDtypeStruct((8, channels), F32),
        ],
        scratch_shapes=[
            pltpu.VMEM((channels // 128, 384, 128), F32),
            pltpu.VMEM((96, TAP_SETS * 64), F32),
            pltpu.VMEM((80, channels), F32),
            pltpu.VMEM((88, channels), F32),
            pltpu.VMEM((88, 128), F32),
            pltpu.VMEM((own, channels), BF16),
            pltpu.VMEM((own, 128), F32),
            pltpu.VMEM(proj.shape, BF16),
            pltpu.VMEM(conv.shape, BF16),
            pltpu.VMEM(lifted.shape, F32),
            pltpu.VMEM(mine.shape, BF16),
            pltpu.VMEM(other.shape, BF16),
            pltpu.SemaphoreType.DMA((4,)),
            pltpu.SemaphoreType.DMA((conv.shape[0],)),
        ],
        compiler_params=params(58),
        cost_estimate=pl.CostEstimate(
            flops=3_000_000_000, bytes_accessed=14_000_000, transcendentals=100_000
        ),
    )(meta, lifted, mine, other, proj, conv, score)


def shards(
    states, kv_weight, queries, hidden, out_proj, disc_in, conv_weight, score_weight, frame_len, state_len
):
    frames = hidden.shape[1]
    dp_size, seq_size = (lax.axis_size("dp"), lax.axis_size("seq"))
    clip, seq = (lax.axis_index("dp"), lax.axis_index("seq"))
    core, half, row = (seq % 2, (seq // 2) % 2, seq // 4)
    pick = jnp.arange(frame_len.shape[0]) == clip
    clip_frames = jnp.sum(jnp.where(pick, frame_len, 0))
    clip_states = jnp.sum(jnp.where(pick, state_len, 0))

    def flip(x, bit):
        return lax.ppermute(x, "seq", [(i, i ^ bit) for i in range(seq_size)])

    def turn(x, hops):
        return lax.ppermute(x, "seq", [(i, (i + 4 * hops) % seq_size) for i in range(seq_size)])

    def swap(x, dp_bits, seq_bits):
        pairs = []
        for i in range(dp_size * seq_size):
            d, q = divmod(i, seq_size)
            pairs.append((i, (d ^ dp_bits) * seq_size + (q ^ seq_bits)))
        return lax.ppermute(x, ("dp", "seq"), pairs)

    def at(x, i):
        return lax.dynamic_index_in_dim(x, i, axis=0, keepdims=False)

    att = 2 * HALF_ATT

    proj_own = jnp.dot(out_proj, disc_in, preferred_element_type=F32).astype(BF16)
    kv_weight, proj_own = lax.optimization_barrier((kv_weight, proj_own))
    proj = lax.all_gather(proj_own, "seq", axis=0, tiled=True)

    def head_cols(which):
        parts = [
            lax.dynamic_slice_in_dim(kv_weight, kind * att + which * HALF_ATT, HALF_ATT, axis=1)
            for kind in (0, 1)
        ]
        return jnp.concatenate(parts, axis=1)

    near = head_cols(half)
    far = swap(head_cols(1 - half), 1, 2)
    hops = (1, 3, 2)
    near_turned = [turn(near, j) for j in hops]
    states_in = states[0]
    state_far, state_near = (flip(states_in, 2), flip(states_in, 1))
    near, near_turned, far, state_far, state_near = lax.optimization_barrier(
        (near, near_turned, far, state_far, state_near)
    )

    lower = clip % 2
    channels = disc_in.shape[1]
    near_blocks = [near] + near_turned
    far_blocks = [far] + [turn(far, j) for j in hops]
    far_blocks[1], queries_in, hidden_in = lax.optimization_barrier((far_blocks[1], queries[0], hidden[0]))
    up = [(i, i + 1) for i in range(seq_size - 1)]
    down = [(i + 1, i) for i in range(seq_size - 1)]
    before = jnp.concatenate([queries_in[frames - HALO :], hidden_in[frames - HALO :]], axis=1)
    after = jnp.concatenate([queries_in[:HALO], hidden_in[:HALO]], axis=1)
    before, after = (lax.ppermute(before, "seq", up), lax.ppermute(after, "seq", down))
    state_last = flip(state_far, 1)

    cols = []
    for hop in (0, 1, 3, 2):
        for flip_half in (0, 1):
            where = (((row - hop) % 4) * 2 + (half ^ flip_half)) * 2 + core
            cols.append(where * kv_weight.shape[0])
    total_frames = frames * seq_size
    cols = jnp.stack(cols + [core]).astype(jnp.int32)
    meta = jnp.stack([clip_states, core, half, row]).astype(jnp.int32)
    meta2 = jnp.stack([clip_frames, seq * frames, half, jnp.int32(total_frames), core])
    meta3 = jnp.stack([row, 2 * half + lower, clip // 2]).astype(jnp.int32)
    blocks = [b for pair in zip(near_blocks, far_blocks) for b in pair]
    tables = (cols, meta, meta2.astype(jnp.int32), meta3)
    blocks, state_last, tables, before, after = lax.optimization_barrier(
        (blocks, state_last, tables, before, after)
    )
    cols, meta, meta2, meta3 = tables
    state_parts = [states_in, state_near, state_far, state_last]
    kept, sent = project(cols, state_parts, blocks)
    mine_kv = (kept + flip(sent, 1)).reshape(256, HALF_ATT)

    mine_kv, conv_in, proj = lax.optimization_barrier((mine_kv, conv_weight, proj))
    got = [mine_kv] + [turn(mine_kv, j) for j in (1, 2, 3)]
    got[1], queries_in, hidden_in, before, after = lax.optimization_barrier(
        (got[1], queries[0], hidden[0], before, after)
    )
    rows_in = jnp.concatenate([queries_in, hidden_in], axis=1)
    rows_ext = jnp.concatenate([before, rows_in, after], axis=0)
    query_ext, hidden_ext = (rows_ext[:, :att], rows_ext[:, att:])
    query_mine = lax.dynamic_slice_in_dim(query_ext, half * HALF_ATT, HALF_ATT, axis=1)
    query_far = flip(lax.dynamic_slice_in_dim(query_ext, (1 - half) * HALF_ATT, HALF_ATT, axis=1), 2)
    lifted = jnp.dot(hidden_ext, disc_in, preferred_element_type=F32)
    conv = arrange(conv_in)
    got, conv, query_mine, query_far, lifted = lax.optimization_barrier(
        (got, conv, query_mine, query_far, lifted)
    )
    other = [flip(g, 1) for g in got]

    attended_far = flip(attend(meta, query_far, got, other), 2)
    attended_mine = attend(meta, query_mine, got, other)

    kept, sent, loss = critic(
        meta2, lifted, attended_mine, attended_far, proj, conv, score_weight.reshape(1, -1)
    )

    own_rows = att // seq_size
    share = own_rows // 2
    own, *pieces = core_sum(meta3, kept, flip(sent, 1), loss)
    arrived = [flip(p, 4 * (j + 1)) for j, p in enumerate(pieces)]
    own, *pieces = row_sum(meta3, own, arrived)
    a, b, c = [swap(p, j & 1, j & 2) for j, p in zip((1, 2, 3), pieces)]
    total = (own + a) + (b + c)
    a, b, c = [swap(total, d, 0) for d in (2, 4, 6)]
    total = (total + a) + (b + c)
    total = total + swap(total, 8, 0)
    total_loss = total[share, 0]
    total = total[:share]
    beside = swap(total, 1, 0)
    first = lower == 0
    total = jnp.concatenate([jnp.where(first, total, beside), jnp.where(first, beside, total)], axis=0)
    grad_proj = lift(total, disc_in)
    counted = jnp.sum((frame_len + STRIDE - 1) // STRIDE).astype(F32)
    return (grad_proj, total_loss / counted)


def solution(mesh):
    return jax.shard_map(
        shards,
        mesh=mesh,
        in_specs=(
            P("dp", "seq", None),
            P("seq", None),
            P("dp", "seq", None),
            P("dp", "seq", None),
            P("seq", None),
            P(),
            P(),
            P(),
            P(),
            P(),
        ),
        out_specs=(P("seq", None), P()),
        check_vma=False,
    )
```

```python
import functools
import math

import jax
import jax.numpy as jnp
from jax import lax
from jax.experimental import pallas as pl
from jax.experimental.pallas import tpu as pltpu
from jax.sharding import PartitionSpec as P

HEAD_DIM = 128
HALF_HEADS = 3
HALF_ATT = HEAD_DIM * HALF_HEADS
GROUP_CH = 64
STRIDE = 4
TAPS = 41
TAP_SETS = 12
MARGIN = 20
HALO = 40
REACH = 5
F32 = jnp.float32
BF16 = jnp.bfloat16
MIB = 1024 * 1024


def params(mib):
    return pltpu.CompilerParams(vmem_limit_bytes=mib * MIB)


def smem():
    return pl.BlockSpec(memory_space=pltpu.SMEM)


def vmem():
    return pl.BlockSpec(memory_space=pltpu.VMEM)


def anywhere():
    return pl.BlockSpec(memory_space=pltpu.HBM)


def low_lanes(shape):
    return lax.broadcasted_iota(jnp.int32, shape, 1) % 128 < 64


def roll_half(x):
    return pltpu.roll(x, 64, 1)


def arrange_kernel(w_ref, o_ref):
    low = low_lanes((GROUP_CH, 128))
    zero = jnp.zeros((GROUP_CH, 128), F32)

    def tap(k):
        return w_ref[k].astype(F32) if k < TAPS else zero

    for b in range(STRIDE):
        for pair in range(TAP_SETS // 2):
            first = tap(8 * pair + b)
            second = tap(8 * pair + 4 + b)
            rows, lanes = (slice(b * 64, b * 64 + 64), slice(pair * 128, pair * 128 + 128))
            o_ref[0, rows, lanes] = jnp.where(low, first, roll_half(second)).astype(BF16)
            o_ref[1, rows, lanes] = jnp.where(low, roll_half(first), second).astype(BF16)


def arrange(conv_weight):
    taps, group_in, channels = conv_weight.shape
    groups = channels // GROUP_CH
    return pl.pallas_call(
        arrange_kernel,
        grid=(channels // 128,),
        in_specs=[pl.BlockSpec((taps, group_in, 128), lambda l: (0, 0, l))],
        out_specs=pl.BlockSpec((2, STRIDE * 64, TAP_SETS * 64), lambda l: (l, 0, 0)),
        out_shape=jax.ShapeDtypeStruct((groups, STRIDE * 64, TAP_SETS * 64), BF16),
        compiler_params=params(58),
        cost_estimate=pl.CostEstimate(flops=20_000_000, bytes_accessed=20_000_000, transcendentals=0),
    )(conv_weight)


def project_kernel(cols_ref, *refs):
    states, weights, (keep_ref, send_ref) = (refs[:3], refs[3:11], refs[11:13])
    state_s, weight_s, total_s, state_sem, weight_sem = refs[13:]
    core = cols_ref[8]
    state_copies = [
        pltpu.make_async_copy(s, state_s.at[place], state_sem.at[i])
        for i, (s, place) in enumerate(
            ((states[0], 0), (states[1], 2), (states[2].at[:64], 1), (states[2].at[64:], 3))
        )
    ]
    weight_copies = [
        pltpu.make_async_copy(w, weight_s.at[i], weight_sem.at[i]) for i, w in enumerate(weights)
    ]
    for copy in state_copies + weight_copies:
        copy.start()
    for copy in state_copies:
        copy.wait()
    for i, copy in enumerate(weight_copies):
        copy.wait()
        start = pl.multiple_of(cols_ref[i], 256)
        left = jnp.concatenate([state_s[j, :, pl.ds(start, 256)] for j in range(4)], axis=0)
        part = jnp.dot(left, weight_s[i], preferred_element_type=F32)
        if i == 0:
            total_s[...] = part
        else:
            total_s[...] += part
    kept = pl.ds(pl.multiple_of(core * HALF_ATT, 128), HALF_ATT)
    sent = pl.ds(pl.multiple_of((1 - core) * HALF_ATT, 128), HALF_ATT)
    for j in range(4):
        rows = slice(64 * j, 64 * j + 64)
        block = 2 * (j // 2) + (core + j) % 2
        keep_ref[block] = total_s[rows, kept]
        send_ref[block] = total_s[rows, sent]


def project(cols, states, weights):
    width = 2 * HALF_ATT
    out = jax.ShapeDtypeStruct((4, 64, HALF_ATT), F32)
    return pl.pallas_call(
        project_kernel,
        in_specs=[smem()] + [anywhere()] * 11,
        out_specs=[vmem(), vmem()],
        out_shape=[out, out],
        scratch_shapes=[
            pltpu.VMEM((4,) + states[0].shape, BF16),
            pltpu.VMEM((8,) + weights[0].shape, BF16),
            pltpu.VMEM((256, width), F32),
            pltpu.SemaphoreType.DMA((4,)),
            pltpu.SemaphoreType.DMA((8,)),
        ],
        compiler_params=params(58),
        cost_estimate=pl.CostEstimate(flops=800_000_000, bytes_accessed=6_000_000, transcendentals=0),
    )(cols, *states, *weights)


def split(x):
    high = x.astype(BF16)
    return high, (x - high.astype(F32)).astype(BF16)


def attend_kernel(meta_ref, q_ref, *refs):
    mine, other, o_ref = (refs[:4], refs[4:8], refs[8])
    live, core, half, row = (meta_ref[0], meta_ref[1], meta_ref[2], meta_ref[3])
    first = core == 0
    keys, values = ([], [])
    for m, o in zip(mine, other):
        keys.append(jnp.where(first, m[...], o[...]))
        values.append(jnp.where(first, o[...], m[...]))
    key_high, key_low = split(jnp.concatenate(keys, axis=0))
    value_high, value_low = split(jnp.concatenate(values, axis=0))
    spot = lax.broadcasted_iota(jnp.int32, (1, 1024), 1)
    hop, block, rest = (spot // 256, (spot // 64) % 4, spot % 64)
    where_y = (row - hop + 4) % 4
    where_h = (half + block // 2) % 2
    position = ((where_y * 2 + where_h) * 2 + block % 2) * 64 + rest
    alive = position < live
    contract = (((1,), (1,)), ((), ()))
    rows = 112
    for start in range(0, q_ref.shape[0], rows):
        q = q_ref[start : start + rows, :]
        scores = lax.dot_general(q, key_high, contract, preferred_element_type=F32)
        scores = scores + lax.dot_general(q, key_low, contract, preferred_element_type=F32)
        scores = jnp.where(alive, scores * (1.0 / math.sqrt(HEAD_DIM)), -1e30)
        top = jnp.max(scores, axis=1, keepdims=True)
        expo = jnp.where(alive, jnp.exp(scores - top), 0.0)
        denom = jnp.sum(expo, axis=1, keepdims=True)
        weights = expo.astype(BF16)
        mixed = jnp.dot(weights, value_high, preferred_element_type=F32)
        mixed = mixed + jnp.dot(weights, value_low, preferred_element_type=F32)
        o_ref[start : start + rows, :] = (mixed / denom).astype(BF16)


def attend(meta, query, mine, other):
    rows, width = query.shape
    block = lambda n: pl.BlockSpec((n, HEAD_DIM), lambda h: (0, h))
    return pl.pallas_call(
        attend_kernel,
        grid=(width // HEAD_DIM,),
        in_specs=[smem(), block(rows)] + [block(256)] * 8,
        out_specs=block(rows),
        out_shape=jax.ShapeDtypeStruct((rows, width), BF16),
        compiler_params=params(12),
        cost_estimate=pl.CostEstimate(
            flops=8 * rows * 1024 * width, bytes_accessed=4_000_000, transcendentals=rows * 3072
        ),
    )(meta, query, *mine, *other)


def coded_rows(value):
    high = value.astype(BF16).astype(F32)
    middle = (value - high).astype(BF16).astype(F32)
    low = value - high - middle
    line = lax.broadcasted_iota(jnp.int32, value.shape, 0)
    return jnp.where(line == 0, high, jnp.where(line == 1, middle, low)).astype(BF16)


def decoded_rows(rows):
    rows = rows.astype(F32)
    return (rows[0:1] + rows[1:2]) + rows[2:3]


def core_sum_kernel(meta_ref, kept_ref, arrived_ref, loss_ref, own_ref, *piece_refs):
    row = meta_ref[0]
    loss = loss_ref[:1] + decoded_rows(arrived_ref[384:, :])
    cells = coded_rows(jnp.broadcast_to(loss, (16, loss.shape[1])))
    for j in range(4):
        where = (row + j) % 4 if j == 0 else lax.bitwise_xor(row, j)
        for q in range(2):
            rows = pl.ds(pl.multiple_of(96 * where + 48 * q, 48), 48)
            total = kept_ref[2 * where + q] + arrived_ref[rows, :].astype(F32)
            if j == 0:
                own_ref[48 * q : 48 * q + 48, :] = total
            else:
                piece_refs[j - 1][48 * q : 48 * q + 48, :] = total.astype(BF16)
        if j == 0:
            own_ref[96:, :] = jnp.broadcast_to(loss, (8, loss.shape[1]))
        else:
            piece_refs[j - 1][96:, :] = cells


def core_sum(meta, kept, arrived, loss):
    channels = kept.shape[2]
    return pl.pallas_call(
        core_sum_kernel,
        in_specs=[smem()] + [vmem()] * 3,
        out_specs=[vmem()] * 4,
        out_shape=[jax.ShapeDtypeStruct((104, channels), F32)]
        + [jax.ShapeDtypeStruct((112, channels), BF16)] * 3,
        compiler_params=params(12),
        cost_estimate=pl.CostEstimate(flops=1_000_000, bytes_accessed=4_000_000, transcendentals=0),
    )(meta, kept, arrived, loss)


def row_sum_kernel(meta_ref, own_ref, one_ref, two_ref, three_ref, *out_refs):
    place = meta_ref[1]
    refs = (one_ref, two_ref, three_ref)
    first, second, third = [decoded_rows(r[96:, :]) for r in refs]
    loss = (own_ref[96:97, :] + first) + (second + third)
    for j in range(4):
        start = pl.multiple_of(24 * lax.bitwise_xor(place, j), 8)
        at = 48 * (lax.bitwise_xor(place, j) // 2)
        total = own_ref[pl.ds(start, 24), :]
        upper = lax.bitwise_xor(place, j) % 2 == 1
        for r in refs:
            rows = r[pl.ds(pl.multiple_of(at, 48), 48), :].astype(F32)
            total = total + jnp.where(upper, rows[24:], rows[:24])
        out_refs[j][:24, :] = total
        out_refs[j][24:, :] = jnp.broadcast_to(loss, (8, loss.shape[1]))


def row_sum(meta, own, arrived):
    channels = own.shape[1]
    return pl.pallas_call(
        row_sum_kernel,
        in_specs=[smem()] + [vmem()] * 4,
        out_specs=[vmem()] * 4,
        out_shape=[jax.ShapeDtypeStruct((32, channels), F32)] * 4,
        compiler_params=params(8),
        cost_estimate=pl.CostEstimate(flops=1_000_000, bytes_accessed=2_000_000, transcendentals=0),
    )(meta, own, *arrived)


def lift_kernel(full_ref, disc_ref, out_ref):
    rows = full_ref.shape[0]
    both = jnp.concatenate(split(full_ref[...]), axis=0)
    wide = disc_ref.shape[0] // 3
    for i in range(3):
        cols = slice(wide * i, wide * i + wide)
        product = lax.dot_general(
            both, disc_ref[cols, :], (((1,), (1,)), ((), ())), preferred_element_type=F32
        )
        out_ref[:, cols] = product[:rows] + product[rows:]


def lift(full, disc_in):
    return pl.pallas_call(
        lift_kernel,
        in_specs=[vmem()] * 2,
        out_specs=vmem(),
        out_shape=jax.ShapeDtypeStruct((full.shape[0], disc_in.shape[0]), F32),
        compiler_params=params(12),
        cost_estimate=pl.CostEstimate(flops=300_000_000, bytes_accessed=3_500_000, transcendentals=0),
    )(full, disc_in)


def critic_kernel(
    meta_ref, lifted_hbm, mine_hbm, other_hbm, proj_hbm, conv_hbm, score_ref,
    keep_ref, send_ref, loss_ref,
    feed_s, y_s, pre_s, grad_s, turned_s, back_s, att_s, proj_s, conv_ref, lifted_ref, mine_ref, other_ref, proj_sem, conv_sem,
):
    live, first_frame, half = (meta_ref[0], meta_ref[1], meta_ref[2])
    total_frames, core = (meta_ref[3], meta_ref[4])
    pairs = [(lifted_hbm, lifted_ref), (mine_hbm, mine_ref), (other_hbm, other_ref), (proj_hbm, proj_s)]
    proj_copies = [pltpu.make_async_copy(a, b, proj_sem.at[i]) for i, (a, b) in enumerate(pairs)]
    conv_copies = [
        pltpu.make_async_copy(conv_hbm.at[g], conv_ref.at[g], conv_sem.at[g])
        for g in range(conv_ref.shape[0])
    ]
    for copy in proj_copies + conv_copies:
        copy.start()
    ext = lifted_ref.shape[0]
    own_out = (ext - 2 * HALO) // STRIDE
    tiles = lifted_ref.shape[1] // 128
    for copy in proj_copies:
        copy.wait()
    feed = lifted_ref[...]
    for ref, which in ((mine_ref, half), (other_ref, 1 - half)):
        proj = proj_s[pl.ds(pl.multiple_of(HALF_ATT * which, HALF_ATT), HALF_ATT), :]
        feed = feed + jnp.dot(ref[...], proj, preferred_element_type=F32)
    frame = first_frame - HALO + lax.broadcasted_iota(jnp.int32, (ext, 1), 0)
    inside = (frame >= 0) & (frame < live)
    feed = jnp.where(inside, feed, 0.0).astype(BF16).astype(F32)
    for i in range(tiles):
        feed_s[i, :ext, :] = feed[:, 128 * i : 128 * i + 128]
        feed_s[i, ext:, :] = jnp.zeros((feed_s.shape[1] - ext, 128), F32)
    rows = y_s.shape[0]
    low = low_lanes((rows, 128))
    low_out = low_lanes((80, 128))
    for copy in conv_copies:
        copy.wait()

    @pl.loop(0, tiles)
    def _(tile):
        lanes = pl.ds(pl.multiple_of(tile * 128, 128), 128)
        phase = [feed_s[tile, pl.ds(b, rows, stride=STRIDE), :] for b in range(STRIDE)]
        turned = [roll_half(p) for p in phase]
        even = [jnp.where(low, phase[b], turned[b + 1]) for b in (0, 2)]
        odd = [jnp.where(low, turned[b], phase[b + 1]) for b in (0, 2)]
        sums = []
        for g, pieces in enumerate((even, odd)):
            left = jnp.concatenate(pieces, axis=1).astype(BF16)
            y_s[...] = jnp.dot(left, conv_ref[2 * tile + g], preferred_element_type=F32)
            at, after = (None, None)
            for pair in range(TAP_SETS // 2):
                cols = slice(128 * pair, 128 * pair + 128)
                a = y_s[2 * pair : 2 * pair + 80, cols]
                b = y_s[2 * pair + 1 : 2 * pair + 81, cols]
                at = a if at is None else at + a
                after = b if after is None else after + b
            sums.append((at, after))
        pre_even = sums[0][0] + roll_half(sums[0][1])
        pre_odd = roll_half(sums[1][0]) + sums[1][1]
        pre_s[:, lanes] = jnp.where(low_out, pre_even, pre_odd)

    pre = pre_s[...]
    sig = 1.0 / (1.0 + jnp.exp(-pre))
    score = score_ref[...]
    critic = jnp.sum(pre * sig * score, axis=1, keepdims=True)
    slot = lax.broadcasted_iota(jnp.int32, (80, 1), 0)
    frame_out = first_frame - STRIDE * REACH + STRIDE * slot
    valid = (frame_out >= 0) & (frame_out < total_frames) & (frame_out < live) & (slot < own_out + 2 * REACH)
    shortfall = 1.0 - critic
    own = valid & (slot >= REACH) & (slot < REACH + own_out)
    loss = jnp.sum(jnp.where(own, shortfall * shortfall, 0.0), axis=0, keepdims=True)
    loss_ref[...] = jnp.broadcast_to(loss, loss_ref.shape)
    send_ref[384:, :] = coded_rows(jnp.broadcast_to(loss, (16, send_ref.shape[1])))
    push = jnp.where(valid, -2.0 * shortfall, 0.0)
    grad = push * score * (sig * (1.0 + pre * (1.0 - sig)))
    grad = jnp.where(valid, grad, 0.0).astype(BF16).astype(F32)
    grad_s[:8, :] = jnp.zeros((8, grad_s.shape[1]), F32)
    grad_s[8:, :] = grad

    contract = (((1,), (1,)), ((), ()))
    low_back = low_lanes((own_out, 128))

    @pl.loop(0, tiles)
    def _(tile):
        lanes = pl.ds(pl.multiple_of(tile * 128, 128), 128)
        turned_s[...] = roll_half(grad_s[:, lanes])
        even, odd = ([], [])
        for pair in range(TAP_SETS // 2):
            up, down = (18 - 2 * pair, 17 - 2 * pair)
            even.append(
                jnp.where(low_back, grad_s[up : up + own_out, lanes], turned_s[down : down + own_out, :])
            )
            odd.append(
                jnp.where(low_back, turned_s[up : up + own_out, :], grad_s[down : down + own_out, lanes])
            )
        back = []
        for g, pieces in enumerate((even, odd)):
            left = jnp.concatenate(pieces, axis=1).astype(BF16)
            back.append(
                lax.dot_general(left, conv_ref[2 * tile + g], contract, preferred_element_type=F32)
            )
        step = lax.broadcasted_iota(jnp.int32, (own_out, 1), 0)
        for b in range(STRIDE):
            cols = slice(128 * (b // 2), 128 * (b // 2) + 128)
            e, o = (back[0][:, cols], back[1][:, cols])
            both = jnp.where(low_back, e, roll_half(o)) if b % 2 == 0 else jnp.where(low_back, roll_half(e), o)
            both = jnp.where(first_frame + STRIDE * step + b < live, both, 0.0)
            back_s[b * own_out : (b + 1) * own_out, lanes] = both.astype(BF16)

    first = core == 0
    for part, ref in enumerate((mine_ref, other_ref)):
        own_rows = ref[...].astype(F32)[HALO : ext - HALO, :]
        lefts = []
        for c in range(HALF_HEADS):
            att_s[...] = own_rows[:, c * 128 : c * 128 + 128]
            left = jnp.concatenate(
                [att_s[pl.ds(b, own_out, stride=STRIDE), :] for b in range(STRIDE)], axis=0
            )
            lefts.append(jnp.transpose(left))
        left = jnp.concatenate(lefts, axis=0).astype(BF16)
        which = half if part == 0 else 1 - half
        for q in range(4):
            block = jnp.dot(left[96 * q : 96 * q + 96], back_s[...], preferred_element_type=F32)
            one, two = (block[:48], block[48:])
            keep_ref[4 * which + q] = jnp.where(first, one, two)
            rows = pl.ds(pl.multiple_of(48 * (4 * which + q), 48), 48)
            send_ref[rows, :] = jnp.where(first, two, one).astype(BF16)


def critic(meta, lifted, mine, other, proj, conv, score):
    ext, channels = lifted.shape
    own = ext - 2 * HALO
    return pl.pallas_call(
        critic_kernel,
        in_specs=[smem()] + [anywhere()] * 5 + [vmem()],
        out_specs=[vmem(), vmem(), vmem()],
        out_shape=[
            jax.ShapeDtypeStruct((8, 48, channels), F32),
            jax.ShapeDtypeStruct((400, channels), BF16),
            jax.ShapeDtypeStruct((8, channels), F32),
        ],
        scratch_shapes=[
            pltpu.VMEM((channels // 128, 384, 128), F32),
            pltpu.VMEM((96, TAP_SETS * 64), F32),
            pltpu.VMEM((80, channels), F32),
            pltpu.VMEM((88, channels), F32),
            pltpu.VMEM((88, 128), F32),
            pltpu.VMEM((own, channels), BF16),
            pltpu.VMEM((own, 128), F32),
            pltpu.VMEM(proj.shape, BF16),
            pltpu.VMEM(conv.shape, BF16),
            pltpu.VMEM(lifted.shape, F32),
            pltpu.VMEM(mine.shape, BF16),
            pltpu.VMEM(other.shape, BF16),
            pltpu.SemaphoreType.DMA((4,)),
            pltpu.SemaphoreType.DMA((conv.shape[0],)),
        ],
        compiler_params=params(58),
        cost_estimate=pl.CostEstimate(
            flops=3_000_000_000, bytes_accessed=14_000_000, transcendentals=100_000
        ),
    )(meta, lifted, mine, other, proj, conv, score)


def shards(
    states, kv_weight, queries, hidden, out_proj, disc_in, conv_weight, score_weight, frame_len, state_len
):
    frames = hidden.shape[1]
    dp_size, seq_size = (lax.axis_size("dp"), lax.axis_size("seq"))
    clip, seq = (lax.axis_index("dp"), lax.axis_index("seq"))
    core, half, row = (seq % 2, (seq // 2) % 2, seq // 4)
    pick = jnp.arange(frame_len.shape[0]) == clip
    clip_frames = jnp.sum(jnp.where(pick, frame_len, 0))
    clip_states = jnp.sum(jnp.where(pick, state_len, 0))

    def flip(x, bit):
        return lax.ppermute(x, "seq", [(i, i ^ bit) for i in range(seq_size)])

    def turn(x, hops):
        return lax.ppermute(x, "seq", [(i, (i + 4 * hops) % seq_size) for i in range(seq_size)])

    def swap(x, dp_bits, seq_bits):
        pairs = []
        for i in range(dp_size * seq_size):
            d, q = divmod(i, seq_size)
            pairs.append((i, (d ^ dp_bits) * seq_size + (q ^ seq_bits)))
        return lax.ppermute(x, ("dp", "seq"), pairs)

    def at(x, i):
        return lax.dynamic_index_in_dim(x, i, axis=0, keepdims=False)

    att = 2 * HALF_ATT

    proj_own = jnp.dot(out_proj, disc_in, preferred_element_type=F32).astype(BF16)
    kv_weight, proj_own = lax.optimization_barrier((kv_weight, proj_own))
    proj = lax.all_gather(proj_own, "seq", axis=0, tiled=True)

    def head_cols(which, kv_weight):
        parts = [
            lax.dynamic_slice_in_dim(kv_weight, kind * att + which * HALF_ATT, HALF_ATT, axis=1)
            for kind in (0, 1)
        ]
        return jnp.concatenate(parts, axis=1)

    far = head_cols(1 - half, kv_weight)
    far, kv_weight = lax.optimization_barrier((far, kv_weight))
    near = head_cols(half, kv_weight)
    far = swap(far, 1, 2)
    hops = (1, 3, 2)
    near_turned = [turn(near, j) for j in hops]
    states_in = states[0]
    near, near_turned, far, state_far, queries_in, hidden_in = lax.optimization_barrier(
        (near, near_turned, far, flip(states_in, 2), queries[0], hidden[0])
    )

    lower = clip % 2
    channels = disc_in.shape[1]
    near_blocks = [near] + near_turned
    far_blocks = [far] + [turn(far, j) for j in hops]
    state_pair = flip(jnp.concatenate([states_in, state_far], axis=0), 1)
    up = [(i, i + 1) for i in range(seq_size - 1)]
    down = [(i + 1, i) for i in range(seq_size - 1)]
    before = jnp.concatenate([queries_in[frames - HALO :], hidden_in[frames - HALO :]], axis=1)
    before = lax.ppermute(before, "seq", up)
    after = jnp.concatenate([queries_in[:HALO], hidden_in[:HALO]], axis=1)

    cols = []
    for hop in (0, 1, 3, 2):
        for flip_half in (0, 1):
            where = (((row - hop) % 4) * 2 + (half ^ flip_half)) * 2 + core
            cols.append(where * kv_weight.shape[0])
    total_frames = frames * seq_size
    cols = jnp.stack(cols + [core]).astype(jnp.int32)
    meta = jnp.stack([clip_states, core, half, row]).astype(jnp.int32)
    meta2 = jnp.stack([clip_frames, seq * frames, half, jnp.int32(total_frames), core])
    meta3 = jnp.stack([row, 2 * half + lower, clip // 2]).astype(jnp.int32)
    blocks = [b for pair in zip(near_blocks, far_blocks) for b in pair]
    tables = (cols, meta, meta2.astype(jnp.int32), meta3)
    blocks, state_pair, tables, before, after = lax.optimization_barrier(
        (blocks, state_pair, tables, before, after)
    )
    cols, meta, meta2, meta3 = tables
    state_parts = [states_in, state_far, state_pair]
    kept, sent = project(cols, state_parts, blocks)
    mine_kv = (kept + flip(sent, 1)).reshape(256, HALF_ATT)

    mine_kv, conv_in, proj, queries_in, hidden_in, before, after = lax.optimization_barrier(
        (mine_kv, conv_weight, proj, queries[0], hidden[0], before, after)
    )
    got = [mine_kv] + [turn(mine_kv, j) for j in (1, 2, 3)]
    rows_in = jnp.concatenate([queries_in, hidden_in], axis=1)
    rows_ext = jnp.concatenate([before, rows_in, lax.ppermute(after, "seq", down)], axis=0)
    query_ext, hidden_ext = (rows_ext[:, :att], rows_ext[:, att:])
    query_mine = lax.dynamic_slice_in_dim(query_ext, half * HALF_ATT, HALF_ATT, axis=1)
    query_far = flip(lax.dynamic_slice_in_dim(query_ext, (1 - half) * HALF_ATT, HALF_ATT, axis=1), 2)
    lifted = jnp.dot(hidden_ext, disc_in, preferred_element_type=F32)
    conv = arrange(conv_in)
    got, conv, query_mine, query_far, lifted = lax.optimization_barrier(
        (got, conv, query_mine, query_far, lifted)
    )
    other = [flip(g, 1) for g in got]

    attended_far = flip(attend(meta, query_far, got, other), 2)
    attended_mine = attend(meta, query_mine, got, other)

    kept, sent, loss = critic(
        meta2, lifted, attended_mine, attended_far, proj, conv, score_weight.reshape(1, -1)
    )

    own_rows = att // seq_size
    share = own_rows // 2
    own, *pieces = core_sum(meta3, kept, flip(sent, 1), loss)
    arrived = [flip(p, 4 * (j + 1)) for j, p in enumerate(pieces)]
    own, *pieces = row_sum(meta3, own, arrived)
    a, b, c = [swap(p, j & 1, j & 2) for j, p in zip((1, 2, 3), pieces)]
    total = (own + a) + (b + c)
    a, b, c = [swap(total, d, 0) for d in (2, 4, 6)]
    total = (total + a) + (b + c)
    total = total + swap(total, 8, 0)
    total_loss = total[share, 0]
    total = total[:share]
    beside = swap(total, 1, 0)
    first = lower == 0
    total = jnp.concatenate([jnp.where(first, total, beside), jnp.where(first, beside, total)], axis=0)
    grad_proj = lift(total, disc_in)
    counted = jnp.sum((frame_len + STRIDE - 1) // STRIDE).astype(F32)
    return (grad_proj, total_loss / counted)


def solution(mesh):
    return jax.shard_map(
        shards,
        mesh=mesh,
        in_specs=(
            P("dp", "seq", None),
            P("seq", None),
            P("dp", "seq", None),
            P("dp", "seq", None),
            P("seq", None),
            P(),
            P(),
            P(),
            P(),
            P(),
        ),
        out_specs=(P("seq", None), P()),
        check_vma=False,
    )
```

```python
import functools
import math

import jax
import jax.numpy as jnp
from jax import lax
from jax.experimental import pallas as pl
from jax.experimental.pallas import tpu as pltpu
from jax.sharding import PartitionSpec as P

HEAD_DIM = 128
HALF_HEADS = 3
HALF_ATT = HEAD_DIM * HALF_HEADS
GROUP_CH = 64
STRIDE = 4
TAPS = 41
TAP_SETS = 12
MARGIN = 20
HALO = 40
REACH = 5
F32 = jnp.float32
BF16 = jnp.bfloat16
MIB = 1024 * 1024


def params(mib):
    return pltpu.CompilerParams(vmem_limit_bytes=mib * MIB)


def smem():
    return pl.BlockSpec(memory_space=pltpu.SMEM)


def vmem():
    return pl.BlockSpec(memory_space=pltpu.VMEM)


def anywhere():
    return pl.BlockSpec(memory_space=pltpu.HBM)


def low_lanes(shape):
    return lax.broadcasted_iota(jnp.int32, shape, 1) % 128 < 64


def roll_half(x):
    return pltpu.roll(x, 64, 1)


def arrange_kernel(w_ref, o_ref):
    low = low_lanes((GROUP_CH, 128))
    zero = jnp.zeros((GROUP_CH, 128), F32)

    def tap(k):
        return w_ref[k].astype(F32) if k < TAPS else zero

    for b in range(STRIDE):
        for pair in range(TAP_SETS // 2):
            first = tap(8 * pair + b)
            second = tap(8 * pair + 4 + b)
            rows, lanes = (slice(b * 64, b * 64 + 64), slice(pair * 128, pair * 128 + 128))
            o_ref[0, rows, lanes] = jnp.where(low, first, roll_half(second)).astype(BF16)
            o_ref[1, rows, lanes] = jnp.where(low, roll_half(first), second).astype(BF16)


def arrange(conv_weight):
    taps, group_in, channels = conv_weight.shape
    groups = channels // GROUP_CH
    return pl.pallas_call(
        arrange_kernel,
        grid=(channels // 128,),
        in_specs=[pl.BlockSpec((taps, group_in, 128), lambda l: (0, 0, l))],
        out_specs=pl.BlockSpec((2, STRIDE * 64, TAP_SETS * 64), lambda l: (l, 0, 0)),
        out_shape=jax.ShapeDtypeStruct((groups, STRIDE * 64, TAP_SETS * 64), BF16),
        compiler_params=params(58),
        cost_estimate=pl.CostEstimate(flops=20_000_000, bytes_accessed=20_000_000, transcendentals=0),
    )(conv_weight)


def project_kernel(cols_ref, *refs):
    states, weights, (keep_ref, send_ref) = (refs[:3], refs[3:11], refs[11:13])
    state_s, weight_s, total_s, state_sem, weight_sem = refs[13:]
    core = cols_ref[8]
    state_copies = [
        pltpu.make_async_copy(s, state_s.at[place], state_sem.at[i])
        for i, (s, place) in enumerate(
            ((states[0], 0), (states[1], 2), (states[2].at[:64], 1), (states[2].at[64:], 3))
        )
    ]
    weight_copies = [
        pltpu.make_async_copy(w, weight_s.at[i], weight_sem.at[i]) for i, w in enumerate(weights)
    ]
    for copy in state_copies + weight_copies:
        copy.start()
    for copy in state_copies:
        copy.wait()
    for i, copy in enumerate(weight_copies):
        copy.wait()
        start = pl.multiple_of(cols_ref[i], 256)
        left = jnp.concatenate([state_s[j, :, pl.ds(start, 256)] for j in range(4)], axis=0)
        part = jnp.dot(left, weight_s[i], preferred_element_type=F32)
        if i == 0:
            total_s[...] = part
        else:
            total_s[...] += part
    kept = pl.ds(pl.multiple_of(core * HALF_ATT, 128), HALF_ATT)
    sent = pl.ds(pl.multiple_of((1 - core) * HALF_ATT, 128), HALF_ATT)
    for j in range(4):
        rows = slice(64 * j, 64 * j + 64)
        block = 2 * (j // 2) + (core + j) % 2
        keep_ref[block] = total_s[rows, kept]
        send_ref[block] = total_s[rows, sent]


def project(cols, states, weights):
    width = 2 * HALF_ATT
    out = jax.ShapeDtypeStruct((4, 64, HALF_ATT), F32)
    return pl.pallas_call(
        project_kernel,
        in_specs=[smem()] + [anywhere()] * 11,
        out_specs=[vmem(), vmem()],
        out_shape=[out, out],
        scratch_shapes=[
            pltpu.VMEM((4,) + states[0].shape, BF16),
            pltpu.VMEM((8,) + weights[0].shape, BF16),
            pltpu.VMEM((256, width), F32),
            pltpu.SemaphoreType.DMA((4,)),
            pltpu.SemaphoreType.DMA((8,)),
        ],
        compiler_params=params(58),
        cost_estimate=pl.CostEstimate(flops=800_000_000, bytes_accessed=6_000_000, transcendentals=0),
    )(cols, *states, *weights)


def split(x):
    high = x.astype(BF16)
    return high, (x - high.astype(F32)).astype(BF16)


def attend_kernel(meta_ref, q_ref, *refs):
    mine, other, o_ref = (refs[:4], refs[4:8], refs[8])
    live, core, half, row = (meta_ref[0], meta_ref[1], meta_ref[2], meta_ref[3])
    first = core == 0
    keys, values = ([], [])
    for m, o in zip(mine, other):
        keys.append(jnp.where(first, m[...], o[...]))
        values.append(jnp.where(first, o[...], m[...]))
    key_high, key_low = split(jnp.concatenate(keys, axis=0) * (1.0 / math.sqrt(HEAD_DIM)))
    value_high, value_low = split(jnp.concatenate(values, axis=0))
    spot = lax.broadcasted_iota(jnp.int32, (1, 1024), 1)
    hop, block, rest = (spot // 256, (spot // 64) % 4, spot % 64)
    where_y = (row - hop + 4) % 4
    where_h = (half + block // 2) % 2
    position = ((where_y * 2 + where_h) * 2 + block % 2) * 64 + rest
    alive = position < live
    contract = (((1,), (1,)), ((), ()))
    rows = 112
    for start in range(0, q_ref.shape[0], rows):
        q = q_ref[start : start + rows, :]
        scores = lax.dot_general(q, key_high, contract, preferred_element_type=F32)
        scores = scores + lax.dot_general(q, key_low, contract, preferred_element_type=F32)
        scores = jnp.where(alive, scores, -1e30)
        top = jnp.max(scores, axis=1, keepdims=True)
        expo = jnp.exp(scores - top)
        denom = jnp.sum(expo, axis=1, keepdims=True)
        weights = expo.astype(BF16)
        mixed = jnp.dot(weights, value_high, preferred_element_type=F32)
        mixed = mixed + jnp.dot(weights, value_low, preferred_element_type=F32)
        o_ref[start : start + rows, :] = (mixed / denom).astype(BF16)


def attend(meta, query, mine, other):
    rows, width = query.shape
    block = lambda n: pl.BlockSpec((n, HEAD_DIM), lambda h: (0, h))
    return pl.pallas_call(
        attend_kernel,
        grid=(width // HEAD_DIM,),
        in_specs=[smem(), block(rows)] + [block(256)] * 8,
        out_specs=block(rows),
        out_shape=jax.ShapeDtypeStruct((rows, width), BF16),
        compiler_params=params(12),
        cost_estimate=pl.CostEstimate(
            flops=8 * rows * 1024 * width, bytes_accessed=4_000_000, transcendentals=rows * 3072
        ),
    )(meta, query, *mine, *other)


def coded_rows(value):
    high = value.astype(BF16).astype(F32)
    middle = (value - high).astype(BF16).astype(F32)
    low = value - high - middle
    line = lax.broadcasted_iota(jnp.int32, value.shape, 0)
    return jnp.where(line == 0, high, jnp.where(line == 1, middle, low)).astype(BF16)


def decoded_rows(rows):
    rows = rows.astype(F32)
    return (rows[0:1] + rows[1:2]) + rows[2:3]


def core_sum_kernel(meta_ref, kept_ref, arrived_ref, loss_ref, own_ref, *piece_refs):
    row = meta_ref[0]
    loss = loss_ref[:1] + decoded_rows(arrived_ref[384:, :])
    cells = coded_rows(jnp.broadcast_to(loss, (16, loss.shape[1])))
    for j in range(4):
        where = (row + j) % 4 if j == 0 else lax.bitwise_xor(row, j)
        for q in range(2):
            rows = pl.ds(pl.multiple_of(96 * where + 48 * q, 48), 48)
            total = kept_ref[2 * where + q] + arrived_ref[rows, :].astype(F32)
            if j == 0:
                own_ref[48 * q : 48 * q + 48, :] = total
            else:
                piece_refs[j - 1][48 * q : 48 * q + 48, :] = total.astype(BF16)
        if j == 0:
            own_ref[96:, :] = jnp.broadcast_to(loss, (8, loss.shape[1]))
        else:
            piece_refs[j - 1][96:, :] = cells


def core_sum(meta, kept, arrived, loss):
    channels = kept.shape[2]
    return pl.pallas_call(
        core_sum_kernel,
        in_specs=[smem()] + [vmem()] * 3,
        out_specs=[vmem()] * 4,
        out_shape=[jax.ShapeDtypeStruct((104, channels), F32)]
        + [jax.ShapeDtypeStruct((112, channels), BF16)] * 3,
        compiler_params=params(12),
        cost_estimate=pl.CostEstimate(flops=1_000_000, bytes_accessed=4_000_000, transcendentals=0),
    )(meta, kept, arrived, loss)


def row_sum_kernel(meta_ref, own_ref, one_ref, two_ref, three_ref, *out_refs):
    place = meta_ref[1]
    refs = (one_ref, two_ref, three_ref)
    first, second, third = [decoded_rows(r[96:, :]) for r in refs]
    loss = (own_ref[96:97, :] + first) + (second + third)
    for j in range(4):
        start = pl.multiple_of(24 * lax.bitwise_xor(place, j), 8)
        at = 48 * (lax.bitwise_xor(place, j) // 2)
        total = own_ref[pl.ds(start, 24), :]
        upper = lax.bitwise_xor(place, j) % 2 == 1
        for r in refs:
            rows = r[pl.ds(pl.multiple_of(at, 48), 48), :].astype(F32)
            total = total + jnp.where(upper, rows[24:], rows[:24])
        out_refs[j][:24, :] = total
        out_refs[j][24:, :] = jnp.broadcast_to(loss, (8, loss.shape[1]))


def row_sum(meta, own, arrived):
    channels = own.shape[1]
    return pl.pallas_call(
        row_sum_kernel,
        in_specs=[smem()] + [vmem()] * 4,
        out_specs=[vmem()] * 4,
        out_shape=[jax.ShapeDtypeStruct((32, channels), F32)] * 4,
        compiler_params=params(8),
        cost_estimate=pl.CostEstimate(flops=1_000_000, bytes_accessed=2_000_000, transcendentals=0),
    )(meta, own, *arrived)


def lift_kernel(full_ref, disc_ref, out_ref):
    rows = full_ref.shape[0]
    both = jnp.concatenate(split(full_ref[...]), axis=0)
    wide = disc_ref.shape[0] // 3
    for i in range(3):
        cols = slice(wide * i, wide * i + wide)
        product = lax.dot_general(
            both, disc_ref[cols, :], (((1,), (1,)), ((), ())), preferred_element_type=F32
        )
        out_ref[:, cols] = product[:rows] + product[rows:]


def lift(full, disc_in):
    return pl.pallas_call(
        lift_kernel,
        in_specs=[vmem()] * 2,
        out_specs=vmem(),
        out_shape=jax.ShapeDtypeStruct((full.shape[0], disc_in.shape[0]), F32),
        compiler_params=params(12),
        cost_estimate=pl.CostEstimate(flops=300_000_000, bytes_accessed=3_500_000, transcendentals=0),
    )(full, disc_in)


def critic_kernel(
    meta_ref, lifted_hbm, mine_hbm, other_hbm, proj_hbm, conv_hbm, score_ref,
    keep_ref, send_ref, loss_ref,
    feed_s, y_s, pre_s, grad_s, turned_s, back_s, att_s, proj_s, conv_ref, lifted_ref, mine_ref, other_ref, proj_sem, conv_sem,
):
    live, first_frame, half = (meta_ref[0], meta_ref[1], meta_ref[2])
    total_frames, core = (meta_ref[3], meta_ref[4])
    pairs = [(lifted_hbm, lifted_ref), (mine_hbm, mine_ref), (other_hbm, other_ref), (proj_hbm, proj_s)]
    proj_copies = [pltpu.make_async_copy(a, b, proj_sem.at[i]) for i, (a, b) in enumerate(pairs)]
    conv_copies = [
        pltpu.make_async_copy(conv_hbm.at[g], conv_ref.at[g], conv_sem.at[g])
        for g in range(conv_ref.shape[0])
    ]
    for copy in proj_copies + conv_copies:
        copy.start()
    ext = lifted_ref.shape[0]
    own_out = (ext - 2 * HALO) // STRIDE
    tiles = lifted_ref.shape[1] // 128
    for copy in proj_copies:
        copy.wait()
    feed = lifted_ref[...]
    for ref, which in ((mine_ref, half), (other_ref, 1 - half)):
        proj = proj_s[pl.ds(pl.multiple_of(HALF_ATT * which, HALF_ATT), HALF_ATT), :]
        feed = feed + jnp.dot(ref[...], proj, preferred_element_type=F32)
    frame = first_frame - HALO + lax.broadcasted_iota(jnp.int32, (ext, 1), 0)
    inside = (frame >= 0) & (frame < live)
    feed = jnp.where(inside, feed, 0.0).astype(BF16).astype(F32)
    for i in range(tiles):
        feed_s[i, :ext, :] = feed[:, 128 * i : 128 * i + 128]
        feed_s[i, ext:, :] = jnp.zeros((feed_s.shape[1] - ext, 128), F32)
    rows = y_s.shape[0]
    low = low_lanes((rows, 128))
    low_out = low_lanes((80, 128))
    for copy in conv_copies:
        copy.wait()

    @pl.loop(0, tiles, unroll=2)
    def _(tile):
        lanes = pl.ds(pl.multiple_of(tile * 128, 128), 128)
        phase = [feed_s[tile, pl.ds(b, rows, stride=STRIDE), :] for b in range(STRIDE)]
        turned = [roll_half(p) for p in phase]
        even = [jnp.where(low, phase[b], turned[b + 1]) for b in (0, 2)]
        odd = [jnp.where(low, turned[b], phase[b + 1]) for b in (0, 2)]
        sums = []
        for g, pieces in enumerate((even, odd)):
            left = jnp.concatenate(pieces, axis=1).astype(BF16)
            y_s[...] = jnp.dot(left, conv_ref[2 * tile + g], preferred_element_type=F32)
            at, after = (None, None)
            for pair in range(TAP_SETS // 2):
                cols = slice(128 * pair, 128 * pair + 128)
                a = y_s[2 * pair : 2 * pair + 80, cols]
                b = y_s[2 * pair + 1 : 2 * pair + 81, cols]
                at = a if at is None else at + a
                after = b if after is None else after + b
            sums.append((at, after))
        pre_even = sums[0][0] + roll_half(sums[0][1])
        pre_odd = roll_half(sums[1][0]) + sums[1][1]
        pre_s[:, lanes] = jnp.where(low_out, pre_even, pre_odd)

    pre = pre_s[...]
    sig = 1.0 / (1.0 + jnp.exp(-pre))
    score = score_ref[...]
    critic = jnp.sum(pre * sig * score, axis=1, keepdims=True)
    slot = lax.broadcasted_iota(jnp.int32, (80, 1), 0)
    frame_out = first_frame - STRIDE * REACH + STRIDE * slot
    valid = (frame_out >= 0) & (frame_out < total_frames) & (frame_out < live) & (slot < own_out + 2 * REACH)
    shortfall = 1.0 - critic
    own = valid & (slot >= REACH) & (slot < REACH + own_out)
    loss = jnp.sum(jnp.where(own, shortfall * shortfall, 0.0), axis=0, keepdims=True)
    loss_ref[...] = jnp.broadcast_to(loss, loss_ref.shape)
    send_ref[384:, :] = coded_rows(jnp.broadcast_to(loss, (16, send_ref.shape[1])))
    push = jnp.where(valid, -2.0 * shortfall, 0.0)
    grad = push * score * (sig * (1.0 + pre * (1.0 - sig)))
    grad = jnp.where(valid, grad, 0.0).astype(BF16).astype(F32)
    grad_s[:8, :] = jnp.zeros((8, grad_s.shape[1]), F32)
    grad_s[8:, :] = grad

    contract = (((1,), (1,)), ((), ()))
    low_back = low_lanes((own_out, 128))

    @pl.loop(0, tiles, unroll=2)
    def _(tile):
        lanes = pl.ds(pl.multiple_of(tile * 128, 128), 128)
        turned_s[...] = roll_half(grad_s[:, lanes])
        even, odd = ([], [])
        for pair in range(TAP_SETS // 2):
            up, down = (18 - 2 * pair, 17 - 2 * pair)
            even.append(
                jnp.where(low_back, grad_s[up : up + own_out, lanes], turned_s[down : down + own_out, :])
            )
            odd.append(
                jnp.where(low_back, turned_s[up : up + own_out, :], grad_s[down : down + own_out, lanes])
            )
        back = []
        for g, pieces in enumerate((even, odd)):
            left = jnp.concatenate(pieces, axis=1).astype(BF16)
            back.append(
                lax.dot_general(left, conv_ref[2 * tile + g], contract, preferred_element_type=F32)
            )
        step = lax.broadcasted_iota(jnp.int32, (own_out, 1), 0)
        for b in range(STRIDE):
            cols = slice(128 * (b // 2), 128 * (b // 2) + 128)
            e, o = (back[0][:, cols], back[1][:, cols])
            both = jnp.where(low_back, e, roll_half(o)) if b % 2 == 0 else jnp.where(low_back, roll_half(e), o)
            both = jnp.where(first_frame + STRIDE * step + b < live, both, 0.0)
            back_s[b * own_out : (b + 1) * own_out, lanes] = both.astype(BF16)

    first = core == 0
    for part, ref in enumerate((mine_ref, other_ref)):
        own_rows = ref[...].astype(F32)[HALO : ext - HALO, :]
        lefts = []
        for c in range(HALF_HEADS):
            att_s[...] = own_rows[:, c * 128 : c * 128 + 128]
            left = jnp.concatenate(
                [att_s[pl.ds(b, own_out, stride=STRIDE), :] for b in range(STRIDE)], axis=0
            )
            lefts.append(jnp.transpose(left))
        left = jnp.concatenate(lefts, axis=0).astype(BF16)
        which = half if part == 0 else 1 - half
        for q in range(4):
            block = jnp.dot(left[96 * q : 96 * q + 96], back_s[...], preferred_element_type=F32)
            one, two = (block[:48], block[48:])
            keep_ref[4 * which + q] = jnp.where(first, one, two)
            rows = pl.ds(pl.multiple_of(48 * (4 * which + q), 48), 48)
            send_ref[rows, :] = jnp.where(first, two, one).astype(BF16)


def critic(meta, lifted, mine, other, proj, conv, score):
    ext, channels = lifted.shape
    own = ext - 2 * HALO
    return pl.pallas_call(
        critic_kernel,
        in_specs=[smem()] + [anywhere()] * 5 + [vmem()],
        out_specs=[vmem(), vmem(), vmem()],
        out_shape=[
            jax.ShapeDtypeStruct((8, 48, channels), F32),
            jax.ShapeDtypeStruct((400, channels), BF16),
            jax.ShapeDtypeStruct((8, channels), F32),
        ],
        scratch_shapes=[
            pltpu.VMEM((channels // 128, 384, 128), F32),
            pltpu.VMEM((96, TAP_SETS * 64), F32),
            pltpu.VMEM((80, channels), F32),
            pltpu.VMEM((88, channels), F32),
            pltpu.VMEM((88, 128), F32),
            pltpu.VMEM((own, channels), BF16),
            pltpu.VMEM((own, 128), F32),
            pltpu.VMEM(proj.shape, BF16),
            pltpu.VMEM(conv.shape, BF16),
            pltpu.VMEM(lifted.shape, F32),
            pltpu.VMEM(mine.shape, BF16),
            pltpu.VMEM(other.shape, BF16),
            pltpu.SemaphoreType.DMA((4,)),
            pltpu.SemaphoreType.DMA((conv.shape[0],)),
        ],
        compiler_params=params(58),
        cost_estimate=pl.CostEstimate(
            flops=3_000_000_000, bytes_accessed=14_000_000, transcendentals=100_000
        ),
    )(meta, lifted, mine, other, proj, conv, score)


def shards(
    states, kv_weight, queries, hidden, out_proj, disc_in, conv_weight, score_weight, frame_len, state_len
):
    frames = hidden.shape[1]
    dp_size, seq_size = (lax.axis_size("dp"), lax.axis_size("seq"))
    clip, seq = (lax.axis_index("dp"), lax.axis_index("seq"))
    core, half, row = (seq % 2, (seq // 2) % 2, seq // 4)
    pick = jnp.arange(frame_len.shape[0]) == clip
    clip_frames = jnp.sum(jnp.where(pick, frame_len, 0))
    clip_states = jnp.sum(jnp.where(pick, state_len, 0))

    def flip(x, bit):
        return lax.ppermute(x, "seq", [(i, i ^ bit) for i in range(seq_size)])

    def turn(x, hops):
        return lax.ppermute(x, "seq", [(i, (i + 4 * hops) % seq_size) for i in range(seq_size)])

    def swap(x, dp_bits, seq_bits):
        pairs = []
        for i in range(dp_size * seq_size):
            d, q = divmod(i, seq_size)
            pairs.append((i, (d ^ dp_bits) * seq_size + (q ^ seq_bits)))
        return lax.ppermute(x, ("dp", "seq"), pairs)

    def at(x, i):
        return lax.dynamic_index_in_dim(x, i, axis=0, keepdims=False)

    att = 2 * HALF_ATT

    proj_own = jnp.dot(out_proj, disc_in, preferred_element_type=F32).astype(BF16)
    kv_weight, proj_own = lax.optimization_barrier((kv_weight, proj_own))
    proj = lax.all_gather(proj_own, "seq", axis=0, tiled=True)

    def head_cols(which, kv_weight):
        parts = [
            lax.dynamic_slice_in_dim(kv_weight, kind * att + which * HALF_ATT, HALF_ATT, axis=1)
            for kind in (0, 1)
        ]
        return jnp.concatenate(parts, axis=1)

    far = head_cols(1 - half, kv_weight)
    far, kv_weight = lax.optimization_barrier((far, kv_weight))
    near = head_cols(half, kv_weight)
    far = swap(far, 1, 2)
    hops = (1, 3, 2)
    near_turned = [turn(near, j) for j in hops]
    states_in = states[0]
    near, near_turned, far, state_far, queries_in, hidden_in, conv_in = lax.optimization_barrier(
        (near, near_turned, far, flip(states_in, 2), queries[0], hidden[0], conv_weight)
    )

    lower = clip % 2
    channels = disc_in.shape[1]
    near_blocks = [near] + near_turned
    far_blocks = [far] + [turn(far, j) for j in hops]
    state_pair = flip(jnp.concatenate([states_in, state_far], axis=0), 1)
    up = [(i, i + 1) for i in range(seq_size - 1)]
    down = [(i + 1, i) for i in range(seq_size - 1)]
    before = jnp.concatenate([queries_in[frames - HALO :], hidden_in[frames - HALO :]], axis=1)
    before = lax.ppermute(before, "seq", up)
    after = jnp.concatenate([queries_in[:HALO], hidden_in[:HALO]], axis=1)

    cols = []
    for hop in (0, 1, 3, 2):
        for flip_half in (0, 1):
            where = (((row - hop) % 4) * 2 + (half ^ flip_half)) * 2 + core
            cols.append(where * kv_weight.shape[0])
    total_frames = frames * seq_size
    cols = jnp.stack(cols + [core]).astype(jnp.int32)
    meta = jnp.stack([clip_states, core, half, row]).astype(jnp.int32)
    meta2 = jnp.stack([clip_frames, seq * frames, half, jnp.int32(total_frames), core])
    meta3 = jnp.stack([row, 2 * half + lower, clip // 2]).astype(jnp.int32)
    blocks = [b for pair in zip(near_blocks, far_blocks) for b in pair]
    tables = (cols, meta, meta2.astype(jnp.int32), meta3)
    conv = arrange(conv_in)
    blocks, state_pair, tables, before, after, conv = lax.optimization_barrier(
        (blocks, state_pair, tables, before, after, conv)
    )
    cols, meta, meta2, meta3 = tables
    state_parts = [states_in, state_far, state_pair]
    kept, sent = project(cols, state_parts, blocks)
    mine_kv = (kept + flip(sent, 1)).reshape(256, HALF_ATT)

    mine_kv, proj, queries_in, hidden_in, before, after = lax.optimization_barrier(
        (mine_kv, proj, queries[0], hidden[0], before, after)
    )
    got = [mine_kv] + [turn(mine_kv, j) for j in (1, 2, 3)]
    rows_in = jnp.concatenate([queries_in, hidden_in], axis=1)
    rows_ext = jnp.concatenate([before, rows_in, lax.ppermute(after, "seq", down)], axis=0)
    query_ext, hidden_ext = (rows_ext[:, :att], rows_ext[:, att:])
    query_mine = lax.dynamic_slice_in_dim(query_ext, half * HALF_ATT, HALF_ATT, axis=1)
    query_far = flip(lax.dynamic_slice_in_dim(query_ext, (1 - half) * HALF_ATT, HALF_ATT, axis=1), 2)
    lifted = jnp.dot(hidden_ext, disc_in, preferred_element_type=F32)
    got, query_mine, query_far, lifted = lax.optimization_barrier((got, query_mine, query_far, lifted))
    other = [flip(g, 1) for g in got]

    attended_far = flip(attend(meta, query_far, got, other), 2)
    attended_mine = attend(meta, query_mine, got, other)

    kept, sent, loss = critic(
        meta2, lifted, attended_mine, attended_far, proj, conv, score_weight.reshape(1, -1)
    )

    own_rows = att // seq_size
    share = own_rows // 2
    own, *pieces = core_sum(meta3, kept, flip(sent, 1), loss)
    arrived = [flip(p, 4 * (j + 1)) for j, p in enumerate(pieces)]
    own, *pieces = row_sum(meta3, own, arrived)
    a, b, c = [swap(p, j & 1, j & 2) for j, p in zip((1, 2, 3), pieces)]
    total = (own + a) + (b + c)
    a, b, c = [swap(total, d, 0) for d in (2, 4, 6)]
    total = (total + a) + (b + c)
    total = total + swap(total, 8, 0)
    total_loss = total[share, 0]
    total = total[:share]
    beside = swap(total, 1, 0)
    first = lower == 0
    total = jnp.concatenate([jnp.where(first, total, beside), jnp.where(first, beside, total)], axis=0)
    grad_proj = lift(total, disc_in)
    counted = jnp.sum((frame_len + STRIDE - 1) // STRIDE).astype(F32)
    return (grad_proj, total_loss / counted)


def solution(mesh):
    return jax.shard_map(
        shards,
        mesh=mesh,
        in_specs=(
            P("dp", "seq", None),
            P("seq", None),
            P("dp", "seq", None),
            P("dp", "seq", None),
            P("seq", None),
            P(),
            P(),
            P(),
            P(),
            P(),
        ),
        out_specs=(P("seq", None), P()),
        check_vma=False,
    )
```

```python
import functools
import math

import jax
import jax.numpy as jnp
from jax import lax
from jax.experimental import pallas as pl
from jax.experimental.pallas import tpu as pltpu
from jax.sharding import PartitionSpec as P

HEAD_DIM = 128
HALF_HEADS = 3
HALF_ATT = HEAD_DIM * HALF_HEADS
GROUP_CH = 64
STRIDE = 4
TAPS = 41
TAP_SETS = 12
MARGIN = 20
HALO = 40
REACH = 5
F32 = jnp.float32
BF16 = jnp.bfloat16
MIB = 1024 * 1024


def params(mib):
    return pltpu.CompilerParams(vmem_limit_bytes=mib * MIB)


def smem():
    return pl.BlockSpec(memory_space=pltpu.SMEM)


def vmem():
    return pl.BlockSpec(memory_space=pltpu.VMEM)


def anywhere():
    return pl.BlockSpec(memory_space=pltpu.HBM)


def low_lanes(shape):
    return lax.broadcasted_iota(jnp.int32, shape, 1) % 128 < 64


def roll_half(x):
    return pltpu.roll(x, 64, 1)


def arrange_kernel(w_ref, o_ref):
    low = low_lanes((GROUP_CH, 128))
    zero = jnp.zeros((GROUP_CH, 128), F32)

    def tap(k):
        return w_ref[k].astype(F32) if k < TAPS else zero

    for b in range(STRIDE):
        for pair in range(TAP_SETS // 2):
            first = tap(8 * pair + b)
            second = tap(8 * pair + 4 + b)
            rows, lanes = (slice(b * 64, b * 64 + 64), slice(pair * 128, pair * 128 + 128))
            o_ref[0, rows, lanes] = jnp.where(low, first, roll_half(second)).astype(BF16)
            o_ref[1, rows, lanes] = jnp.where(low, roll_half(first), second).astype(BF16)


def arrange(conv_weight):
    taps, group_in, channels = conv_weight.shape
    groups = channels // GROUP_CH
    return pl.pallas_call(
        arrange_kernel,
        grid=(channels // 128,),
        in_specs=[pl.BlockSpec((taps, group_in, 128), lambda l: (0, 0, l))],
        out_specs=pl.BlockSpec((2, STRIDE * 64, TAP_SETS * 64), lambda l: (l, 0, 0)),
        out_shape=jax.ShapeDtypeStruct((groups, STRIDE * 64, TAP_SETS * 64), BF16),
        compiler_params=params(58),
        cost_estimate=pl.CostEstimate(flops=20_000_000, bytes_accessed=20_000_000, transcendentals=0),
    )(conv_weight)


def project_kernel(cols_ref, *refs):
    states, weights, (keep_ref, send_ref) = (refs[:3], refs[3:13], refs[13:15])
    state_s, weight_s, total_s, state_sem, weight_sem = refs[15:]
    core = cols_ref[8]
    state_copies = [
        pltpu.make_async_copy(s, state_s.at[place], state_sem.at[i])
        for i, (s, place) in enumerate(
            ((states[0], 0), (states[1], 2), (states[2].at[:64], 1), (states[2].at[64:], 3))
        )
    ]
    weight_copies = [
        pltpu.make_async_copy(w, weight_s.at[i], weight_sem.at[i]) for i, w in enumerate(weights[:6])
    ]
    half_rows = weights[6].shape[0]
    for i in (6, 7):
        for side in range(2):
            source = 2 * i - 6 + side
            rows = pl.ds(half_rows * side, half_rows)
            weight_copies.append(
                pltpu.make_async_copy(weights[source], weight_s.at[i, rows], weight_sem.at[source])
            )
    for copy in state_copies + weight_copies:
        copy.start()
    for copy in state_copies:
        copy.wait()
    for i in range(8):
        for copy in weight_copies[i : i + 1] if i < 6 else weight_copies[2 * i - 6 : 2 * i - 4]:
            copy.wait()
        start = pl.multiple_of(cols_ref[i], 256)
        left = jnp.concatenate([state_s[j, :, pl.ds(start, 256)] for j in range(4)], axis=0)
        part = jnp.dot(left, weight_s[i], preferred_element_type=F32)
        if i == 0:
            total_s[...] = part
        else:
            total_s[...] += part
    kept = pl.ds(pl.multiple_of(core * HALF_ATT, 128), HALF_ATT)
    sent = pl.ds(pl.multiple_of((1 - core) * HALF_ATT, 128), HALF_ATT)
    for j in range(4):
        rows = slice(64 * j, 64 * j + 64)
        block = 2 * (j // 2) + (core + j) % 2
        keep_ref[block] = total_s[rows, kept]
        send_ref[block] = total_s[rows, sent]


def project(cols, states, weights):
    width = 2 * HALF_ATT
    out = jax.ShapeDtypeStruct((4, 64, HALF_ATT), F32)
    return pl.pallas_call(
        project_kernel,
        in_specs=[smem()] + [anywhere()] * 13,
        out_specs=[vmem(), vmem()],
        out_shape=[out, out],
        scratch_shapes=[
            pltpu.VMEM((4,) + states[0].shape, BF16),
            pltpu.VMEM((8,) + weights[0].shape, BF16),
            pltpu.VMEM((256, width), F32),
            pltpu.SemaphoreType.DMA((4,)),
            pltpu.SemaphoreType.DMA((10,)),
        ],
        compiler_params=params(58),
        cost_estimate=pl.CostEstimate(flops=800_000_000, bytes_accessed=6_000_000, transcendentals=0),
    )(cols, *states, *weights)


def split(x):
    high = x.astype(BF16)
    return high, (x - high.astype(F32)).astype(BF16)


def attend_kernel(meta_ref, q_ref, *refs):
    mine, other, o_ref = (refs[:4], refs[4:8], refs[8])
    live, core, half, row = (meta_ref[0], meta_ref[1], meta_ref[2], meta_ref[3])
    first = core == 0
    keys, values = ([], [])
    for m, o in zip(mine, other):
        keys.append(jnp.where(first, m[...], o[...]))
        values.append(jnp.where(first, o[...], m[...]))
    key_high, key_low = split(jnp.concatenate(keys, axis=0) * (1.0 / math.sqrt(HEAD_DIM)))
    value_high, value_low = split(jnp.concatenate(values, axis=0))
    spot = lax.broadcasted_iota(jnp.int32, (1, 1024), 1)
    hop, block, rest = (spot // 256, (spot // 64) % 4, spot % 64)
    where_y = (row - hop + 4) % 4
    where_h = (half + block // 2) % 2
    position = ((where_y * 2 + where_h) * 2 + block % 2) * 64 + rest
    alive = position < live
    contract = (((1,), (1,)), ((), ()))
    rows = 112
    for start in range(0, q_ref.shape[0], rows):
        q = q_ref[start : start + rows, :]
        scores = lax.dot_general(q, key_high, contract, preferred_element_type=F32)
        scores = scores + lax.dot_general(q, key_low, contract, preferred_element_type=F32)
        scores = jnp.where(alive, scores, -1e30)
        top = jnp.max(scores, axis=1, keepdims=True)
        expo = jnp.exp(scores - top)
        denom = jnp.sum(expo, axis=1, keepdims=True)
        weights = expo.astype(BF16)
        mixed = jnp.dot(weights, value_high, preferred_element_type=F32)
        mixed = mixed + jnp.dot(weights, value_low, preferred_element_type=F32)
        o_ref[start : start + rows, :] = (mixed / denom).astype(BF16)


def attend(meta, query, mine, other):
    rows, width = query.shape
    block = lambda n: pl.BlockSpec((n, HEAD_DIM), lambda h: (0, h))
    return pl.pallas_call(
        attend_kernel,
        grid=(width // HEAD_DIM,),
        in_specs=[smem(), block(rows)] + [block(256)] * 8,
        out_specs=block(rows),
        out_shape=jax.ShapeDtypeStruct((rows, width), BF16),
        compiler_params=params(12),
        cost_estimate=pl.CostEstimate(
            flops=8 * rows * 1024 * width, bytes_accessed=4_000_000, transcendentals=rows * 3072
        ),
    )(meta, query, *mine, *other)


def coded_rows(value):
    high = value.astype(BF16).astype(F32)
    middle = (value - high).astype(BF16).astype(F32)
    low = value - high - middle
    line = lax.broadcasted_iota(jnp.int32, value.shape, 0)
    return jnp.where(line == 0, high, jnp.where(line == 1, middle, low)).astype(BF16)


def decoded_rows(rows):
    rows = rows.astype(F32)
    return (rows[0:1] + rows[1:2]) + rows[2:3]


def core_sum_kernel(meta_ref, kept_ref, arrived_ref, loss_ref, own_ref, *piece_refs):
    row = meta_ref[0]
    loss = loss_ref[:1] + decoded_rows(arrived_ref[384:, :])
    cells = coded_rows(jnp.broadcast_to(loss, (16, loss.shape[1])))
    for j in range(4):
        where = (row + j) % 4 if j == 0 else lax.bitwise_xor(row, j)
        for q in range(2):
            rows = pl.ds(pl.multiple_of(96 * where + 48 * q, 48), 48)
            total = kept_ref[2 * where + q] + arrived_ref[rows, :].astype(F32)
            if j == 0:
                own_ref[48 * q : 48 * q + 48, :] = total
            else:
                piece_refs[j - 1][48 * q : 48 * q + 48, :] = total.astype(BF16)
        if j == 0:
            own_ref[96:, :] = jnp.broadcast_to(loss, (8, loss.shape[1]))
        else:
            piece_refs[j - 1][96:, :] = cells


def core_sum(meta, kept, arrived, loss):
    channels = kept.shape[2]
    return pl.pallas_call(
        core_sum_kernel,
        in_specs=[smem()] + [vmem()] * 3,
        out_specs=[vmem()] * 4,
        out_shape=[jax.ShapeDtypeStruct((104, channels), F32)]
        + [jax.ShapeDtypeStruct((112, channels), BF16)] * 3,
        compiler_params=params(12),
        cost_estimate=pl.CostEstimate(flops=1_000_000, bytes_accessed=4_000_000, transcendentals=0),
    )(meta, kept, arrived, loss)


def row_sum_kernel(meta_ref, own_ref, one_ref, two_ref, three_ref, *out_refs):
    place = meta_ref[1]
    refs = (one_ref, two_ref, three_ref)
    first, second, third = [decoded_rows(r[96:, :]) for r in refs]
    loss = (own_ref[96:97, :] + first) + (second + third)
    for j in range(4):
        start = pl.multiple_of(24 * lax.bitwise_xor(place, j), 8)
        at = 48 * (lax.bitwise_xor(place, j) // 2)
        total = own_ref[pl.ds(start, 24), :]
        upper = lax.bitwise_xor(place, j) % 2 == 1
        for r in refs:
            rows = r[pl.ds(pl.multiple_of(at, 48), 48), :].astype(F32)
            total = total + jnp.where(upper, rows[24:], rows[:24])
        out_refs[j][:24, :] = total
        out_refs[j][24:, :] = jnp.broadcast_to(loss, (8, loss.shape[1]))


def row_sum(meta, own, arrived):
    channels = own.shape[1]
    return pl.pallas_call(
        row_sum_kernel,
        in_specs=[smem()] + [vmem()] * 4,
        out_specs=[vmem()] * 4,
        out_shape=[jax.ShapeDtypeStruct((32, channels), F32)] * 4,
        compiler_params=params(8),
        cost_estimate=pl.CostEstimate(flops=1_000_000, bytes_accessed=2_000_000, transcendentals=0),
    )(meta, own, *arrived)


def lift_kernel(full_ref, disc_ref, out_ref):
    rows = full_ref.shape[0]
    both = jnp.concatenate(split(full_ref[...]), axis=0)
    wide = disc_ref.shape[0] // 3
    for i in range(3):
        cols = slice(wide * i, wide * i + wide)
        product = lax.dot_general(
            both, disc_ref[cols, :], (((1,), (1,)), ((), ())), preferred_element_type=F32
        )
        out_ref[:, cols] = product[:rows] + product[rows:]


def lift(full, disc_in):
    return pl.pallas_call(
        lift_kernel,
        in_specs=[vmem()] * 2,
        out_specs=vmem(),
        out_shape=jax.ShapeDtypeStruct((full.shape[0], disc_in.shape[0]), F32),
        compiler_params=params(12),
        cost_estimate=pl.CostEstimate(flops=300_000_000, bytes_accessed=3_500_000, transcendentals=0),
    )(full, disc_in)


def critic_kernel(
    meta_ref, lifted_hbm, mine_hbm, other_hbm, proj_hbm, conv_hbm, score_ref,
    keep_ref, send_ref, loss_ref,
    feed_s, y_s, pre_s, grad_s, turned_s, back_s, att_s, proj_s, conv_ref, lifted_ref, mine_ref, other_ref, proj_sem, conv_sem,
):
    live, first_frame, half = (meta_ref[0], meta_ref[1], meta_ref[2])
    total_frames, core = (meta_ref[3], meta_ref[4])
    pairs = [(lifted_hbm, lifted_ref), (mine_hbm, mine_ref), (other_hbm, other_ref), (proj_hbm, proj_s)]
    proj_copies = [pltpu.make_async_copy(a, b, proj_sem.at[i]) for i, (a, b) in enumerate(pairs)]
    conv_copies = [
        pltpu.make_async_copy(conv_hbm.at[g], conv_ref.at[g], conv_sem.at[g])
        for g in range(conv_ref.shape[0])
    ]
    for copy in proj_copies + conv_copies:
        copy.start()
    ext = lifted_ref.shape[0]
    own_out = (ext - 2 * HALO) // STRIDE
    tiles = lifted_ref.shape[1] // 128
    for copy in proj_copies:
        copy.wait()
    feed = lifted_ref[...]
    for ref, which in ((mine_ref, half), (other_ref, 1 - half)):
        proj = proj_s[pl.ds(pl.multiple_of(HALF_ATT * which, HALF_ATT), HALF_ATT), :]
        feed = feed + jnp.dot(ref[...], proj, preferred_element_type=F32)
    frame = first_frame - HALO + lax.broadcasted_iota(jnp.int32, (ext, 1), 0)
    inside = (frame >= 0) & (frame < live)
    feed = jnp.where(inside, feed, 0.0).astype(BF16).astype(F32)
    for i in range(tiles):
        feed_s[i, :ext, :] = feed[:, 128 * i : 128 * i + 128]
        feed_s[i, ext:, :] = jnp.zeros((feed_s.shape[1] - ext, 128), F32)
    rows = y_s.shape[0]
    low = low_lanes((rows, 128))
    low_out = low_lanes((80, 128))
    for copy in conv_copies:
        copy.wait()

    @pl.loop(0, tiles, unroll=4)
    def _(tile):
        lanes = pl.ds(pl.multiple_of(tile * 128, 128), 128)
        phase = [feed_s[tile, pl.ds(b, rows, stride=STRIDE), :] for b in range(STRIDE)]
        turned = [roll_half(p) for p in phase]
        even = [jnp.where(low, phase[b], turned[b + 1]) for b in (0, 2)]
        odd = [jnp.where(low, turned[b], phase[b + 1]) for b in (0, 2)]
        sums = []
        for g, pieces in enumerate((even, odd)):
            left = jnp.concatenate(pieces, axis=1).astype(BF16)
            y_s[...] = jnp.dot(left, conv_ref[2 * tile + g], preferred_element_type=F32)
            at, after = (None, None)
            for pair in range(TAP_SETS // 2):
                cols = slice(128 * pair, 128 * pair + 128)
                a = y_s[2 * pair : 2 * pair + 80, cols]
                b = y_s[2 * pair + 1 : 2 * pair + 81, cols]
                at = a if at is None else at + a
                after = b if after is None else after + b
            sums.append((at, after))
        pre_even = sums[0][0] + roll_half(sums[0][1])
        pre_odd = roll_half(sums[1][0]) + sums[1][1]
        pre_s[:, lanes] = jnp.where(low_out, pre_even, pre_odd)

    pre = pre_s[...]
    sig = 1.0 / (1.0 + jnp.exp(-pre))
    score = score_ref[...]
    critic = jnp.sum(pre * sig * score, axis=1, keepdims=True)
    slot = lax.broadcasted_iota(jnp.int32, (80, 1), 0)
    frame_out = first_frame - STRIDE * REACH + STRIDE * slot
    valid = (frame_out >= 0) & (frame_out < total_frames) & (frame_out < live) & (slot < own_out + 2 * REACH)
    shortfall = 1.0 - critic
    own = valid & (slot >= REACH) & (slot < REACH + own_out)
    loss = jnp.sum(jnp.where(own, shortfall * shortfall, 0.0), axis=0, keepdims=True)
    loss_ref[...] = jnp.broadcast_to(loss, loss_ref.shape)
    send_ref[384:, :] = coded_rows(jnp.broadcast_to(loss, (16, send_ref.shape[1])))
    push = jnp.where(valid, -2.0 * shortfall, 0.0)
    grad = push * score * (sig * (1.0 + pre * (1.0 - sig)))
    grad = jnp.where(valid, grad, 0.0).astype(BF16).astype(F32)
    grad_s[:8, :] = jnp.zeros((8, grad_s.shape[1]), F32)
    grad_s[8:, :] = grad

    contract = (((1,), (1,)), ((), ()))
    low_back = low_lanes((own_out, 128))

    @pl.loop(0, tiles, unroll=4)
    def _(tile):
        lanes = pl.ds(pl.multiple_of(tile * 128, 128), 128)
        turned_s[...] = roll_half(grad_s[:, lanes])
        even, odd = ([], [])
        for pair in range(TAP_SETS // 2):
            up, down = (18 - 2 * pair, 17 - 2 * pair)
            even.append(
                jnp.where(low_back, grad_s[up : up + own_out, lanes], turned_s[down : down + own_out, :])
            )
            odd.append(
                jnp.where(low_back, turned_s[up : up + own_out, :], grad_s[down : down + own_out, lanes])
            )
        back = []
        for g, pieces in enumerate((even, odd)):
            left = jnp.concatenate(pieces, axis=1).astype(BF16)
            back.append(
                lax.dot_general(left, conv_ref[2 * tile + g], contract, preferred_element_type=F32)
            )
        step = lax.broadcasted_iota(jnp.int32, (own_out, 1), 0)
        for b in range(STRIDE):
            cols = slice(128 * (b // 2), 128 * (b // 2) + 128)
            e, o = (back[0][:, cols], back[1][:, cols])
            both = jnp.where(low_back, e, roll_half(o)) if b % 2 == 0 else jnp.where(low_back, roll_half(e), o)
            both = jnp.where(first_frame + STRIDE * step + b < live, both, 0.0)
            back_s[b * own_out : (b + 1) * own_out, lanes] = both.astype(BF16)

    first = core == 0
    for part, ref in enumerate((mine_ref, other_ref)):
        own_rows = ref[...].astype(F32)[HALO : ext - HALO, :]
        lefts = []
        for c in range(HALF_HEADS):
            att_s[...] = own_rows[:, c * 128 : c * 128 + 128]
            left = jnp.concatenate(
                [att_s[pl.ds(b, own_out, stride=STRIDE), :] for b in range(STRIDE)], axis=0
            )
            lefts.append(jnp.transpose(left))
        left = jnp.concatenate(lefts, axis=0).astype(BF16)
        which = half if part == 0 else 1 - half
        for q in range(4):
            block = jnp.dot(left[96 * q : 96 * q + 96], back_s[...], preferred_element_type=F32)
            one, two = (block[:48], block[48:])
            keep_ref[4 * which + q] = jnp.where(first, one, two)
            rows = pl.ds(pl.multiple_of(48 * (4 * which + q), 48), 48)
            send_ref[rows, :] = jnp.where(first, two, one).astype(BF16)


def critic(meta, lifted, mine, other, proj, conv, score):
    ext, channels = lifted.shape
    own = ext - 2 * HALO
    return pl.pallas_call(
        critic_kernel,
        in_specs=[smem()] + [anywhere()] * 5 + [vmem()],
        out_specs=[vmem(), vmem(), vmem()],
        out_shape=[
            jax.ShapeDtypeStruct((8, 48, channels), F32),
            jax.ShapeDtypeStruct((400, channels), BF16),
            jax.ShapeDtypeStruct((8, channels), F32),
        ],
        scratch_shapes=[
            pltpu.VMEM((channels // 128, 384, 128), F32),
            pltpu.VMEM((96, TAP_SETS * 64), F32),
            pltpu.VMEM((80, channels), F32),
            pltpu.VMEM((88, channels), F32),
            pltpu.VMEM((88, 128), F32),
            pltpu.VMEM((own, channels), BF16),
            pltpu.VMEM((own, 128), F32),
            pltpu.VMEM(proj.shape, BF16),
            pltpu.VMEM(conv.shape, BF16),
            pltpu.VMEM(lifted.shape, F32),
            pltpu.VMEM(mine.shape, BF16),
            pltpu.VMEM(other.shape, BF16),
            pltpu.SemaphoreType.DMA((4,)),
            pltpu.SemaphoreType.DMA((conv.shape[0],)),
        ],
        compiler_params=params(58),
        cost_estimate=pl.CostEstimate(
            flops=3_000_000_000, bytes_accessed=14_000_000, transcendentals=100_000
        ),
    )(meta, lifted, mine, other, proj, conv, score)


def shards(
    states, kv_weight, queries, hidden, out_proj, disc_in, conv_weight, score_weight, frame_len, state_len
):
    frames = hidden.shape[1]
    dp_size, seq_size = (lax.axis_size("dp"), lax.axis_size("seq"))
    clip, seq = (lax.axis_index("dp"), lax.axis_index("seq"))
    core, half, row = (seq % 2, (seq // 2) % 2, seq // 4)
    pick = jnp.arange(frame_len.shape[0]) == clip
    clip_frames = jnp.sum(jnp.where(pick, frame_len, 0))
    clip_states = jnp.sum(jnp.where(pick, state_len, 0))

    def flip(x, bit):
        return lax.ppermute(x, "seq", [(i, i ^ bit) for i in range(seq_size)])

    def turn(x, hops):
        return lax.ppermute(x, "seq", [(i, (i + 4 * hops) % seq_size) for i in range(seq_size)])

    def swap(x, dp_bits, seq_bits):
        pairs = []
        for i in range(dp_size * seq_size):
            d, q = divmod(i, seq_size)
            pairs.append((i, (d ^ dp_bits) * seq_size + (q ^ seq_bits)))
        return lax.ppermute(x, ("dp", "seq"), pairs)

    def at(x, i):
        return lax.dynamic_index_in_dim(x, i, axis=0, keepdims=False)

    att = 2 * HALF_ATT

    proj_own = jnp.dot(out_proj, disc_in, preferred_element_type=F32).astype(BF16)
    kv_weight, proj_own = lax.optimization_barrier((kv_weight, proj_own))
    proj = lax.all_gather(proj_own, "seq", axis=0, tiled=True)

    def head_cols(which, kv_weight):
        parts = [
            lax.dynamic_slice_in_dim(kv_weight, kind * att + which * HALF_ATT, HALF_ATT, axis=1)
            for kind in (0, 1)
        ]
        return jnp.concatenate(parts, axis=1)

    far = head_cols(1 - half, kv_weight)
    far, kv_weight = lax.optimization_barrier((far, kv_weight))
    near = head_cols(half, kv_weight)
    far = swap(far, 1, 2)
    near_turned = [turn(near, j) for j in (1, 3)]

    def pass_on(turned):
        rows = near.shape[0] // 2
        return [turn(turned[0][:rows], 1), turn(turned[1][rows:], 3)]

    states_in = states[0]
    near, near_turned, far, state_far, queries_in, hidden_in, conv_in = lax.optimization_barrier(
        (near, near_turned, far, flip(states_in, 2), queries[0], hidden[0], conv_weight)
    )

    lower = clip % 2
    channels = disc_in.shape[1]
    near_over = pass_on(near_turned)
    far_turned = [turn(far, j) for j in (1, 3)]
    state_pair = flip(jnp.concatenate([states_in, state_far], axis=0), 1)
    up = [(i, i + 1) for i in range(seq_size - 1)]
    down = [(i + 1, i) for i in range(seq_size - 1)]
    near_over, far_turned, state_pair, queries_in, hidden_in = lax.optimization_barrier(
        (near_over, far_turned, state_pair, queries_in, hidden_in)
    )

    far_over = pass_on(far_turned)
    before = jnp.concatenate([queries_in[frames - HALO :], hidden_in[frames - HALO :]], axis=1)
    before = lax.ppermute(before, "seq", up)
    after = jnp.concatenate([queries_in[:HALO], hidden_in[:HALO]], axis=1)

    cols = []
    for hop in (0, 1, 3, 2):
        for flip_half in (0, 1):
            where = (((row - hop) % 4) * 2 + (half ^ flip_half)) * 2 + core
            cols.append(where * kv_weight.shape[0])
    total_frames = frames * seq_size
    cols = jnp.stack(cols + [core]).astype(jnp.int32)
    meta = jnp.stack([clip_states, core, half, row]).astype(jnp.int32)
    meta2 = jnp.stack([clip_frames, seq * frames, half, jnp.int32(total_frames), core])
    meta3 = jnp.stack([row, 2 * half + lower, clip // 2]).astype(jnp.int32)
    blocks = [near, far, near_turned[0], far_turned[0], near_turned[1], far_turned[1]] + near_over + far_over
    tables = (cols, meta, meta2.astype(jnp.int32), meta3)
    conv = arrange(conv_in)
    blocks, state_pair, tables, before, after, conv = lax.optimization_barrier(
        (blocks, state_pair, tables, before, after, conv)
    )
    cols, meta, meta2, meta3 = tables
    state_parts = [states_in, state_far, state_pair]
    kept, sent = project(cols, state_parts, blocks)
    mine_kv = (kept + flip(sent, 1)).reshape(256, HALF_ATT)

    mine_kv, proj, queries_in, hidden_in, before, after = lax.optimization_barrier(
        (mine_kv, proj, queries[0], hidden[0], before, after)
    )
    got = [mine_kv] + [turn(mine_kv, j) for j in (1, 2, 3)]
    rows_in = jnp.concatenate([queries_in, hidden_in], axis=1)
    rows_ext = jnp.concatenate([before, rows_in, lax.ppermute(after, "seq", down)], axis=0)
    query_ext, hidden_ext = (rows_ext[:, :att], rows_ext[:, att:])
    query_mine = lax.dynamic_slice_in_dim(query_ext, half * HALF_ATT, HALF_ATT, axis=1)
    query_far = flip(lax.dynamic_slice_in_dim(query_ext, (1 - half) * HALF_ATT, HALF_ATT, axis=1), 2)
    lifted = jnp.dot(hidden_ext, disc_in, preferred_element_type=F32)
    got, query_mine, query_far, lifted = lax.optimization_barrier((got, query_mine, query_far, lifted))
    other = [flip(g, 1) for g in got]

    attended_far = flip(attend(meta, query_far, got, other), 2)
    attended_mine = attend(meta, query_mine, got, other)

    kept, sent, loss = critic(
        meta2, lifted, attended_mine, attended_far, proj, conv, score_weight.reshape(1, -1)
    )

    own_rows = att // seq_size
    share = own_rows // 2
    own, *pieces = core_sum(meta3, kept, flip(sent, 1), loss)
    arrived = [flip(p, 4 * (j + 1)) for j, p in enumerate(pieces)]
    own, *pieces = row_sum(meta3, own, arrived)
    a, b, c = [swap(p, j & 1, j & 2) for j, p in zip((1, 2, 3), pieces)]
    total = (own + a) + (b + c)
    a, b, c = [swap(total, d, 0) for d in (2, 4, 6)]
    total = (total + a) + (b + c)
    total = total + swap(total, 8, 0)
    total_loss = total[share, 0]
    total = total[:share]
    beside = swap(total, 1, 0)
    first = lower == 0
    total = jnp.concatenate([jnp.where(first, total, beside), jnp.where(first, beside, total)], axis=0)
    grad_proj = lift(total, disc_in)
    counted = jnp.sum((frame_len + STRIDE - 1) // STRIDE).astype(F32)
    return (grad_proj, total_loss / counted)


def solution(mesh):
    return jax.shard_map(
        shards,
        mesh=mesh,
        in_specs=(
            P("dp", "seq", None),
            P("seq", None),
            P("dp", "seq", None),
            P("dp", "seq", None),
            P("seq", None),
            P(),
            P(),
            P(),
            P(),
            P(),
        ),
        out_specs=(P("seq", None), P()),
        check_vma=False,
    )
```

```python
import functools
import math

import jax
import jax.numpy as jnp
from jax import lax
from jax.experimental import pallas as pl
from jax.experimental.pallas import tpu as pltpu
from jax.sharding import PartitionSpec as P

HEAD_DIM = 128
HALF_HEADS = 3
HALF_ATT = HEAD_DIM * HALF_HEADS
GROUP_CH = 64
STRIDE = 4
TAPS = 41
TAP_SETS = 12
MARGIN = 20
HALO = 40
REACH = 5
F32 = jnp.float32
BF16 = jnp.bfloat16
MIB = 1024 * 1024


def params(mib):
    return pltpu.CompilerParams(vmem_limit_bytes=mib * MIB)


def smem():
    return pl.BlockSpec(memory_space=pltpu.SMEM)


def vmem():
    return pl.BlockSpec(memory_space=pltpu.VMEM)


def anywhere():
    return pl.BlockSpec(memory_space=pltpu.HBM)


def low_lanes(shape):
    return lax.broadcasted_iota(jnp.int32, shape, 1) % 128 < 64


def roll_half(x):
    return pltpu.roll(x, 64, 1)


def arrange_kernel(w_ref, o_ref):
    low = low_lanes((GROUP_CH, 128))
    zero = jnp.zeros((GROUP_CH, 128), F32)

    def tap(k):
        return w_ref[k].astype(F32) if k < TAPS else zero

    for b in range(STRIDE):
        for pair in range(TAP_SETS // 2):
            first = tap(8 * pair + b)
            second = tap(8 * pair + 4 + b)
            rows, lanes = (slice(b * 64, b * 64 + 64), slice(pair * 128, pair * 128 + 128))
            o_ref[0, rows, lanes] = jnp.where(low, first, roll_half(second)).astype(BF16)
            o_ref[1, rows, lanes] = jnp.where(low, roll_half(first), second).astype(BF16)


def arrange(conv_weight):
    taps, group_in, channels = conv_weight.shape
    groups = channels // GROUP_CH
    return pl.pallas_call(
        arrange_kernel,
        grid=(channels // 128,),
        in_specs=[pl.BlockSpec((taps, group_in, 128), lambda l: (0, 0, l))],
        out_specs=pl.BlockSpec((2, STRIDE * 64, TAP_SETS * 64), lambda l: (l, 0, 0)),
        out_shape=jax.ShapeDtypeStruct((groups, STRIDE * 64, TAP_SETS * 64), BF16),
        compiler_params=params(58),
        cost_estimate=pl.CostEstimate(flops=20_000_000, bytes_accessed=20_000_000, transcendentals=0),
    )(conv_weight)


def project_kernel(cols_ref, *refs):
    states, weights, (keep_ref, send_ref) = (refs[:3], refs[3:13], refs[13:15])
    state_s, weight_s, total_s, state_sem, weight_sem = refs[15:]
    core = cols_ref[8]
    state_copies = [
        pltpu.make_async_copy(s, state_s.at[place], state_sem.at[i])
        for i, (s, place) in enumerate(
            ((states[0], 0), (states[1], 2), (states[2].at[:64], 1), (states[2].at[64:], 3))
        )
    ]
    weight_copies = [
        pltpu.make_async_copy(w, weight_s.at[i], weight_sem.at[i]) for i, w in enumerate(weights[:6])
    ]
    half_rows = weights[6].shape[0]
    for i in (6, 7):
        for side in range(2):
            source = 2 * i - 6 + side
            rows = pl.ds(half_rows * side, half_rows)
            weight_copies.append(
                pltpu.make_async_copy(weights[source], weight_s.at[i, rows], weight_sem.at[source])
            )
    for copy in state_copies + weight_copies:
        copy.start()
    for copy in state_copies:
        copy.wait()
    for i in range(8):
        for copy in weight_copies[i : i + 1] if i < 6 else weight_copies[2 * i - 6 : 2 * i - 4]:
            copy.wait()
        start = pl.multiple_of(cols_ref[i], 256)
        left = jnp.concatenate([state_s[j, :, pl.ds(start, 256)] for j in range(4)], axis=0)
        part = jnp.dot(left, weight_s[i], preferred_element_type=F32)
        if i == 0:
            total_s[...] = part
        else:
            total_s[...] += part
    kept = pl.ds(pl.multiple_of(core * HALF_ATT, 128), HALF_ATT)
    sent = pl.ds(pl.multiple_of((1 - core) * HALF_ATT, 128), HALF_ATT)
    for j in range(4):
        rows = slice(64 * j, 64 * j + 64)
        block = 2 * (j // 2) + (core + j) % 2
        keep_ref[block] = total_s[rows, kept]
        send_ref[block] = total_s[rows, sent]


def project(cols, states, weights):
    width = 2 * HALF_ATT
    out = jax.ShapeDtypeStruct((4, 64, HALF_ATT), F32)
    return pl.pallas_call(
        project_kernel,
        in_specs=[smem()] + [anywhere()] * 13,
        out_specs=[vmem(), vmem()],
        out_shape=[out, out],
        scratch_shapes=[
            pltpu.VMEM((4,) + states[0].shape, BF16),
            pltpu.VMEM((8,) + weights[0].shape, BF16),
            pltpu.VMEM((256, width), F32),
            pltpu.SemaphoreType.DMA((4,)),
            pltpu.SemaphoreType.DMA((10,)),
        ],
        compiler_params=params(58),
        cost_estimate=pl.CostEstimate(flops=800_000_000, bytes_accessed=6_000_000, transcendentals=0),
    )(cols, *states, *weights)


def split(x):
    high = x.astype(BF16)
    return high, (x - high.astype(F32)).astype(BF16)


def attend_kernel(meta_ref, q_ref, *refs):
    mine, other, o_ref = (refs[:4], refs[4:8], refs[8])
    live, core, half, row = (meta_ref[0], meta_ref[1], meta_ref[2], meta_ref[3])
    first = core == 0
    keys, values = ([], [])
    for m, o in zip(mine, other):
        keys.append(jnp.where(first, m[...], o[...]))
        values.append(jnp.where(first, o[...], m[...]))
    key_high, key_low = split(jnp.concatenate(keys, axis=0) * (1.0 / math.sqrt(HEAD_DIM)))
    value_high, value_low = split(jnp.concatenate(values, axis=0))
    spot = lax.broadcasted_iota(jnp.int32, (1, 1024), 1)
    hop, block, rest = (spot // 256, (spot // 64) % 4, spot % 64)
    where_y = (row - hop + 4) % 4
    where_h = (half + block // 2) % 2
    position = ((where_y * 2 + where_h) * 2 + block % 2) * 64 + rest
    alive = position < live
    contract = (((1,), (1,)), ((), ()))
    rows = 112
    for start in range(0, q_ref.shape[0], rows):
        q = q_ref[start : start + rows, :]
        scores = lax.dot_general(q, key_high, contract, preferred_element_type=F32)
        scores = scores + lax.dot_general(q, key_low, contract, preferred_element_type=F32)
        scores = jnp.where(alive, scores, -1e30)
        top = jnp.max(scores, axis=1, keepdims=True)
        expo = jnp.exp(scores - top)
        denom = jnp.sum(expo, axis=1, keepdims=True)
        weights = expo.astype(BF16)
        mixed = jnp.dot(weights, value_high, preferred_element_type=F32)
        mixed = mixed + jnp.dot(weights, value_low, preferred_element_type=F32)
        o_ref[start : start + rows, :] = (mixed / denom).astype(BF16)


def attend(meta, query, mine, other):
    rows, width = query.shape
    block = lambda n: pl.BlockSpec((n, HEAD_DIM), lambda h: (0, h))
    return pl.pallas_call(
        attend_kernel,
        grid=(width // HEAD_DIM,),
        in_specs=[smem(), block(rows)] + [block(256)] * 8,
        out_specs=block(rows),
        out_shape=jax.ShapeDtypeStruct((rows, width), BF16),
        compiler_params=params(12),
        cost_estimate=pl.CostEstimate(
            flops=8 * rows * 1024 * width, bytes_accessed=4_000_000, transcendentals=rows * 3072
        ),
    )(meta, query, *mine, *other)


def coded_rows(value):
    high = value.astype(BF16).astype(F32)
    middle = (value - high).astype(BF16).astype(F32)
    low = value - high - middle
    line = lax.broadcasted_iota(jnp.int32, value.shape, 0)
    return jnp.where(line == 0, high, jnp.where(line == 1, middle, low)).astype(BF16)


def decoded_rows(rows):
    rows = rows.astype(F32)
    return (rows[0:1] + rows[1:2]) + rows[2:3]


def core_sum_kernel(meta_ref, kept_ref, arrived_ref, loss_ref, own_ref, *piece_refs):
    row = meta_ref[0]
    loss = loss_ref[:1] + decoded_rows(arrived_ref[384:, :])
    cells = coded_rows(jnp.broadcast_to(loss, (16, loss.shape[1])))
    for j in range(4):
        where = (row + j) % 4 if j == 0 else lax.bitwise_xor(row, j)
        for q in range(2):
            rows = pl.ds(pl.multiple_of(96 * where + 48 * q, 48), 48)
            total = kept_ref[2 * where + q] + arrived_ref[rows, :].astype(F32)
            if j == 0:
                own_ref[48 * q : 48 * q + 48, :] = total
            else:
                piece_refs[j - 1][48 * q : 48 * q + 48, :] = total.astype(BF16)
        if j == 0:
            own_ref[96:, :] = jnp.broadcast_to(loss, (8, loss.shape[1]))
        else:
            piece_refs[j - 1][96:, :] = cells


def core_sum(meta, kept, arrived, loss):
    channels = kept.shape[2]
    return pl.pallas_call(
        core_sum_kernel,
        in_specs=[smem()] + [vmem()] * 3,
        out_specs=[vmem()] * 4,
        out_shape=[jax.ShapeDtypeStruct((104, channels), F32)]
        + [jax.ShapeDtypeStruct((112, channels), BF16)] * 3,
        compiler_params=params(12),
        cost_estimate=pl.CostEstimate(flops=1_000_000, bytes_accessed=4_000_000, transcendentals=0),
    )(meta, kept, arrived, loss)


def row_sum_kernel(meta_ref, own_ref, one_ref, two_ref, three_ref, *out_refs):
    place = meta_ref[1]
    refs = (one_ref, two_ref, three_ref)
    first, second, third = [decoded_rows(r[96:, :]) for r in refs]
    loss = (own_ref[96:97, :] + first) + (second + third)
    for j in range(4):
        start = pl.multiple_of(24 * lax.bitwise_xor(place, j), 8)
        at = 48 * (lax.bitwise_xor(place, j) // 2)
        total = own_ref[pl.ds(start, 24), :]
        upper = lax.bitwise_xor(place, j) % 2 == 1
        for r in refs:
            rows = r[pl.ds(pl.multiple_of(at, 48), 48), :].astype(F32)
            total = total + jnp.where(upper, rows[24:], rows[:24])
        out_refs[j][:24, :] = total
        out_refs[j][24:, :] = jnp.broadcast_to(loss, (8, loss.shape[1]))


def row_sum(meta, own, arrived):
    channels = own.shape[1]
    return pl.pallas_call(
        row_sum_kernel,
        in_specs=[smem()] + [vmem()] * 4,
        out_specs=[vmem()] * 4,
        out_shape=[jax.ShapeDtypeStruct((32, channels), F32)] * 4,
        compiler_params=params(8),
        cost_estimate=pl.CostEstimate(flops=1_000_000, bytes_accessed=2_000_000, transcendentals=0),
    )(meta, own, *arrived)


def lift_kernel(full_ref, disc_ref, out_ref):
    rows = full_ref.shape[0]
    both = jnp.concatenate(split(full_ref[...]), axis=0)
    wide = disc_ref.shape[0] // 3
    for i in range(3):
        cols = slice(wide * i, wide * i + wide)
        product = lax.dot_general(
            both, disc_ref[cols, :], (((1,), (1,)), ((), ())), preferred_element_type=F32
        )
        out_ref[:, cols] = product[:rows] + product[rows:]


def lift(full, disc_in):
    return pl.pallas_call(
        lift_kernel,
        in_specs=[vmem()] * 2,
        out_specs=vmem(),
        out_shape=jax.ShapeDtypeStruct((full.shape[0], disc_in.shape[0]), F32),
        compiler_params=params(12),
        cost_estimate=pl.CostEstimate(flops=300_000_000, bytes_accessed=3_500_000, transcendentals=0),
    )(full, disc_in)


def critic_kernel(
    meta_ref, lifted_hbm, mine_hbm, other_hbm, proj_hbm, conv_hbm, score_ref,
    keep_ref, send_ref, loss_ref,
    feed_s, y_s, pre_s, grad_s, turned_s, back_s, att_s, proj_s, conv_ref, lifted_ref, mine_ref, other_ref, proj_sem, conv_sem,
):
    live, first_frame, half = (meta_ref[0], meta_ref[1], meta_ref[2])
    total_frames, core = (meta_ref[3], meta_ref[4])
    pairs = [(lifted_hbm, lifted_ref), (mine_hbm, mine_ref), (other_hbm, other_ref), (proj_hbm, proj_s)]
    proj_copies = [pltpu.make_async_copy(a, b, proj_sem.at[i]) for i, (a, b) in enumerate(pairs)]
    conv_copies = [
        pltpu.make_async_copy(conv_hbm.at[g], conv_ref.at[g], conv_sem.at[g])
        for g in range(conv_ref.shape[0])
    ]
    for copy in proj_copies + conv_copies:
        copy.start()
    ext = lifted_ref.shape[0]
    own_out = (ext - 2 * HALO) // STRIDE
    tiles = lifted_ref.shape[1] // 128
    for copy in proj_copies:
        copy.wait()
    feed = lifted_ref[...]
    for ref, which in ((mine_ref, half), (other_ref, 1 - half)):
        proj = proj_s[pl.ds(pl.multiple_of(HALF_ATT * which, HALF_ATT), HALF_ATT), :]
        feed = feed + jnp.dot(ref[...], proj, preferred_element_type=F32)
    frame = first_frame - HALO + lax.broadcasted_iota(jnp.int32, (ext, 1), 0)
    inside = (frame >= 0) & (frame < live)
    feed = jnp.where(inside, feed, 0.0).astype(BF16).astype(F32)
    for i in range(tiles):
        feed_s[i, :ext, :] = feed[:, 128 * i : 128 * i + 128]
        feed_s[i, ext:, :] = jnp.zeros((feed_s.shape[1] - ext, 128), F32)
    rows = y_s.shape[0]
    low = low_lanes((rows, 128))
    low_out = low_lanes((80, 128))
    for copy in conv_copies:
        copy.wait()

    @pl.loop(0, tiles, unroll=4)
    def _(tile):
        lanes = pl.ds(pl.multiple_of(tile * 128, 128), 128)
        phase = [feed_s[tile, pl.ds(b, rows, stride=STRIDE), :] for b in range(STRIDE)]
        turned = [roll_half(p) for p in phase]
        even = [jnp.where(low, phase[b], turned[b + 1]) for b in (0, 2)]
        odd = [jnp.where(low, turned[b], phase[b + 1]) for b in (0, 2)]
        sums = []
        for g, pieces in enumerate((even, odd)):
            left = jnp.concatenate(pieces, axis=1).astype(BF16)
            y_s[...] = jnp.dot(left, conv_ref[2 * tile + g], preferred_element_type=F32)
            at, after = (None, None)
            for pair in range(TAP_SETS // 2):
                cols = slice(128 * pair, 128 * pair + 128)
                a = y_s[2 * pair : 2 * pair + 80, cols]
                b = y_s[2 * pair + 1 : 2 * pair + 81, cols]
                at = a if at is None else at + a
                after = b if after is None else after + b
            sums.append((at, after))
        pre_even = sums[0][0] + roll_half(sums[0][1])
        pre_odd = roll_half(sums[1][0]) + sums[1][1]
        pre_s[:, lanes] = jnp.where(low_out, pre_even, pre_odd)

    pre = pre_s[...]
    sig = 1.0 / (1.0 + jnp.exp(-pre))
    score = score_ref[...]
    critic = jnp.sum(pre * sig * score, axis=1, keepdims=True)
    slot = lax.broadcasted_iota(jnp.int32, (80, 1), 0)
    frame_out = first_frame - STRIDE * REACH + STRIDE * slot
    valid = (frame_out >= 0) & (frame_out < total_frames) & (frame_out < live) & (slot < own_out + 2 * REACH)
    shortfall = 1.0 - critic
    own = valid & (slot >= REACH) & (slot < REACH + own_out)
    loss = jnp.sum(jnp.where(own, shortfall * shortfall, 0.0), axis=0, keepdims=True)
    loss_ref[...] = jnp.broadcast_to(loss, loss_ref.shape)
    send_ref[384:, :] = coded_rows(jnp.broadcast_to(loss, (16, send_ref.shape[1])))
    push = jnp.where(valid, -2.0 * shortfall, 0.0)
    grad = push * score * (sig * (1.0 + pre * (1.0 - sig)))
    grad = jnp.where(valid, grad, 0.0).astype(BF16).astype(F32)
    grad_s[:8, :] = jnp.zeros((8, grad_s.shape[1]), F32)
    grad_s[8:, :] = grad

    contract = (((1,), (1,)), ((), ()))
    low_back = low_lanes((own_out, 128))

    @pl.loop(0, tiles, unroll=4)
    def _(tile):
        lanes = pl.ds(pl.multiple_of(tile * 128, 128), 128)
        turned_s[...] = roll_half(grad_s[:, lanes])
        even, odd = ([], [])
        for pair in range(TAP_SETS // 2):
            up, down = (18 - 2 * pair, 17 - 2 * pair)
            even.append(
                jnp.where(low_back, grad_s[up : up + own_out, lanes], turned_s[down : down + own_out, :])
            )
            odd.append(
                jnp.where(low_back, turned_s[up : up + own_out, :], grad_s[down : down + own_out, lanes])
            )
        back = []
        for g, pieces in enumerate((even, odd)):
            left = jnp.concatenate(pieces, axis=1).astype(BF16)
            back.append(
                lax.dot_general(left, conv_ref[2 * tile + g], contract, preferred_element_type=F32)
            )
        step = lax.broadcasted_iota(jnp.int32, (own_out, 1), 0)
        for b in range(STRIDE):
            cols = slice(128 * (b // 2), 128 * (b // 2) + 128)
            e, o = (back[0][:, cols], back[1][:, cols])
            both = jnp.where(low_back, e, roll_half(o)) if b % 2 == 0 else jnp.where(low_back, roll_half(e), o)
            both = jnp.where(first_frame + STRIDE * step + b < live, both, 0.0)
            back_s[b * own_out : (b + 1) * own_out, lanes] = both.astype(BF16)

    first = core == 0
    for part, ref in enumerate((mine_ref, other_ref)):
        own_rows = ref[...].astype(F32)[HALO : ext - HALO, :]
        lefts = []
        for c in range(HALF_HEADS):
            att_s[...] = own_rows[:, c * 128 : c * 128 + 128]
            left = jnp.concatenate(
                [att_s[pl.ds(b, own_out, stride=STRIDE), :] for b in range(STRIDE)], axis=0
            )
            lefts.append(jnp.transpose(left))
        left = jnp.concatenate(lefts, axis=0).astype(BF16)
        which = half if part == 0 else 1 - half
        for q in range(4):
            block = jnp.dot(left[96 * q : 96 * q + 96], back_s[...], preferred_element_type=F32)
            one, two = (block[:48], block[48:])
            keep_ref[4 * which + q] = jnp.where(first, one, two)
            rows = pl.ds(pl.multiple_of(48 * (4 * which + q), 48), 48)
            send_ref[rows, :] = jnp.where(first, two, one).astype(BF16)


def critic(meta, lifted, mine, other, proj, conv, score):
    ext, channels = lifted.shape
    own = ext - 2 * HALO
    return pl.pallas_call(
        critic_kernel,
        in_specs=[smem()] + [anywhere()] * 5 + [vmem()],
        out_specs=[vmem(), vmem(), vmem()],
        out_shape=[
            jax.ShapeDtypeStruct((8, 48, channels), F32),
            jax.ShapeDtypeStruct((400, channels), BF16),
            jax.ShapeDtypeStruct((8, channels), F32),
        ],
        scratch_shapes=[
            pltpu.VMEM((channels // 128, 384, 128), F32),
            pltpu.VMEM((96, TAP_SETS * 64), F32),
            pltpu.VMEM((80, channels), F32),
            pltpu.VMEM((88, channels), F32),
            pltpu.VMEM((88, 128), F32),
            pltpu.VMEM((own, channels), BF16),
            pltpu.VMEM((own, 128), F32),
            pltpu.VMEM(proj.shape, BF16),
            pltpu.VMEM(conv.shape, BF16),
            pltpu.VMEM(lifted.shape, F32),
            pltpu.VMEM(mine.shape, BF16),
            pltpu.VMEM(other.shape, BF16),
            pltpu.SemaphoreType.DMA((4,)),
            pltpu.SemaphoreType.DMA((conv.shape[0],)),
        ],
        compiler_params=params(58),
        cost_estimate=pl.CostEstimate(
            flops=3_000_000_000, bytes_accessed=14_000_000, transcendentals=100_000
        ),
    )(meta, lifted, mine, other, proj, conv, score)


def shards(
    states, kv_weight, queries, hidden, out_proj, disc_in, conv_weight, score_weight, frame_len, state_len
):
    frames = hidden.shape[1]
    dp_size, seq_size = (lax.axis_size("dp"), lax.axis_size("seq"))
    clip, seq = (lax.axis_index("dp"), lax.axis_index("seq"))
    core, half, row = (seq % 2, (seq // 2) % 2, seq // 4)
    pick = jnp.arange(frame_len.shape[0]) == clip
    clip_frames = jnp.sum(jnp.where(pick, frame_len, 0))
    clip_states = jnp.sum(jnp.where(pick, state_len, 0))

    def flip(x, bit):
        return lax.ppermute(x, "seq", [(i, i ^ bit) for i in range(seq_size)])

    def turn(x, hops):
        return lax.ppermute(x, "seq", [(i, (i + 4 * hops) % seq_size) for i in range(seq_size)])

    def swap(x, dp_bits, seq_bits):
        pairs = []
        for i in range(dp_size * seq_size):
            d, q = divmod(i, seq_size)
            pairs.append((i, (d ^ dp_bits) * seq_size + (q ^ seq_bits)))
        return lax.ppermute(x, ("dp", "seq"), pairs)

    def at(x, i):
        return lax.dynamic_index_in_dim(x, i, axis=0, keepdims=False)

    att = 2 * HALF_ATT

    proj_own = jnp.dot(out_proj, disc_in, preferred_element_type=F32).astype(BF16)
    kv_weight, proj_own = lax.optimization_barrier((kv_weight, proj_own))
    proj = lax.all_gather(proj_own, "seq", axis=0, tiled=True)

    def head_cols(which, kv_weight):
        parts = [
            lax.dynamic_slice_in_dim(kv_weight, kind * att + which * HALF_ATT, HALF_ATT, axis=1)
            for kind in (0, 1)
        ]
        return jnp.concatenate(parts, axis=1)

    far = head_cols(1 - half, kv_weight)
    far, kv_weight = lax.optimization_barrier((far, kv_weight))
    near = head_cols(half, kv_weight)
    far = swap(far, 1, 2)
    near_turned = [turn(near, j) for j in (1, 3)]

    def pass_on(turned):
        rows = near.shape[0] // 2
        return [turn(turned[0][:rows], 1), turn(turned[1][rows:], 3)]

    states_in = states[0]
    near, near_turned, far, state_far, queries_in, hidden_in, conv = lax.optimization_barrier(
        (near, near_turned, far, flip(states_in, 2), queries[0], hidden[0], arrange(conv_weight))
    )

    lower = clip % 2
    channels = disc_in.shape[1]
    near_over = pass_on(near_turned)
    far_turned = [turn(far, j) for j in (1, 3)]
    state_pair = flip(jnp.concatenate([states_in, state_far], axis=0), 1)
    up = [(i, i + 1) for i in range(seq_size - 1)]
    down = [(i + 1, i) for i in range(seq_size - 1)]
    near_over, far_turned, state_pair, queries_in, hidden_in = lax.optimization_barrier(
        (near_over, far_turned, state_pair, queries_in, hidden_in)
    )

    far_over = pass_on(far_turned)
    before = jnp.concatenate([queries_in[frames - HALO :], hidden_in[frames - HALO :]], axis=1)
    before = lax.ppermute(before, "seq", up)
    after = jnp.concatenate([queries_in[:HALO], hidden_in[:HALO]], axis=1)

    cols = []
    for hop in (0, 1, 3, 2):
        for flip_half in (0, 1):
            where = (((row - hop) % 4) * 2 + (half ^ flip_half)) * 2 + core
            cols.append(where * kv_weight.shape[0])
    total_frames = frames * seq_size
    cols = jnp.stack(cols + [core]).astype(jnp.int32)
    meta = jnp.stack([clip_states, core, half, row]).astype(jnp.int32)
    meta2 = jnp.stack([clip_frames, seq * frames, half, jnp.int32(total_frames), core])
    meta3 = jnp.stack([row, 2 * half + lower, clip // 2]).astype(jnp.int32)
    blocks = [near, far, near_turned[0], far_turned[0], near_turned[1], far_turned[1]] + near_over + far_over
    tables = (cols, meta, meta2.astype(jnp.int32), meta3)
    blocks, state_pair, tables, before, after = lax.optimization_barrier(
        (blocks, state_pair, tables, before, after)
    )
    cols, meta, meta2, meta3 = tables
    state_parts = [states_in, state_far, state_pair]
    kept, sent = project(cols, state_parts, blocks)
    mine_kv = (kept + flip(sent, 1)).reshape(256, HALF_ATT)

    mine_kv, proj, queries_in, hidden_in, before, after = lax.optimization_barrier(
        (mine_kv, proj, queries[0], hidden[0], before, after)
    )
    got = [mine_kv] + [turn(mine_kv, j) for j in (1, 2, 3)]
    rows_in = jnp.concatenate([queries_in, hidden_in], axis=1)
    rows_ext = jnp.concatenate([before, rows_in, lax.ppermute(after, "seq", down)], axis=0)
    query_ext, hidden_ext = (rows_ext[:, :att], rows_ext[:, att:])
    query_mine = lax.dynamic_slice_in_dim(query_ext, half * HALF_ATT, HALF_ATT, axis=1)
    query_far = flip(lax.dynamic_slice_in_dim(query_ext, (1 - half) * HALF_ATT, HALF_ATT, axis=1), 2)
    lifted = jnp.dot(hidden_ext, disc_in, preferred_element_type=F32)
    got, query_mine, query_far, lifted = lax.optimization_barrier((got, query_mine, query_far, lifted))
    other = [flip(g, 1) for g in got]

    attended_far = flip(attend(meta, query_far, got, other), 2)
    attended_mine = attend(meta, query_mine, got, other)

    kept, sent, loss = critic(
        meta2, lifted, attended_mine, attended_far, proj, conv, score_weight.reshape(1, -1)
    )

    own_rows = att // seq_size
    share = own_rows // 2
    own, *pieces = core_sum(meta3, kept, flip(sent, 1), loss)
    arrived = [flip(p, 4 * (j + 1)) for j, p in enumerate(pieces)]
    own, *pieces = row_sum(meta3, own, arrived)
    a, b, c = [swap(p, j & 1, j & 2) for j, p in zip((1, 2, 3), pieces)]
    total = (own + a) + (b + c)
    a, b, c = [swap(total, d, 0) for d in (2, 4, 6)]
    total = (total + a) + (b + c)
    total = total + swap(total, 8, 0)
    total_loss = total[share, 0]
    total = total[:share]
    beside = swap(total, 1, 0)
    first = lower == 0
    total = jnp.concatenate([jnp.where(first, total, beside), jnp.where(first, beside, total)], axis=0)
    grad_proj = lift(total, disc_in)
    counted = jnp.sum((frame_len + STRIDE - 1) // STRIDE).astype(F32)
    return (grad_proj, total_loss / counted)


def solution(mesh):
    return jax.shard_map(
        shards,
        mesh=mesh,
        in_specs=(
            P("dp", "seq", None),
            P("seq", None),
            P("dp", "seq", None),
            P("dp", "seq", None),
            P("seq", None),
            P(),
            P(),
            P(),
            P(),
            P(),
        ),
        out_specs=(P("seq", None), P()),
        check_vma=False,
    )
```

```python
import functools
import math

import jax
import jax.numpy as jnp
from jax import lax
from jax.experimental import pallas as pl
from jax.experimental.pallas import tpu as pltpu
from jax.sharding import PartitionSpec as P

HEAD_DIM = 128
HALF_HEADS = 3
HALF_ATT = HEAD_DIM * HALF_HEADS
GROUP_CH = 64
STRIDE = 4
TAPS = 41
TAP_SETS = 12
MARGIN = 20
HALO = 40
REACH = 5
F32 = jnp.float32
BF16 = jnp.bfloat16
MIB = 1024 * 1024


def params(mib):
    return pltpu.CompilerParams(vmem_limit_bytes=mib * MIB)


def smem():
    return pl.BlockSpec(memory_space=pltpu.SMEM)


def vmem():
    return pl.BlockSpec(memory_space=pltpu.VMEM)


def anywhere():
    return pl.BlockSpec(memory_space=pltpu.HBM)


def low_lanes(shape):
    return lax.broadcasted_iota(jnp.int32, shape, 1) % 128 < 64


def roll_half(x):
    return pltpu.roll(x, 64, 1)


def arrange_kernel(w_ref, o_ref):
    low = low_lanes((GROUP_CH, 128))
    zero = jnp.zeros((GROUP_CH, 128), F32)

    def tap(k):
        return w_ref[k].astype(F32) if k < TAPS else zero

    for b in range(STRIDE):
        for pair in range(TAP_SETS // 2):
            first = tap(8 * pair + b)
            second = tap(8 * pair + 4 + b)
            rows, lanes = (slice(b * 64, b * 64 + 64), slice(pair * 128, pair * 128 + 128))
            o_ref[0, rows, lanes] = jnp.where(low, first, roll_half(second)).astype(BF16)
            o_ref[1, rows, lanes] = jnp.where(low, roll_half(first), second).astype(BF16)


def arrange(conv_weight):
    taps, group_in, channels = conv_weight.shape
    groups = channels // GROUP_CH
    return pl.pallas_call(
        arrange_kernel,
        grid=(channels // 128,),
        in_specs=[pl.BlockSpec((taps, group_in, 128), lambda l: (0, 0, l))],
        out_specs=pl.BlockSpec((2, STRIDE * 64, TAP_SETS * 64), lambda l: (l, 0, 0)),
        out_shape=jax.ShapeDtypeStruct((groups, STRIDE * 64, TAP_SETS * 64), BF16),
        compiler_params=params(58),
        cost_estimate=pl.CostEstimate(flops=20_000_000, bytes_accessed=20_000_000, transcendentals=0),
    )(conv_weight)


def project_kernel(cols_ref, *refs):
    states, weights, (keep_ref, send_ref) = (refs[:3], refs[3:11], refs[11:13])
    state_s, weight_s, total_s, state_sem, weight_sem = refs[13:]
    core = cols_ref[8]
    state_copies = [
        pltpu.make_async_copy(s, state_s.at[place], state_sem.at[i])
        for i, (s, place) in enumerate(
            ((states[0], 0), (states[1], 2), (states[2].at[:64], 1), (states[2].at[64:], 3))
        )
    ]
    weight_copies = [
        pltpu.make_async_copy(w, weight_s.at[i], weight_sem.at[i]) for i, w in enumerate(weights)
    ]
    for copy in state_copies + weight_copies:
        copy.start()
    for copy in state_copies:
        copy.wait()
    for i, copy in enumerate(weight_copies):
        copy.wait()
        start = pl.multiple_of(cols_ref[i], 256)
        left = jnp.concatenate([state_s[j, :, pl.ds(start, 256)] for j in range(4)], axis=0)
        part = jnp.dot(left, weight_s[i], preferred_element_type=F32)
        if i == 0:
            total_s[...] = part
        else:
            total_s[...] += part
    kept = pl.ds(pl.multiple_of(core * HALF_ATT, 128), HALF_ATT)
    sent = pl.ds(pl.multiple_of((1 - core) * HALF_ATT, 128), HALF_ATT)
    for j in range(4):
        rows = slice(64 * j, 64 * j + 64)
        block = 2 * (j // 2) + (core + j) % 2
        keep_ref[block] = total_s[rows, kept]
        send_ref[block] = total_s[rows, sent]


def project(cols, states, weights):
    width = 2 * HALF_ATT
    out = jax.ShapeDtypeStruct((4, 64, HALF_ATT), F32)
    return pl.pallas_call(
        project_kernel,
        in_specs=[smem()] + [anywhere()] * 11,
        out_specs=[vmem(), vmem()],
        out_shape=[out, out],
        scratch_shapes=[
            pltpu.VMEM((4,) + states[0].shape, BF16),
            pltpu.VMEM((8,) + weights[0].shape, BF16),
            pltpu.VMEM((256, width), F32),
            pltpu.SemaphoreType.DMA((4,)),
            pltpu.SemaphoreType.DMA((8,)),
        ],
        compiler_params=params(58),
        cost_estimate=pl.CostEstimate(flops=800_000_000, bytes_accessed=6_000_000, transcendentals=0),
    )(cols, *states, *weights)


def split(x):
    high = x.astype(BF16)
    return high, (x - high.astype(F32)).astype(BF16)


def attend_kernel(meta_ref, q_ref, *refs):
    mine, other, o_ref = (refs[:4], refs[4:8], refs[8])
    live, core, half, row = (meta_ref[0], meta_ref[1], meta_ref[2], meta_ref[3])
    first = core == 0
    keys, values = ([], [])
    for m, o in zip(mine, other):
        keys.append(jnp.where(first, m[...], o[...]))
        values.append(jnp.where(first, o[...], m[...]))
    key_high, key_low = split(jnp.concatenate(keys, axis=0) * (1.0 / math.sqrt(HEAD_DIM)))
    value_high, value_low = split(jnp.concatenate(values, axis=0))
    spot = lax.broadcasted_iota(jnp.int32, (1, 1024), 1)
    hop, block, rest = (spot // 256, (spot // 64) % 4, spot % 64)
    where_y = (row - hop + 4) % 4
    where_h = (half + block // 2) % 2
    position = ((where_y * 2 + where_h) * 2 + block % 2) * 64 + rest
    alive = position < live
    contract = (((1,), (1,)), ((), ()))
    rows = 112
    for start in range(0, q_ref.shape[0], rows):
        q = q_ref[start : start + rows, :]
        scores = lax.dot_general(q, key_high, contract, preferred_element_type=F32)
        scores = scores + lax.dot_general(q, key_low, contract, preferred_element_type=F32)
        scores = jnp.where(alive, scores, -1e30)
        top = jnp.max(scores, axis=1, keepdims=True)
        expo = jnp.exp(scores - top)
        denom = jnp.sum(expo, axis=1, keepdims=True)
        weights = expo.astype(BF16)
        mixed = jnp.dot(weights, value_high, preferred_element_type=F32)
        mixed = mixed + jnp.dot(weights, value_low, preferred_element_type=F32)
        o_ref[start : start + rows, :] = (mixed / denom).astype(BF16)


def attend(meta, query, mine, other):
    rows, width = query.shape
    block = lambda n: pl.BlockSpec((n, HEAD_DIM), lambda h: (0, h))
    return pl.pallas_call(
        attend_kernel,
        grid=(width // HEAD_DIM,),
        in_specs=[smem(), block(rows)] + [block(256)] * 8,
        out_specs=block(rows),
        out_shape=jax.ShapeDtypeStruct((rows, width), BF16),
        compiler_params=params(12),
        cost_estimate=pl.CostEstimate(
            flops=8 * rows * 1024 * width, bytes_accessed=4_000_000, transcendentals=rows * 3072
        ),
    )(meta, query, *mine, *other)


def coded_rows(value):
    high = value.astype(BF16).astype(F32)
    middle = (value - high).astype(BF16).astype(F32)
    low = value - high - middle
    line = lax.broadcasted_iota(jnp.int32, value.shape, 0)
    return jnp.where(line == 0, high, jnp.where(line == 1, middle, low)).astype(BF16)


def decoded_rows(rows):
    rows = rows.astype(F32)
    return (rows[0:1] + rows[1:2]) + rows[2:3]


def core_sum_kernel(meta_ref, kept_ref, arrived_ref, loss_ref, own_ref, *piece_refs):
    row = meta_ref[0]
    loss = loss_ref[:1] + decoded_rows(arrived_ref[384:, :])
    cells = coded_rows(jnp.broadcast_to(loss, (16, loss.shape[1])))
    for j in range(4):
        where = (row + j) % 4 if j == 0 else lax.bitwise_xor(row, j)
        for q in range(2):
            rows = pl.ds(pl.multiple_of(96 * where + 48 * q, 48), 48)
            total = kept_ref[2 * where + q] + arrived_ref[rows, :].astype(F32)
            if j == 0:
                own_ref[48 * q : 48 * q + 48, :] = total
            else:
                piece_refs[j - 1][48 * q : 48 * q + 48, :] = total.astype(BF16)
        if j == 0:
            own_ref[96:, :] = jnp.broadcast_to(loss, (8, loss.shape[1]))
        else:
            piece_refs[j - 1][96:, :] = cells


def core_sum(meta, kept, arrived, loss):
    channels = kept.shape[2]
    return pl.pallas_call(
        core_sum_kernel,
        in_specs=[smem()] + [vmem()] * 3,
        out_specs=[vmem()] * 4,
        out_shape=[jax.ShapeDtypeStruct((104, channels), F32)]
        + [jax.ShapeDtypeStruct((112, channels), BF16)] * 3,
        compiler_params=params(12),
        cost_estimate=pl.CostEstimate(flops=1_000_000, bytes_accessed=4_000_000, transcendentals=0),
    )(meta, kept, arrived, loss)


def row_sum_kernel(meta_ref, own_ref, one_ref, two_ref, three_ref, *out_refs):
    place = meta_ref[1]
    refs = (one_ref, two_ref, three_ref)
    first, second, third = [decoded_rows(r[96:, :]) for r in refs]
    loss = (own_ref[96:97, :] + first) + (second + third)
    for j in range(4):
        start = pl.multiple_of(24 * lax.bitwise_xor(place, j), 8)
        at = 48 * (lax.bitwise_xor(place, j) // 2)
        total = own_ref[pl.ds(start, 24), :]
        upper = lax.bitwise_xor(place, j) % 2 == 1
        for r in refs:
            rows = r[pl.ds(pl.multiple_of(at, 48), 48), :].astype(F32)
            total = total + jnp.where(upper, rows[24:], rows[:24])
        out_refs[j][:24, :] = total
        out_refs[j][24:, :] = jnp.broadcast_to(loss, (8, loss.shape[1]))


def row_sum(meta, own, arrived):
    channels = own.shape[1]
    return pl.pallas_call(
        row_sum_kernel,
        in_specs=[smem()] + [vmem()] * 4,
        out_specs=[vmem()] * 4,
        out_shape=[jax.ShapeDtypeStruct((32, channels), F32)] * 4,
        compiler_params=params(8),
        cost_estimate=pl.CostEstimate(flops=1_000_000, bytes_accessed=2_000_000, transcendentals=0),
    )(meta, own, *arrived)


def lift_kernel(full_ref, disc_ref, out_ref):
    rows = full_ref.shape[0]
    both = jnp.concatenate(split(full_ref[...]), axis=0)
    wide = disc_ref.shape[0] // 3
    for i in range(3):
        cols = slice(wide * i, wide * i + wide)
        product = lax.dot_general(
            both, disc_ref[cols, :], (((1,), (1,)), ((), ())), preferred_element_type=F32
        )
        out_ref[:, cols] = product[:rows] + product[rows:]


def lift(full, disc_in):
    return pl.pallas_call(
        lift_kernel,
        in_specs=[vmem()] * 2,
        out_specs=vmem(),
        out_shape=jax.ShapeDtypeStruct((full.shape[0], disc_in.shape[0]), F32),
        compiler_params=params(12),
        cost_estimate=pl.CostEstimate(flops=300_000_000, bytes_accessed=3_500_000, transcendentals=0),
    )(full, disc_in)


def critic_kernel(
    meta_ref, lifted_hbm, mine_hbm, other_hbm, proj_hbm, conv_hbm, score_ref,
    keep_ref, send_ref, loss_ref,
    feed_s, y_s, pre_s, grad_s, turned_s, back_s, att_s, proj_s, conv_ref, lifted_ref, mine_ref, other_ref, proj_sem, conv_sem,
):
    live, first_frame, half = (meta_ref[0], meta_ref[1], meta_ref[2])
    total_frames, core = (meta_ref[3], meta_ref[4])
    pairs = [(lifted_hbm, lifted_ref), (mine_hbm, mine_ref), (other_hbm, other_ref), (proj_hbm, proj_s)]
    proj_copies = [pltpu.make_async_copy(a, b, proj_sem.at[i]) for i, (a, b) in enumerate(pairs)]
    conv_copies = [
        pltpu.make_async_copy(conv_hbm.at[g], conv_ref.at[g], conv_sem.at[g])
        for g in range(conv_ref.shape[0])
    ]
    for copy in proj_copies + conv_copies:
        copy.start()
    ext = lifted_ref.shape[0]
    own_out = (ext - 2 * HALO) // STRIDE
    tiles = lifted_ref.shape[1] // 128
    for copy in proj_copies:
        copy.wait()
    feed = lifted_ref[...]
    for ref, which in ((mine_ref, half), (other_ref, 1 - half)):
        proj = proj_s[pl.ds(pl.multiple_of(HALF_ATT * which, HALF_ATT), HALF_ATT), :]
        feed = feed + jnp.dot(ref[...], proj, preferred_element_type=F32)
    frame = first_frame - HALO + lax.broadcasted_iota(jnp.int32, (ext, 1), 0)
    inside = (frame >= 0) & (frame < live)
    feed = jnp.where(inside, feed, 0.0).astype(BF16).astype(F32)
    for i in range(tiles):
        feed_s[i, :ext, :] = feed[:, 128 * i : 128 * i + 128]
        feed_s[i, ext:, :] = jnp.zeros((feed_s.shape[1] - ext, 128), F32)
    rows = y_s.shape[0]
    low = low_lanes((rows, 128))
    low_out = low_lanes((80, 128))
    for copy in conv_copies:
        copy.wait()

    @pl.loop(0, tiles, unroll=4)
    def _(tile):
        lanes = pl.ds(pl.multiple_of(tile * 128, 128), 128)
        phase = [feed_s[tile, pl.ds(b, rows, stride=STRIDE), :] for b in range(STRIDE)]
        turned = [roll_half(p) for p in phase]
        even = [jnp.where(low, phase[b], turned[b + 1]) for b in (0, 2)]
        odd = [jnp.where(low, turned[b], phase[b + 1]) for b in (0, 2)]
        sums = []
        for g, pieces in enumerate((even, odd)):
            left = jnp.concatenate(pieces, axis=1).astype(BF16)
            y_s[...] = jnp.dot(left, conv_ref[2 * tile + g], preferred_element_type=F32)
            at, after = (None, None)
            for pair in range(TAP_SETS // 2):
                cols = slice(128 * pair, 128 * pair + 128)
                a = y_s[2 * pair : 2 * pair + 80, cols]
                b = y_s[2 * pair + 1 : 2 * pair + 81, cols]
                at = a if at is None else at + a
                after = b if after is None else after + b
            sums.append((at, after))
        pre_even = sums[0][0] + roll_half(sums[0][1])
        pre_odd = roll_half(sums[1][0]) + sums[1][1]
        pre_s[:, lanes] = jnp.where(low_out, pre_even, pre_odd)

    pre = pre_s[...]
    sig = 1.0 / (1.0 + jnp.exp(-pre))
    score = score_ref[...]
    critic = jnp.sum(pre * sig * score, axis=1, keepdims=True)
    slot = lax.broadcasted_iota(jnp.int32, (80, 1), 0)
    frame_out = first_frame - STRIDE * REACH + STRIDE * slot
    valid = (frame_out >= 0) & (frame_out < total_frames) & (frame_out < live) & (slot < own_out + 2 * REACH)
    shortfall = 1.0 - critic
    own = valid & (slot >= REACH) & (slot < REACH + own_out)
    loss = jnp.sum(jnp.where(own, shortfall * shortfall, 0.0), axis=0, keepdims=True)
    loss_ref[...] = jnp.broadcast_to(loss, loss_ref.shape)
    send_ref[384:, :] = coded_rows(jnp.broadcast_to(loss, (16, send_ref.shape[1])))
    push = jnp.where(valid, -2.0 * shortfall, 0.0)
    grad = push * score * (sig * (1.0 + pre * (1.0 - sig)))
    grad = jnp.where(valid, grad, 0.0).astype(BF16).astype(F32)
    grad_s[:8, :] = jnp.zeros((8, grad_s.shape[1]), F32)
    grad_s[8:, :] = grad

    contract = (((1,), (1,)), ((), ()))
    low_back = low_lanes((own_out, 128))

    @pl.loop(0, tiles, unroll=4)
    def _(tile):
        lanes = pl.ds(pl.multiple_of(tile * 128, 128), 128)
        turned_s[...] = roll_half(grad_s[:, lanes])
        even, odd = ([], [])
        for pair in range(TAP_SETS // 2):
            up, down = (18 - 2 * pair, 17 - 2 * pair)
            even.append(
                jnp.where(low_back, grad_s[up : up + own_out, lanes], turned_s[down : down + own_out, :])
            )
            odd.append(
                jnp.where(low_back, turned_s[up : up + own_out, :], grad_s[down : down + own_out, lanes])
            )
        back = []
        for g, pieces in enumerate((even, odd)):
            left = jnp.concatenate(pieces, axis=1).astype(BF16)
            back.append(
                lax.dot_general(left, conv_ref[2 * tile + g], contract, preferred_element_type=F32)
            )
        step = lax.broadcasted_iota(jnp.int32, (own_out, 1), 0)
        for b in range(STRIDE):
            cols = slice(128 * (b // 2), 128 * (b // 2) + 128)
            e, o = (back[0][:, cols], back[1][:, cols])
            both = jnp.where(low_back, e, roll_half(o)) if b % 2 == 0 else jnp.where(low_back, roll_half(e), o)
            both = jnp.where(first_frame + STRIDE * step + b < live, both, 0.0)
            back_s[b * own_out : (b + 1) * own_out, lanes] = both.astype(BF16)

    first = core == 0
    for part, ref in enumerate((mine_ref, other_ref)):
        own_rows = ref[...].astype(F32)[HALO : ext - HALO, :]
        lefts = []
        for c in range(HALF_HEADS):
            att_s[...] = own_rows[:, c * 128 : c * 128 + 128]
            left = jnp.concatenate(
                [att_s[pl.ds(b, own_out, stride=STRIDE), :] for b in range(STRIDE)], axis=0
            )
            lefts.append(jnp.transpose(left))
        left = jnp.concatenate(lefts, axis=0).astype(BF16)
        which = half if part == 0 else 1 - half
        for q in range(4):
            block = jnp.dot(left[96 * q : 96 * q + 96], back_s[...], preferred_element_type=F32)
            one, two = (block[:48], block[48:])
            keep_ref[4 * which + q] = jnp.where(first, one, two)
            rows = pl.ds(pl.multiple_of(48 * (4 * which + q), 48), 48)
            send_ref[rows, :] = jnp.where(first, two, one).astype(BF16)


def critic(meta, lifted, mine, other, proj, conv, score):
    ext, channels = lifted.shape
    own = ext - 2 * HALO
    return pl.pallas_call(
        critic_kernel,
        in_specs=[smem()] + [anywhere()] * 5 + [vmem()],
        out_specs=[vmem(), vmem(), vmem()],
        out_shape=[
            jax.ShapeDtypeStruct((8, 48, channels), F32),
            jax.ShapeDtypeStruct((400, channels), BF16),
            jax.ShapeDtypeStruct((8, channels), F32),
        ],
        scratch_shapes=[
            pltpu.VMEM((channels // 128, 384, 128), F32),
            pltpu.VMEM((96, TAP_SETS * 64), F32),
            pltpu.VMEM((80, channels), F32),
            pltpu.VMEM((88, channels), F32),
            pltpu.VMEM((88, 128), F32),
            pltpu.VMEM((own, channels), BF16),
            pltpu.VMEM((own, 128), F32),
            pltpu.VMEM(proj.shape, BF16),
            pltpu.VMEM(conv.shape, BF16),
            pltpu.VMEM(lifted.shape, F32),
            pltpu.VMEM(mine.shape, BF16),
            pltpu.VMEM(other.shape, BF16),
            pltpu.SemaphoreType.DMA((4,)),
            pltpu.SemaphoreType.DMA((conv.shape[0],)),
        ],
        compiler_params=params(58),
        cost_estimate=pl.CostEstimate(
            flops=3_000_000_000, bytes_accessed=14_000_000, transcendentals=100_000
        ),
    )(meta, lifted, mine, other, proj, conv, score)


def shards(
    states, kv_weight, queries, hidden, out_proj, disc_in, conv_weight, score_weight, frame_len, state_len
):
    frames = hidden.shape[1]
    dp_size, seq_size = (lax.axis_size("dp"), lax.axis_size("seq"))
    clip, seq = (lax.axis_index("dp"), lax.axis_index("seq"))
    core, half, row = (seq % 2, (seq // 2) % 2, seq // 4)
    pick = jnp.arange(frame_len.shape[0]) == clip
    clip_frames = jnp.sum(jnp.where(pick, frame_len, 0))
    clip_states = jnp.sum(jnp.where(pick, state_len, 0))

    def flip(x, bit):
        return lax.ppermute(x, "seq", [(i, i ^ bit) for i in range(seq_size)])

    def turn(x, hops):
        return lax.ppermute(x, "seq", [(i, (i + 4 * hops) % seq_size) for i in range(seq_size)])

    def swap(x, dp_bits, seq_bits):
        pairs = []
        for i in range(dp_size * seq_size):
            d, q = divmod(i, seq_size)
            pairs.append((i, (d ^ dp_bits) * seq_size + (q ^ seq_bits)))
        return lax.ppermute(x, ("dp", "seq"), pairs)

    def at(x, i):
        return lax.dynamic_index_in_dim(x, i, axis=0, keepdims=False)

    att = 2 * HALF_ATT

    proj_own = jnp.dot(out_proj, disc_in, preferred_element_type=F32).astype(BF16)
    kv_weight, proj_own = lax.optimization_barrier((kv_weight, proj_own))
    proj = lax.all_gather(proj_own, "seq", axis=0, tiled=True)

    def head_cols(which, kv_weight):
        parts = [
            lax.dynamic_slice_in_dim(kv_weight, kind * att + which * HALF_ATT, HALF_ATT, axis=1)
            for kind in (0, 1)
        ]
        return jnp.concatenate(parts, axis=1)

    far = head_cols(1 - half, kv_weight)
    far, kv_weight = lax.optimization_barrier((far, kv_weight))
    near = head_cols(half, kv_weight)
    far = swap(far, 1, 2)
    hops = (1, 3, 2)
    near_turned = [turn(near, j) for j in hops]
    states_in = states[0]
    near, near_turned, far, state_far, queries_in, hidden_in, conv_in = lax.optimization_barrier(
        (near, near_turned, far, flip(states_in, 2), queries[0], hidden[0], conv_weight)
    )

    lower = clip % 2
    channels = disc_in.shape[1]
    near_blocks = [near] + near_turned
    far_blocks = [far] + [turn(far, j) for j in hops]
    state_pair = flip(jnp.concatenate([states_in, state_far], axis=0), 1)
    up = [(i, i + 1) for i in range(seq_size - 1)]
    down = [(i + 1, i) for i in range(seq_size - 1)]
    before = jnp.concatenate([queries_in[frames - HALO :], hidden_in[frames - HALO :]], axis=1)
    before = lax.ppermute(before, "seq", up)
    after = jnp.concatenate([queries_in[:HALO], hidden_in[:HALO]], axis=1)

    cols = []
    for hop in (0, 1, 3, 2):
        for flip_half in (0, 1):
            where = (((row - hop) % 4) * 2 + (half ^ flip_half)) * 2 + core
            cols.append(where * kv_weight.shape[0])
    total_frames = frames * seq_size
    cols = jnp.stack(cols + [core]).astype(jnp.int32)
    meta = jnp.stack([clip_states, core, half, row]).astype(jnp.int32)
    meta2 = jnp.stack([clip_frames, seq * frames, half, jnp.int32(total_frames), core])
    meta3 = jnp.stack([row, 2 * half + lower, clip // 2]).astype(jnp.int32)
    blocks = [b for pair in zip(near_blocks, far_blocks) for b in pair]
    tables = (cols, meta, meta2.astype(jnp.int32), meta3)
    conv = arrange(conv_in)
    blocks, state_pair, tables, before, after, conv = lax.optimization_barrier(
        (blocks, state_pair, tables, before, after, conv)
    )
    cols, meta, meta2, meta3 = tables
    state_parts = [states_in, state_far, state_pair]
    kept, sent = project(cols, state_parts, blocks)
    mine_kv = (kept + flip(sent, 1)).reshape(256, HALF_ATT)

    mine_kv, proj, queries_in, hidden_in, before, after = lax.optimization_barrier(
        (mine_kv, proj, queries[0], hidden[0], before, after)
    )
    got = [mine_kv] + [turn(mine_kv, j) for j in (1, 2, 3)]
    rows_in = jnp.concatenate([queries_in, hidden_in], axis=1)
    rows_ext = jnp.concatenate([before, rows_in, lax.ppermute(after, "seq", down)], axis=0)
    query_ext, hidden_ext = (rows_ext[:, :att], rows_ext[:, att:])
    query_mine = lax.dynamic_slice_in_dim(query_ext, half * HALF_ATT, HALF_ATT, axis=1)
    query_far = flip(lax.dynamic_slice_in_dim(query_ext, (1 - half) * HALF_ATT, HALF_ATT, axis=1), 2)
    lifted = jnp.dot(hidden_ext, disc_in, preferred_element_type=F32)
    got, query_mine, query_far, lifted = lax.optimization_barrier((got, query_mine, query_far, lifted))
    other = [flip(g, 1) for g in got]

    attended_far = flip(attend(meta, query_far, got, other), 2)
    attended_mine = attend(meta, query_mine, got, other)

    kept, sent, loss = critic(
        meta2, lifted, attended_mine, attended_far, proj, conv, score_weight.reshape(1, -1)
    )

    own_rows = att // seq_size
    share = own_rows // 2
    own, *pieces = core_sum(meta3, kept, flip(sent, 1), loss)
    arrived = [flip(p, 4 * (j + 1)) for j, p in enumerate(pieces)]
    own, *pieces = row_sum(meta3, own, arrived)
    a, b, c = [swap(p, j & 1, j & 2) for j, p in zip((1, 2, 3), pieces)]
    total = (own + a) + (b + c)
    a, b, c = [swap(total, d, 0) for d in (2, 4, 6)]
    total = (total + a) + (b + c)
    total = total + swap(total, 8, 0)
    total_loss = total[share, 0]
    total = total[:share]
    beside = swap(total, 1, 0)
    first = lower == 0
    total = jnp.concatenate([jnp.where(first, total, beside), jnp.where(first, beside, total)], axis=0)
    grad_proj = lift(total, disc_in)
    counted = jnp.sum((frame_len + STRIDE - 1) // STRIDE).astype(F32)
    return (grad_proj, total_loss / counted)


def solution(mesh):
    return jax.shard_map(
        shards,
        mesh=mesh,
        in_specs=(
            P("dp", "seq", None),
            P("seq", None),
            P("dp", "seq", None),
            P("dp", "seq", None),
            P("seq", None),
            P(),
            P(),
            P(),
            P(),
            P(),
        ),
        out_specs=(P("seq", None), P()),
        check_vma=False,
    )
```
